32 devices in a mesh: gx: 8 (over z, x), gy: 4 (over y, core).
Axes of the slice: x: 2, y: 2, z: 4, core: 2. Of those that a mesh axis runs over, the one named last changes fastest.
Arguments:
- velocity: float32 [3, 1, 1024, 2560], P(None, None, 'gy', 'gx'), may hold values from -12 to 12
- grid_x: float32 [33], replicated, may hold values from 0.05 to 1
- grid_y: float32 [1024, 33], P('gy'), may hold values from 0.05 to 1
- test_x: float32 [33], replicated, may hold values from 0.05 to 1
- test_y: float32 [1024, 33], P('gy'), may hold values from 0.05 to 1
Outputs:
- subgrid: float32 [6, 1, 1024, 2560], P(None, None, 'gy', 'gx')
- germano: float32 [6, 1, 1024, 2560], P(None, None, 'gy', 'gx')
The draws below stay inside these ranges and needn't reach their ends.
All inputs are finite; a program needn't handle non-finite values.
Results may differ from the reference program's by a relative error of at most 0.0001.
Values sent between devices are 32-bit elements; how exact they have to be, the bound alone decides.
A program may use at most 64 MiB of HBM per device.

```python
import math
import jax
import jax.numpy as jnp
from jax import lax

NZ = 1
TAPS = 33
NX = 2560
NY = 1024


def block_scale(key, dims, cuts, low, top_value):
    gain, own = 1.0, jax.random.fold_in(key, 6)
    for position, shards_of in cuts:
        draws = jnp.exp(jax.random.uniform(jax.random.fold_in(own, position), (shards_of,), jnp.float32, low / len(cuts), top_value / len(cuts)))
        gain = gain * jnp.repeat(draws, dims[position] // shards_of).reshape([-1 if axis == position else 1 for axis in range(len(dims))])
    return gain


def scatter_about(rng, extent, deviation, most, pieces=(), kind=jnp.bfloat16):
    level = block_scale(rng, extent, pieces, -0.22, 0.18) if pieces else 1.0
    values = jax.random.normal(rng, extent, jnp.float32) * deviation * level
    return jnp.minimum(jnp.maximum(values, -most), most).astype(kind)


def setup_inputs(seed: int = 0) -> dict:
    keys = jax.random.split(jax.random.key(seed), 6)
    return {
        "velocity": scatter_about(keys[0], (3, NZ, NY, NX), 2.0, 12.0, ((2, 4), (3, 8)), jnp.float32),
        "grid_x": jnp.clip(jnp.exp(jax.random.uniform(keys[1], (TAPS,), jnp.float32, math.log(0.05), math.log(1.0))), 0.05, 1.0),
        "grid_y": jnp.clip(jnp.exp(math.log(1.0) - 2.9957323 * jax.random.uniform(keys[2], (NY, TAPS), jnp.float32) ** block_scale(keys[2], (NY, TAPS), ((0, 4),), -0.2, 0.2)), 0.05, 1.0),
        "test_x": jnp.clip(jnp.exp(jax.random.uniform(keys[3], (TAPS,), jnp.float32, math.log(0.05), math.log(1.0))), 0.05, 1.0),
        "test_y": jnp.clip(jnp.exp(math.log(1.0) - 2.9957323 * jax.random.uniform(keys[4], (NY, TAPS), jnp.float32) ** block_scale(keys[4], (NY, TAPS), ((0, 4),), -0.2, 0.2)), 0.05, 1.0),
    }


COMPONENT_PAIRS = [(0, 0), (0, 1), (0, 2), (1, 1), (1, 2), (2, 2)]


def x_smooth(field, weights):
    taps_count = weights.shape[0]
    margin = (taps_count - 1) // 2
    normed = weights / jnp.sum(weights)
    padded = jnp.concatenate([field[..., -margin:], field, field[..., :margin]], axis=-1)
    lead_shape = field.shape[:-1]
    flat = padded.reshape((-1, 1, padded.shape[-1]))
    kernel = normed.reshape((1, 1, taps_count)).astype(field.dtype)
    result = lax.conv_general_dilated(flat, kernel, (1,), "VALID", precision=lax.Precision.HIGHEST)
    return result.reshape(lead_shape + (field.shape[-1],))


def y_smooth(field, table):
    rows_count = table.shape[0]
    taps_count = table.shape[1]
    margin = (taps_count - 1) // 2
    global_row = jnp.arange(rows_count, dtype=jnp.int32)
    source = global_row[:, None] + jnp.arange(taps_count, dtype=jnp.int32)[None, :] - margin
    inside = (source >= 0) & (source < rows_count)
    masked = jnp.where(inside, table, jnp.zeros_like(table))
    normed = masked / jnp.sum(masked, axis=1, keepdims=True)
    padded = jnp.pad(field, ((0, 0), (margin, margin), (0, 0)))
    result = jnp.zeros_like(field)
    for offset in range(taps_count):
        result = result + normed[:, offset][None, :, None] * padded[:, offset:offset + rows_count, :]
    return result


def smooth(field, weights, table):
    return y_smooth(x_smooth(field, weights), table)


def reference(velocity, grid_x, grid_y, test_x, test_y):
    coarse = [smooth(velocity[comp], grid_x, grid_y) for comp in range(3)]
    tested = [smooth(coarse[comp], test_x, test_y) for comp in range(3)]
    subgrid = []
    germano = []
    for first_comp, second_comp in COMPONENT_PAIRS:
        product = velocity[first_comp] * velocity[second_comp]
        subgrid.append(smooth(product, grid_x, grid_y) - coarse[first_comp] * coarse[second_comp])
        resolved = coarse[first_comp] * coarse[second_comp]
        germano.append(smooth(resolved, test_x, test_y) - tested[first_comp] * tested[second_comp])
    return jnp.stack(subgrid), jnp.stack(germano)
```

```python
import functools

import jax
import jax.numpy as jnp
from jax import lax
from jax.experimental import pallas as pl
from jax.experimental.pallas import tpu as pltpu
from jax.sharding import PartitionSpec as P

MESH = pl.DeviceIdType.MESH
LANES = 128
SUB = 8
DIRECTIONS = [(1, 0), (-1, 0), (0, 1), (0, -1), (1, 1), (-1, 1), (1, -1), (-1, -1)]
BF = jnp.bfloat16
F32 = jnp.float32


def round_up(value, unit):
    return (value + unit - 1) // unit * unit


def split(value):
    high = value.astype(BF)
    return high, (value - high.astype(F32)).astype(BF)


def pair_of(p):
    first = jnp.where(p < 3, 0, jnp.where(p < 5, 1, 2))
    second = jnp.where(p < 3, p, jnp.where(p < 5, p - 2, 2))
    return first, second


def dot(a, b):
    return jnp.dot(a, b, preferred_element_type=F32)


def x_weights(w_ref, step, out, edge):
    taps = w_ref.shape[1]
    w = jnp.concatenate([w_ref[...], jnp.zeros((1, LANES - taps), F32)], axis=1)
    w = w / jnp.sum(w)
    band = pltpu.roll(jnp.broadcast_to(w, (LANES, LANES)), 0, 1, stride=1, stride_axis=0)
    high, low = split(band[0:step])
    out[0:step, 0:LANES] = high
    out[0:step, LANES:] = high
    out[step:, 0:LANES] = low
    out[step:, LANES:] = jnp.zeros((step, LANES), BF)
    width = edge.shape[0]
    high, low = split(band[0:width])
    high = high.astype(F32)
    edge[:, 0:LANES] = (high + pltpu.roll(high, 2 * width, 1)).astype(BF)
    edge[:, LANES:] = low


def y_weights(table, taps, first_row, total, cols, main, edge=None, tiles=None):
    margin = (taps - 1) // 2
    width = 2 * margin
    lanes = table.shape[1]
    wide = cols + LANES
    k = lax.broadcasted_iota(jnp.int32, (LANES, lanes), 0)
    lane = lax.broadcasted_iota(jnp.int32, (LANES, lanes), 1)
    y = first_row + jnp.where(lane < cols + LANES // 2, lane, lane - wide)
    source = y + k - margin
    keep = (k < taps) & (source >= 0) & (source < total) & (y >= 0) & (y < total)
    w = jnp.where(keep, jnp.concatenate(
        [table, jnp.zeros((LANES - table.shape[0], lanes), F32)], axis=0), 0.0)
    s = jnp.sum(w, axis=0, keepdims=True)
    w = (w / jnp.where(s > 0.0, s, 1.0)).T
    zeros = jnp.zeros((LANES, cols), F32)
    for t in (range(lanes // LANES) if tiles is None else tiles):
        at = slice(t * LANES, (t + 1) * LANES)
        tile = jnp.concatenate([w[at], zeros], axis=1)
        band = pltpu.roll(tile, (t * LANES - margin) % wide, 1, stride=1, stride_axis=0)
        if t * LANES < cols:
            own, halo = band[:, 0:cols].T, band[:, cols:]
            own_high, own_low = split(own)
            main[0:cols, at] = own_high
            main[cols:2 * cols, at] = own_low
            main[2 * cols:3 * cols, at] = own_high
            high = halo.astype(BF).astype(F32)
            packed = high + pltpu.roll(high, 2 * margin, 1) + pltpu.roll(halo - high, 4 * margin, 1)
            main[3 * cols:, at] = packed.T.astype(BF)
        else:
            low_own, high_own, halo = band[:, 0:LANES].T, band[:, cols - LANES:cols].T, band[:, cols:].T
            near = jnp.concatenate([
                halo[0:width], low_own[0:LANES // 2 - width], high_own[LANES // 2 + width:],
                halo[LANES - width:]], axis=0)
            high, low = split(near)
            edge[0:LANES] = high
            edge[LANES:2 * LANES] = high
            edge[2 * LANES:] = low


def y_filter(value, margin, cols, main, put, edge=None):
    high, low = split(value[:, 0:cols])
    halo = value[:, cols:]
    lane = lax.broadcasted_iota(jnp.int32, halo.shape, 1)
    near = jnp.where((lane < margin) | (lane >= LANES - margin), halo, 0.0)
    near_high = near.astype(BF).astype(F32)
    packed = near_high + pltpu.roll(near - near_high, 2 * margin, 1) + pltpu.roll(near_high, 4 * margin, 1)
    put(dot(jnp.concatenate([high, high, low, packed.astype(BF)], axis=1), main[...]), slice(0, cols))
    if edge is not None:
        width = 2 * margin
        own = jnp.where(lane < LANES // 2, pltpu.roll(value[:, 0:LANES], width, 1),
                        pltpu.roll(value[:, cols - LANES:cols], LANES - width, 1))
        ends = jnp.where((lane < width) | (lane >= LANES - width), halo, own)
        high, low = split(ends)
        put(dot(jnp.concatenate([high, low, high], axis=1), edge[...]), slice(cols, cols + LANES))


def x_filter(zh, zl, start, count, lanes, weights, put):
    step = weights.shape[0] // 2
    for s in range(0, count, step):
        size = min(step, count - s)
        at = slice(start + s, start + s + LANES)
        data = jnp.concatenate([zh[at, lanes], zl[at, lanes]], axis=0)
        if size == step:
            r = dot(weights[...], data)
        else:
            r = dot(jnp.concatenate([weights[0:size], weights[step:step + size]], axis=0), data)
        put(s, size, r[0:size] + r[size:])


def stacked(values):
    return jnp.concatenate(values, axis=0)


def interior_kernel(nx, ny, width, batch, v_hbm, t_hbm, gx_hbm, tx_hbm, ty_hbm,
                    halo, corners, z1h, z1l, zph, zpl, z2h, z2l, sub, ger, gxe, txe, gym, gye, tym,
                    ext, v_ref, t_ref, gx_ref, tx_ref, ty_ref, text_ref, gxw, txw,
                    pack_d, pack_u, from_d, from_u, t_low, t_high,
                    coarse, tested, zh, zl, load_sem, send_sem, recv_sem, ready):
    comps, rows, cols = v_ref.shape
    taps = t_ref.shape[0]
    margin = width // 2
    pairs, inner, _ = sub.shape
    innermost = ger.shape[1]
    me_x, me_y = lax.axis_index("gx"), lax.axis_index("gy")
    first, last = me_x == 0, me_x == nx - 1
    has_up, has_down = me_y < ny - 1, me_y > 0
    vertical = jnp.where(has_up, 1, 0) + jnp.where(has_down, 1, 0)
    not_first, not_last = me_x > 0, me_x < nx - 1
    sides = ((1, has_up), (-1, has_down))

    def device(dx, dy):
        return {"gx": lax.rem(me_x + dx + nx, nx), "gy": lax.rem(me_y + dy + ny, ny)}

    def signal(sem, dx, dy):
        pl.semaphore_signal(sem, inc=1, device_id=device(dx, dy), device_id_type=MESH)

    barrier = pltpu.get_barrier_semaphore()
    signal(barrier, -1, 0)
    pl.when(not_last)(lambda: signal(barrier, 1, 0))
    for sign, present in sides:
        @pl.when(present)
        def _(sign=sign):
            signal(barrier, 0, sign)
            signal(barrier, -1, sign)

        pl.when(present & not_last)(lambda sign=sign: signal(barrier, 1, sign))

    loads = [pltpu.make_async_copy(src, dst, load_sem.at[i]) for i, (src, dst) in enumerate((
        (v_hbm, v_ref), (t_hbm, t_ref), (gx_hbm, gx_ref), (tx_hbm, tx_ref), (ty_hbm, ty_ref)))]
    for load in loads:
        load.start()
    per = LANES // width
    groups = rows // width
    loads[0].wait()
    for c in range(comps):
        for g in range(groups):
            for q in range(per):
                src = pl.ds(g * width + q * SUB, SUB)
                dst = pl.ds(g * SUB, SUB)
                pack_u[c, dst, q * width:(q + 1) * width] = v_ref[c, src, cols - width:cols]
                pack_d[c, dst, q * width:(q + 1) * width] = v_ref[c, src, 0:width]
    pl.semaphore_wait(barrier, 1 + 2 * vertical + jnp.where(first, 0, 1 + vertical))

    head, tail = pl.ds(0, SUB), pl.ds((groups - 1) * SUB, SUB)
    sources = [
        v_hbm.at[:, pl.ds(rows - width, width), :], v_hbm.at[:, pl.ds(0, width), :],
        pack_u, pack_d,
        pack_u.at[:, tail, :], pack_u.at[:, head, :], pack_d.at[:, tail, :], pack_d.at[:, head, :],
    ]
    targets = [halo.at[0], halo.at[1], from_d, from_u] + [corners.at[i] for i in range(4)]
    copies = {}
    for i, where in enumerate(DIRECTIONS):
        copies[where] = pltpu.make_async_remote_copy(
            src_ref=sources[i], dst_ref=targets[i], send_sem=send_sem.at[i],
            recv_sem=recv_sem.at[i], device_id=device(*where), device_id_type=MESH)
    tables = {}
    for i, (sign, src, dst) in enumerate((
        (1, t_ref.at[:, pl.ds(cols - LANES, LANES)], t_low),
        (-1, t_ref.at[:, pl.ds(0, LANES)], t_high),
    )):
        n = len(DIRECTIONS) + i
        tables[sign] = pltpu.make_async_remote_copy(
            src_ref=src, dst_ref=dst, send_sem=send_sem.at[n],
            recv_sem=recv_sem.at[n], device_id=device(0, sign), device_id_type=MESH)

    copies[1, 0].start()

    @pl.when(last)
    def _():
        signal(ready, 1, 0)
        for sign, present in sides:
            pl.when(present)(lambda sign=sign: signal(ready, 1, sign))

    pl.when(not_first)(lambda: copies[-1, 0].start())
    loads[1].wait()
    for sign, present in sides:
        @pl.when(present)
        def _(sign=sign):
            copies[0, sign].start()
            tables[sign].start()
            copies[1, sign].start()

        pl.when(present & not_first)(lambda sign=sign: copies[-1, sign].start())

    ext[:, :, cols:] = jnp.zeros((comps, rows, LANES), F32)
    text_ref[...] = jnp.zeros_like(text_ref)
    for sign, present in sides:
        @pl.when(jnp.logical_not(present))
        def _(sign=sign):
            for side in range(2):
                corners[side + (2 if sign > 0 else 0)] = jnp.zeros(corners.shape[1:], F32)

    for c in range(comps):
        ext[c, :, 0:cols] = v_ref[c]
    text_ref[0:taps, 0:cols] = t_ref[...]
    for load in loads[2:]:
        load.wait()
    first_row, total = me_y * cols, cols * ny
    x_weights(gx_ref, gxw.shape[0] // 2, gxw, gxe)
    x_weights(tx_ref, txw.shape[0] // 2, txw, txe)
    own_tiles = range(cols // LANES)
    y_weights(t_ref[...], taps, first_row, total, cols, gym, tiles=own_tiles)
    y_weights(ty_ref[...], taps, first_row, total, cols, tym, tiles=own_tiles)
    filled = zh.shape[1]
    for slot in range(zh.shape[0]):
        zh[slot, inner:filled, :] = jnp.zeros((filled - inner, cols + LANES), BF)
        zl[slot, inner:filled, :] = jnp.zeros((filled - inner, cols + LANES), BF)

    for sign, present, lane, mid, tile, at in (
        (1, has_down, cols + LANES - width, from_d, t_low, LANES - margin),
        (-1, has_up, cols, from_u, t_high, 0),
    ):
        @pl.when(present)
        def _(sign=sign, lane=lane, mid=mid, tile=tile, at=at):
            copies[0, sign].wait_recv()
            tables[sign].wait_recv()
            for c in range(comps):
                for g in range(groups):
                    for q in range(per):
                        ext[c, pl.ds(g * width + q * SUB, SUB), lane:lane + width] = (
                            mid[c, pl.ds(g * SUB, SUB), q * width:(q + 1) * width])
            text_ref[0:taps, cols + at:cols + at + margin] = tile[:, at:at + margin]

    y_weights(text_ref[...], taps, first_row, total, cols, gym, gye, tiles=(cols // LANES,))

    own = slice(0, cols)
    everything = slice(0, cols + LANES)

    def store(slot, n, count):
        def put(z, lanes):
            high, low = split(z)
            for b in range(n):
                at = slice(b * count, (b + 1) * count)
                zh[slot + b, 0:count, lanes], zl[slot + b, 0:count, lanes] = high[at], low[at]
        return put

    def keep(slot, count, size, lanes, high, low, index):
        for side, at in enumerate((slice(0, size), slice(count - size, count))):
            high[index, side] = zh[slot, at, lanes]
            low[index, side] = zl[slot, at, lanes]

    y_filter(stacked([ext[c] for c in range(comps)]), margin, cols, gym, store(0, comps, rows), gye)
    for c in range(comps):
        def put(start, size, value, c=c):
            coarse[c, pl.ds(start, size), :] = value

        x_filter(zh.at[c], zl.at[c], 0, inner, everything, gxw, put)
        keep(c, rows, width, everything, z1h, z1l, c)
    y_filter(stacked([coarse[c] for c in range(comps)]), margin, cols, tym, store(0, comps, inner))
    for c in range(comps):
        def put_tested(start, size, value, c=c):
            tested[c, pl.ds(start, size), :] = value

        x_filter(zh.at[c], zl.at[c], 0, innermost, own, txw, put_tested)
        keep(c, inner, width, own, z2h, z2l, c)

    @pl.when(first)
    def _():
        pl.semaphore_wait(ready, 1 + vertical)
        copies[-1, 0].start()
        for sign, present in sides:
            pl.when(present)(lambda sign=sign: copies[-1, sign].start())

    @pl.loop(0, pairs // batch)
    def _(step):
        indices = [(step * batch + b,) + pair_of(step * batch + b) for b in range(batch)]
        y_filter(stacked([ext[i] * ext[j] for _, i, j in indices]), margin, cols, gym, store(0, batch, rows))
        y_filter(stacked([coarse[i] * coarse[j] for _, i, j in indices]),
                 margin, cols, tym, store(batch, batch, inner))
        for b, (p, i, j) in enumerate(indices):
            def put_sub(start, size, value, p=p, i=i, j=j):
                at = pl.ds(start, size)
                sub[p, at, :] = value - coarse[i, at, own] * coarse[j, at, own]

            x_filter(zh.at[b], zl.at[b], 0, inner, own, gxw, put_sub)
            keep(b, rows, width + margin, own, zph, zpl, p)
        for b, (p, i, j) in enumerate(indices):
            def put_ger(start, size, value, p=p, i=i, j=j):
                at = pl.ds(start, size)
                ger[p, at, :] = value - tested[i, at, :] * tested[j, at, :]

            x_filter(zh.at[batch + b], zl.at[batch + b], 0, innermost, own, txw, put_ger)
            keep(batch + b, inner, width, own, z2h, z2l, comps + p)

    copies[1, 0].wait_recv()
    copies[-1, 0].wait_recv()
    for sign, present in ((1, has_down), (-1, has_up)):
        @pl.when(present)
        def _(sign=sign):
            copies[1, sign].wait_recv()
            copies[-1, sign].wait_recv()

    copies[1, 0].wait_send()
    copies[-1, 0].wait_send()
    for sign, present in sides:
        @pl.when(present)
        def _(sign=sign):
            for dx in (0, 1, -1):
                copies[dx, sign].wait_send()
            tables[sign].wait_send()


def edge_kernel(margin, halo, corners, z1h, z1l, zph, zpl, z2h, z2l, sub_in, ger_in,
                gxe, txe, gym, gye, tym, sub_ref, ger_ref, sub_e, ger_e, sems):
    comps, cols = halo.shape[1], halo.shape[3]
    pairs, rows, _ = sub_ref.shape
    width = 2 * margin
    inner, innermost = sub_in.shape[1], ger_in.shape[1]
    order = [(i, j) for i in range(comps) for j in range(i, comps)]
    outs = []

    def leave(source, target):
        copy = pltpu.make_async_copy(source, target, sems.at[len(outs)])
        copy.start()
        outs.append(copy)

    for p in range(pairs):
        leave(sub_in.at[p], sub_ref.at[p, pl.ds(margin, inner), :])
        leave(ger_in.at[p], ger_ref.at[p, pl.ds(width, innermost), :])

    lane = lax.broadcasted_iota(jnp.int32, (SUB, LANES), 1)

    def ends(side, c):
        up, down = corners[2 + side, c], corners[side, c]
        blocks = []
        for q in range(width // SUB):
            low = pltpu.roll(up, (LANES - q * width) % LANES, 1)
            high = pltpu.roll(down, (LANES - (q + 1) * width) % LANES, 1)
            blocks.append(jnp.where(lane < width, low, jnp.where(lane >= LANES - width, high, 0.0)))
        return jnp.concatenate([halo[side, c], jnp.concatenate(blocks, axis=0)], axis=1)

    def filtered(values, main, edge=None):
        parts = []
        y_filter(stacked(values), margin, cols, main, lambda z, lanes: parts.append(z), edge)
        high, low = split(parts[0] if edge is None else jnp.concatenate(parts, axis=1))
        size = values[0].shape[0]
        return [(high[n * size:(n + 1) * size], low[n * size:(n + 1) * size]) for n in range(len(values))]

    def window(side, late, high, low):
        h = (late[0], high) if side == 0 else (high, late[0])
        l = (late[1], low) if side == 0 else (low, late[1])
        return stacked((h + l) * 2)

    both = [(c, side) for c in range(comps) for side in range(2)]
    every = [(p, side) for p in range(pairs) for side in range(2)]
    ext = {key: ends(key[1], key[0]) for key in both}
    late = filtered([ext[key] for key in both], gym, gye)
    coarse = {}
    for (c, side), z in zip(both, late):
        coarse[c, side] = dot(gxe[...], window(side, z, z1h[c, side], z1l[c, side]))
    at = (slice(width - margin, width), slice(0, margin))
    late = filtered([ext[order[p][0], side][at[side]] * ext[order[p][1], side][at[side]] for p, side in every], gym)
    for (p, side), z in zip(every, late):
        weights = gxe[0:margin] if side == 0 else gxe[width - margin:width]
        value = dot(weights, window(side, z, zph[p, side], zpl[p, side]))
        i, j = order[p]
        sub_e[p, side] = value - coarse[i, side][at[side], 0:cols] * coarse[j, side][at[side], 0:cols]
    leave(sub_e.at[:, 0], sub_ref.at[:, pl.ds(0, margin), :])
    leave(sub_e.at[:, 1], sub_ref.at[:, pl.ds(rows - margin, margin), :])
    late = filtered([coarse[key] for key in both]
                    + [coarse[order[p][0], side] * coarse[order[p][1], side] for p, side in every], tym)
    tested = {}
    for (c, side), z in zip(both, late):
        tested[c, side] = dot(txe[...], window(side, z, z2h[c, side], z2l[c, side]))
    for (p, side), z in zip(every, late[len(both):]):
        value = dot(txe[...], window(side, z, z2h[comps + p, side], z2l[comps + p, side]))
        i, j = order[p]
        ger_e[p, side] = value - tested[i, side] * tested[j, side]
    leave(ger_e.at[:, 0], ger_ref.at[:, pl.ds(0, width), :])
    leave(ger_e.at[:, 1], ger_ref.at[:, pl.ds(rows - width, width), :])
    for copy in outs:
        copy.wait()


def local(nx, ny, velocity, grid_x, grid_y, test_x, test_y):
    comps, planes, cols, rows = velocity.shape
    taps = grid_x.shape[0]
    margin = (taps - 1) // 2
    width = 2 * margin
    wide = cols + LANES
    step = LANES - width
    pairs = comps * (comps + 1) // 2
    batch = 2
    slots = max(comps, 2 * batch)
    vmem = pl.BlockSpec(memory_space=pltpu.VMEM)
    anywhere = pl.BlockSpec(memory_space=pl.ANY)
    packed = rows // width * SUB
    inner, innermost = rows - width, rows - 2 * width
    filled = max((n + step - 1) // step * step + width for n in (inner, innermost))
    fields = comps + pairs
    subs, gers = [], []
    shape = jax.ShapeDtypeStruct
    for plane in range(planes):
        v = jnp.swapaxes(velocity[:, plane], 1, 2)
        parts = pl.pallas_call(
            functools.partial(interior_kernel, nx, ny, width, batch),
            out_shape=(
                shape((2, comps, width, cols), F32),
                shape((4, comps, SUB, LANES), F32),
                shape((comps, 2, width, wide), BF),
                shape((comps, 2, width, wide), BF),
                shape((pairs, 2, width + margin, cols), BF),
                shape((pairs, 2, width + margin, cols), BF),
                shape((fields, 2, width, cols), BF),
                shape((fields, 2, width, cols), BF),
                shape((pairs, inner, cols), F32),
                shape((pairs, innermost, cols), F32),
                shape((width, 2 * LANES), BF),
                shape((width, 2 * LANES), BF),
                shape((3 * cols + LANES, cols), BF),
                shape((3 * LANES, LANES), BF),
                shape((3 * cols + LANES, cols), BF),
            ),
            in_specs=[pl.BlockSpec(memory_space=pltpu.HBM)] * 5,
            out_specs=(vmem,) * 15,
            scratch_shapes=[
                pltpu.VMEM((comps, rows, wide), F32),
                pltpu.VMEM((comps, rows, cols), F32),
                pltpu.VMEM((taps, cols), F32),
                pltpu.VMEM((1, taps), F32),
                pltpu.VMEM((1, taps), F32),
                pltpu.VMEM((taps, cols), F32),
                pltpu.VMEM((round_up(taps, SUB), wide), F32),
                pltpu.VMEM((2 * step, 2 * LANES), BF),
                pltpu.VMEM((2 * step, 2 * LANES), BF),
                pltpu.VMEM((comps, packed, LANES), F32),
                pltpu.VMEM((comps, packed, LANES), F32),
                pltpu.VMEM((comps, packed, LANES), F32),
                pltpu.VMEM((comps, packed, LANES), F32),
                pltpu.VMEM((taps, LANES), F32),
                pltpu.VMEM((taps, LANES), F32),
                pltpu.VMEM((comps, inner, wide), F32),
                pltpu.VMEM((comps, innermost, cols), F32),
                pltpu.VMEM((slots, max(rows, filled), wide), BF),
                pltpu.VMEM((slots, max(rows, filled), wide), BF),
                pltpu.SemaphoreType.DMA((5,)),
                pltpu.SemaphoreType.DMA((len(DIRECTIONS) + 2,)),
                pltpu.SemaphoreType.DMA((len(DIRECTIONS) + 2,)),
                pltpu.SemaphoreType.REGULAR,
            ],
            compiler_params=pltpu.CompilerParams(
                collective_id=plane, has_side_effects=True, vmem_limit_bytes=48 << 20),
            name="interior",
        )(*[pltpu.with_memory_space_constraint(x, pltpu.HBM) for x in (
            v, grid_y.T, grid_x.reshape(1, taps), test_x.reshape(1, taps), test_y.T)])
        out = shape((pairs, rows, cols), F32)
        sub, ger = pl.pallas_call(
            functools.partial(edge_kernel, margin),
            out_shape=(out, out),
            in_specs=[vmem] * 15,
            out_specs=(anywhere, anywhere),
            scratch_shapes=[
                pltpu.VMEM((pairs, 2, margin, cols), F32),
                pltpu.VMEM((pairs, 2, width, cols), F32),
                pltpu.SemaphoreType.DMA((2 * pairs + 4,)),
            ],
            compiler_params=pltpu.CompilerParams(vmem_limit_bytes=48 << 20),
            name="edge",
        )(*parts)
        subs.append(jnp.swapaxes(sub, 1, 2))
        gers.append(jnp.swapaxes(ger, 1, 2))
    return jnp.stack(subs, axis=1), jnp.stack(gers, axis=1)


def solution(mesh):
    nx, ny = mesh.shape["gx"], mesh.shape["gy"]
    field = P(None, None, "gy", "gx")
    return jax.shard_map(
        functools.partial(local, nx, ny),
        mesh=mesh,
        in_specs=(field, P(), P("gy", None), P(), P("gy", None)),
        out_specs=(field, field),
        check_vma=False,
    )
```

```python
import functools

import jax
import jax.numpy as jnp
from jax import lax
from jax.experimental import pallas as pl
from jax.experimental.pallas import tpu as pltpu
from jax.sharding import PartitionSpec as P

MESH = pl.DeviceIdType.MESH
LANES = 128
SUB = 8
BF = jnp.bfloat16
F32 = jnp.float32


def round_up(value, unit):
    return (value + unit - 1) // unit * unit


def split(value):
    high = value.astype(BF)
    return high, (value - high.astype(F32)).astype(BF)


def pair_of(p):
    first = jnp.where(p < 3, 0, jnp.where(p < 5, 1, 2))
    second = jnp.where(p < 3, p, jnp.where(p < 5, p - 2, 2))
    return first, second


def dot(a, b):
    return jnp.dot(a, b, preferred_element_type=F32)


def x_weights(w_ref, step, out, edge):
    taps = w_ref.shape[1]
    w = jnp.concatenate([w_ref[...], jnp.zeros((1, LANES - taps), F32)], axis=1)
    w = w / jnp.sum(w)
    band = pltpu.roll(jnp.broadcast_to(w, (LANES, LANES)), 0, 1, stride=1, stride_axis=0)
    high, low = split(band[0:step])
    out[0:step, 0:LANES] = high
    out[0:step, LANES:] = high
    out[step:, 0:LANES] = low
    out[step:, LANES:] = jnp.zeros((step, LANES), BF)
    width = edge.shape[0] // 2
    high, low = split(band[0:width])
    high = high.astype(F32)
    edge[0:width] = (high + pltpu.roll(high, 2 * width, 1)).astype(BF)
    edge[width:] = low


def y_weights(table, taps, first_row, total, cols, main, edge=None, tiles=None):
    margin = (taps - 1) // 2
    width = 2 * margin
    lanes = table.shape[1]
    wide = cols + LANES
    k = lax.broadcasted_iota(jnp.int32, (LANES, lanes), 0)
    lane = lax.broadcasted_iota(jnp.int32, (LANES, lanes), 1)
    y = first_row + jnp.where(lane < cols + LANES // 2, lane, lane - wide)
    source = y + k - margin
    keep = (k < taps) & (source >= 0) & (source < total) & (y >= 0) & (y < total)
    w = jnp.where(keep, jnp.concatenate(
        [table, jnp.zeros((LANES - table.shape[0], lanes), F32)], axis=0), 0.0)
    s = jnp.sum(w, axis=0, keepdims=True)
    w = (w / jnp.where(s > 0.0, s, 1.0)).T
    zeros = jnp.zeros((LANES, cols), F32)
    for t in (range(lanes // LANES) if tiles is None else tiles):
        at = slice(t * LANES, (t + 1) * LANES)
        tile = jnp.concatenate([w[at], zeros], axis=1)
        band = pltpu.roll(tile, (t * LANES - margin) % wide, 1, stride=1, stride_axis=0)
        if t * LANES < cols:
            own, halo = band[:, 0:cols].T, band[:, cols:]
            own_high, own_low = split(own)
            main[0:cols, at] = own_high
            main[cols:2 * cols, at] = own_low
            main[2 * cols:3 * cols, at] = own_high
            high = halo.astype(BF).astype(F32)
            packed = high + pltpu.roll(high, 2 * margin, 1) + pltpu.roll(halo - high, 4 * margin, 1)
            main[3 * cols:, at] = packed.T.astype(BF)
        else:
            low_own, high_own, halo = band[:, 0:LANES].T, band[:, cols - LANES:cols].T, band[:, cols:].T
            near = jnp.concatenate([
                halo[0:width], low_own[0:LANES // 2 - width], high_own[LANES // 2 + width:],
                halo[LANES - width:]], axis=0)
            high, low = split(near)
            edge[0:LANES] = high
            edge[LANES:2 * LANES] = high
            edge[2 * LANES:] = low


def y_own(value, cols, main):
    high, low = split(value)
    return dot(jnp.concatenate([high, high, low], axis=1), main[0:3 * cols])


def packed_halo(halo, margin):
    lane = lax.broadcasted_iota(jnp.int32, halo.shape, 1)
    near = jnp.where((lane < margin) | (lane >= LANES - margin), halo, 0.0)
    high = near.astype(BF).astype(F32)
    return (high + pltpu.roll(near - high, 2 * margin, 1) + pltpu.roll(high, 4 * margin, 1)).astype(BF)


def y_halo(halo, margin, cols, main):
    return dot(packed_halo(halo, margin), main[3 * cols:])


def y_filter(value, margin, cols, main):
    high, low = split(value[:, 0:cols])
    return dot(jnp.concatenate([high, high, low, packed_halo(value[:, cols:], margin)], axis=1), main[...])


def y_ends(value, margin, cols, edge):
    width = 2 * margin
    halo = value[:, cols:]
    lane = lax.broadcasted_iota(jnp.int32, halo.shape, 1)
    own = jnp.where(lane < LANES // 2, pltpu.roll(value[:, 0:LANES], width, 1),
                    pltpu.roll(value[:, cols - LANES:cols], LANES - width, 1))
    high, low = split(jnp.where((lane < width) | (lane >= LANES - width), halo, own))
    return dot(jnp.concatenate([high, low, high], axis=1), edge[...])


def side_lanes(up, down, q, width):
    lane = lax.broadcasted_iota(jnp.int32, up.shape, 1)
    low = pltpu.roll(up, (LANES - q * width) % LANES, 1)
    high = pltpu.roll(down, (LANES - (q + 1) * width) % LANES, 1)
    return jnp.where(lane < width, low, jnp.where(lane >= LANES - width, high, 0.0))


def x_filter(zh, zl, start, count, lanes, weights, put):
    step = weights.shape[0] // 2
    for s in range(0, count, step):
        size = min(step, count - s)
        at = slice(start + s, start + s + LANES)
        data = jnp.concatenate([zh[at, lanes], zl[at, lanes]], axis=0)
        if size == step:
            r = dot(weights[...], data)
        else:
            r = dot(jnp.concatenate([weights[0:size], weights[step:step + size]], axis=0), data)
        put(s, size, r[0:size] + r[size:])


def stacked(values):
    return jnp.concatenate(values, axis=0)


def interior_kernel(nx, ny, width, batch, v_hbm, t_hbm, gx_hbm, tx_hbm, ty_hbm,
                    halo, corners, z1h, z1l, zph, zpl, z2h, z2l, sub, ger, gxe, txe, gym, gye, tym,
                    ext, t_ref, gx_ref, tx_ref, ty_ref, text_ref, gxw, txw,
                    pack_d, pack_u, from_d, from_u, t_low, t_high,
                    own_v, own_p, coarse, tested, zh, zl, load_sem, send_sem, recv_sem, ready):
    comps, rows, _ = ext.shape
    taps, cols = t_ref.shape
    margin = width // 2
    pairs, inner, _ = sub.shape
    innermost = ger.shape[1]
    me_x, me_y = lax.axis_index("gx"), lax.axis_index("gy")
    first, last = me_x == 0, me_x == nx - 1
    has_up, has_down = me_y < ny - 1, me_y > 0
    vertical = jnp.where(has_up, 1, 0) + jnp.where(has_down, 1, 0)
    not_first, not_last = me_x > 0, me_x < nx - 1
    sides = ((1, has_up), (-1, has_down))

    def device(dx, dy):
        return {"gx": lax.rem(me_x + dx + nx, nx), "gy": lax.rem(me_y + dy + ny, ny)}

    def signal(sem, dx, dy):
        pl.semaphore_signal(sem, inc=1, device_id=device(dx, dy), device_id_type=MESH)

    barrier = pltpu.get_barrier_semaphore()
    signal(barrier, -1, 0)
    pl.when(not_last)(lambda: signal(barrier, 1, 0))
    for sign, present in sides:
        @pl.when(present)
        def _(sign=sign):
            signal(barrier, 0, sign)
            signal(barrier, -1, sign)

        pl.when(present & not_last)(lambda sign=sign: signal(barrier, 1, sign))

    own = slice(0, cols)
    everything = slice(0, cols + LANES)
    loads = [pltpu.make_async_copy(src, dst, load_sem.at[i]) for i, (src, dst) in enumerate((
        (t_hbm, t_ref), (gx_hbm, gx_ref), (tx_hbm, tx_ref), (ty_hbm, ty_ref),
        (v_hbm, ext.at[:, :, own])))]
    for load in loads:
        load.start()

    text_ref[...] = jnp.zeros_like(text_ref)
    filled = zh.shape[1]
    for slot in range(zh.shape[0]):
        zh[slot, inner:filled, :] = jnp.zeros((filled - inner, cols + LANES), BF)
        zl[slot, inner:filled, :] = jnp.zeros((filled - inner, cols + LANES), BF)
    for sign, present, mid in ((1, has_up, from_u), (-1, has_down, from_d)):
        @pl.when(jnp.logical_not(present))
        def _(sign=sign, mid=mid):
            mid[...] = jnp.zeros_like(mid)
            for side in range(2):
                corners[side + (2 if sign > 0 else 0)] = jnp.zeros(corners.shape[1:], F32)

    for load in loads[:4]:
        load.wait()
    text_ref[0:taps, 0:cols] = t_ref[...]
    first_row, total = me_y * cols, cols * ny
    own_tiles = range(cols // LANES)
    y_weights(t_ref[...], taps, first_row, total, cols, gym, tiles=own_tiles)

    per = LANES // width
    groups = rows // width
    loads[4].wait()
    for c in range(comps):
        for g in range(groups):
            for q in range(per):
                src = pl.ds(g * width + q * SUB, SUB)
                dst = pl.ds(g * SUB, SUB)
                pack_u[c, dst, q * width:(q + 1) * width] = ext[c, src, cols - width:cols]
                pack_d[c, dst, q * width:(q + 1) * width] = ext[c, src, 0:width]
    pl.semaphore_wait(barrier, 1 + 2 * vertical + jnp.where(first, 0, 1 + vertical))

    head, tail = pl.ds(0, SUB), pl.ds((groups - 1) * SUB, SUB)
    low_x, high_x = v_hbm.at[:, pl.ds(0, width), :], v_hbm.at[:, pl.ds(rows - width, width), :]
    copies = {}

    def remote(key, src, dst, dx, dy):
        n = len(copies)
        copies[key] = pltpu.make_async_remote_copy(
            src_ref=src, dst_ref=dst, send_sem=send_sem.at[n], recv_sem=recv_sem.at[n],
            device_id=device(dx, dy), device_id_type=MESH)

    remote((1, 0), high_x, halo.at[0], 1, 0)
    remote((-1, 0), low_x, halo.at[1], -1, 0)
    remote((1, 1), pack_u.at[:, tail, :], corners.at[0], 1, 1)
    remote((-1, 1), pack_u.at[:, head, :], corners.at[1], -1, 1)
    remote((1, -1), pack_d.at[:, tail, :], corners.at[2], 1, -1)
    remote((-1, -1), pack_d.at[:, head, :], corners.at[3], -1, -1)
    remote(("t", 1), t_ref.at[:, pl.ds(cols - LANES, LANES)], t_low, 0, 1)
    remote(("t", -1), t_ref.at[:, pl.ds(0, LANES)], t_high, 0, -1)
    for c in range(comps):
        remote((c, "v", 1), pack_u.at[c], from_d.at[c], 0, 1)
        remote((c, "v", -1), pack_d.at[c], from_u.at[c], 0, -1)

    pl.when(last)(lambda: copies[1, 0].start())
    for sign, present in sides:
        @pl.when(present)
        def _(sign=sign):
            copies["t", sign].start()
            for c in range(comps):
                copies[c, "v", sign].start()

    @pl.when(last)
    def _():
        signal(ready, 1, 0)
        for sign, present in sides:
            pl.when(present)(lambda sign=sign: signal(ready, 1, sign))

    pl.when(not_last)(lambda: copies[1, 0].start())
    pl.when(not_first)(lambda: copies[-1, 0].start())
    for sign, present in sides:
        pl.when(present)(lambda sign=sign: copies[1, sign].start())
        pl.when(present & not_first)(lambda sign=sign: copies[-1, sign].start())

    for c in range(comps):
        own_v[c] = y_own(ext[c, :, own], cols, gym)

    @pl.loop(0, pairs // batch)
    def _(step):
        indices = [(step * batch + b,) + pair_of(step * batch + b) for b in range(batch)]
        z = y_own(stacked([ext[i, :, own] * ext[j, :, own] for _, i, j in indices]), cols, gym)
        for b, (p, _, _) in enumerate(indices):
            own_p[p] = z[b * rows:(b + 1) * rows]

    x_weights(gx_ref, gxw.shape[0] // 2, gxw, gxe)
    x_weights(tx_ref, txw.shape[0] // 2, txw, txe)
    y_weights(ty_ref[...], taps, first_row, total, cols, tym, tiles=own_tiles)

    for sign, present, tile, at in ((1, has_down, t_low, LANES - margin), (-1, has_up, t_high, 0)):
        @pl.when(present)
        def _(sign=sign, tile=tile, at=at):
            copies["t", sign].wait_recv()
            text_ref[0:taps, cols + at:cols + at + margin] = tile[:, at:at + margin]

    y_weights(text_ref[...], taps, first_row, total, cols, gym, gye, tiles=(cols // LANES,))

    def store(slot, count, lanes, z):
        high, low = split(z)
        for b in range(z.shape[0] // count):
            at = slice(b * count, (b + 1) * count)
            zh[slot + b, 0:count, lanes], zl[slot + b, 0:count, lanes] = high[at], low[at]

    def keep(slot, count, size, lanes, high, low, index):
        for side, at in enumerate((slice(0, size), slice(count - size, count))):
            high[index, side] = zh[slot, at, lanes]
            low[index, side] = zl[slot, at, lanes]

    for c in range(comps):
        for sign, present in ((1, has_down), (-1, has_up)):
            pl.when(present)(lambda sign=sign, c=c: copies[c, "v", sign].wait_recv())
        for g in range(groups):
            at = pl.ds(g * SUB, SUB)
            up, down = from_u[c, at, :], from_d[c, at, :]
            for q in range(per):
                ext[c, pl.ds(g * width + q * SUB, SUB), cols:] = side_lanes(up, down, q, width)
        store(c, rows, own, own_v[c] + y_halo(ext[c, :, cols:], margin, cols, gym))
        store(c, rows, slice(cols, cols + LANES), y_ends(ext[c], margin, cols, gye))

        def put(start, size, value, c=c):
            coarse[c, pl.ds(start, size), :] = value

        x_filter(zh.at[c], zl.at[c], 0, inner, everything, gxw, put)
        keep(c, rows, width, everything, z1h, z1l, c)
    store(0, inner, own, y_filter(stacked([coarse[c] for c in range(comps)]), margin, cols, tym))
    for c in range(comps):
        def put_tested(start, size, value, c=c):
            tested[c, pl.ds(start, size), :] = value

        x_filter(zh.at[c], zl.at[c], 0, innermost, own, txw, put_tested)
        keep(c, inner, width, own, z2h, z2l, c)

    @pl.when(first)
    def _():
        pl.semaphore_wait(ready, 1 + vertical)
        copies[-1, 0].start()
        for sign, present in sides:
            pl.when(present)(lambda sign=sign: copies[-1, sign].start())

    @pl.loop(0, pairs // batch)
    def _(step):
        indices = [(step * batch + b,) + pair_of(step * batch + b) for b in range(batch)]
        halos = y_halo(stacked([ext[i, :, cols:] * ext[j, :, cols:] for _, i, j in indices]), margin, cols, gym)
        store(0, rows, own, stacked([own_p[p] for p, _, _ in indices]) + halos)
        store(batch, inner, own,
              y_filter(stacked([coarse[i] * coarse[j] for _, i, j in indices]), margin, cols, tym))
        for b, (p, i, j) in enumerate(indices):
            def put_sub(start, size, value, p=p, i=i, j=j):
                at = pl.ds(start, size)
                sub[p, at, :] = value - coarse[i, at, own] * coarse[j, at, own]

            x_filter(zh.at[b], zl.at[b], 0, inner, own, gxw, put_sub)
            keep(b, rows, width + margin, own, zph, zpl, p)
        for b, (p, i, j) in enumerate(indices):
            def put_ger(start, size, value, p=p, i=i, j=j):
                at = pl.ds(start, size)
                ger[p, at, :] = value - tested[i, at, :] * tested[j, at, :]

            x_filter(zh.at[batch + b], zl.at[batch + b], 0, innermost, own, txw, put_ger)
            keep(batch + b, inner, width, own, z2h, z2l, comps + p)

    copies[1, 0].wait_recv()
    copies[-1, 0].wait_recv()
    for sign, present in ((1, has_down), (-1, has_up)):
        @pl.when(present)
        def _(sign=sign):
            copies[1, sign].wait_recv()
            copies[-1, sign].wait_recv()

    copies[1, 0].wait_send()
    copies[-1, 0].wait_send()
    for sign, present in sides:
        @pl.when(present)
        def _(sign=sign):
            copies[1, sign].wait_send()
            copies[-1, sign].wait_send()
            copies["t", sign].wait_send()
            for c in range(comps):
                copies[c, "v", sign].wait_send()


def edge_kernel(margin, halo, corners, z1h, z1l, zph, zpl, z2h, z2l, sub_in, ger_in,
                gxe, txe, gym, gye, tym, sub_ref, ger_ref, sub_e, ger_e, sems):
    comps, cols = halo.shape[1], halo.shape[3]
    pairs, rows, _ = sub_ref.shape
    width = 2 * margin
    inner, innermost = sub_in.shape[1], ger_in.shape[1]
    order = [(i, j) for i in range(comps) for j in range(i, comps)]
    outs = []

    def leave(source, target):
        copy = pltpu.make_async_copy(source, target, sems.at[len(outs)])
        copy.start()
        outs.append(copy)

    for p in range(pairs):
        leave(sub_in.at[p], sub_ref.at[p, pl.ds(margin, inner), :])
        leave(ger_in.at[p], ger_ref.at[p, pl.ds(width, innermost), :])

    def ends(side, c):
        up, down = corners[2 + side, c], corners[side, c]
        blocks = [side_lanes(up, down, q, width) for q in range(width // SUB)]
        return jnp.concatenate([halo[side, c], jnp.concatenate(blocks, axis=0)], axis=1)

    def pieces(z, size, count):
        high, low = split(z)
        return [(high[n * size:(n + 1) * size], low[n * size:(n + 1) * size]) for n in range(count)]

    def x_ends(side, late, high, low, weights):
        h = (late[0], high) if side == 0 else (high, late[0])
        l = (late[1], low) if side == 0 else (low, late[1])
        r = dot(weights, stacked(h + l))
        half = weights.shape[0] // 2
        return r[0:half] + r[half:]

    both = [(c, side) for c in range(comps) for side in range(2)]
    every = [(p, side) for p in range(pairs) for side in range(2)]
    near = (slice(width - margin, width), slice(0, margin))
    ext = {key: ends(key[1], key[0]) for key in both}
    values = stacked([ext[key] for key in both])
    products = stacked([ext[order[p][0], side][near[side]] * ext[order[p][1], side][near[side]] for p, side in every])
    z = y_filter(stacked([values, products]), margin, cols, gym)
    count = len(both) * width
    late = pieces(jnp.concatenate([z[0:count], y_ends(values, margin, cols, gye)], axis=1), width, len(both))
    coarse = {}
    for (c, side), part in zip(both, late):
        coarse[c, side] = x_ends(side, part, z1h[c, side], z1l[c, side], gxe[...])
    late = pieces(z[count:], margin, len(every))
    for (p, side), part in zip(every, late):
        weights = stacked([gxe[0:margin], gxe[width:width + margin]] if side == 0 else
                          [gxe[width - margin:width], gxe[2 * width - margin:]])
        value = x_ends(side, part, zph[p, side], zpl[p, side], weights)
        i, j = order[p]
        sub_e[p, side] = value - coarse[i, side][near[side], 0:cols] * coarse[j, side][near[side], 0:cols]
    leave(sub_e.at[:, 0], sub_ref.at[:, pl.ds(0, margin), :])
    leave(sub_e.at[:, 1], sub_ref.at[:, pl.ds(rows - margin, margin), :])
    z = y_filter(stacked([coarse[key] for key in both]
                         + [coarse[order[p][0], side] * coarse[order[p][1], side] for p, side in every]),
                 margin, cols, tym)
    late = pieces(z, width, len(both) + len(every))
    tested = {}
    for (c, side), part in zip(both, late):
        tested[c, side] = x_ends(side, part, z2h[c, side], z2l[c, side], txe[...])
    for (p, side), part in zip(every, late[len(both):]):
        value = x_ends(side, part, z2h[comps + p, side], z2l[comps + p, side], txe[...])
        i, j = order[p]
        ger_e[p, side] = value - tested[i, side] * tested[j, side]
    leave(ger_e.at[:, 0], ger_ref.at[:, pl.ds(0, width), :])
    leave(ger_e.at[:, 1], ger_ref.at[:, pl.ds(rows - width, width), :])
    for copy in outs:
        copy.wait()


def local(nx, ny, velocity, grid_x, grid_y, test_x, test_y):
    comps, planes, cols, rows = velocity.shape
    taps = grid_x.shape[0]
    margin = (taps - 1) // 2
    width = 2 * margin
    wide = cols + LANES
    step = LANES - width
    pairs = comps * (comps + 1) // 2
    batch = 2
    slots = max(comps, 2 * batch)
    vmem = pl.BlockSpec(memory_space=pltpu.VMEM)
    anywhere = pl.BlockSpec(memory_space=pl.ANY)
    packed = rows // width * SUB
    inner, innermost = rows - width, rows - 2 * width
    filled = max((n + step - 1) // step * step + width for n in (inner, innermost))
    fields = comps + pairs
    subs, gers = [], []
    shape = jax.ShapeDtypeStruct
    for plane in range(planes):
        v = jnp.swapaxes(velocity[:, plane], 1, 2)
        parts = pl.pallas_call(
            functools.partial(interior_kernel, nx, ny, width, batch),
            out_shape=(
                shape((2, comps, width, cols), F32),
                shape((4, comps, SUB, LANES), F32),
                shape((comps, 2, width, wide), BF),
                shape((comps, 2, width, wide), BF),
                shape((pairs, 2, width + margin, cols), BF),
                shape((pairs, 2, width + margin, cols), BF),
                shape((fields, 2, width, cols), BF),
                shape((fields, 2, width, cols), BF),
                shape((pairs, inner, cols), F32),
                shape((pairs, innermost, cols), F32),
                shape((2 * width, LANES), BF),
                shape((2 * width, LANES), BF),
                shape((3 * cols + LANES, cols), BF),
                shape((3 * LANES, LANES), BF),
                shape((3 * cols + LANES, cols), BF),
            ),
            in_specs=[pl.BlockSpec(memory_space=pltpu.HBM)] * 5,
            out_specs=(vmem,) * 15,
            scratch_shapes=[
                pltpu.VMEM((comps, rows, wide), F32),
                pltpu.VMEM((taps, cols), F32),
                pltpu.VMEM((1, taps), F32),
                pltpu.VMEM((1, taps), F32),
                pltpu.VMEM((taps, cols), F32),
                pltpu.VMEM((round_up(taps, SUB), wide), F32),
                pltpu.VMEM((2 * step, 2 * LANES), BF),
                pltpu.VMEM((2 * step, 2 * LANES), BF),
                pltpu.VMEM((comps, packed, LANES), F32),
                pltpu.VMEM((comps, packed, LANES), F32),
                pltpu.VMEM((comps, packed, LANES), F32),
                pltpu.VMEM((comps, packed, LANES), F32),
                pltpu.VMEM((taps, LANES), F32),
                pltpu.VMEM((taps, LANES), F32),
                pltpu.VMEM((comps, rows, cols), F32),
                pltpu.VMEM((pairs, rows, cols), F32),
                pltpu.VMEM((comps, inner, wide), F32),
                pltpu.VMEM((comps, innermost, cols), F32),
                pltpu.VMEM((slots, max(rows, filled), wide), BF),
                pltpu.VMEM((slots, max(rows, filled), wide), BF),
                pltpu.SemaphoreType.DMA((5,)),
                pltpu.SemaphoreType.DMA((8 + 2 * comps,)),
                pltpu.SemaphoreType.DMA((8 + 2 * comps,)),
                pltpu.SemaphoreType.REGULAR,
            ],
            compiler_params=pltpu.CompilerParams(
                collective_id=plane, has_side_effects=True, vmem_limit_bytes=48 << 20),
            name="interior",
        )(*[pltpu.with_memory_space_constraint(x, pltpu.HBM) for x in (
            v, grid_y.T, grid_x.reshape(1, taps), test_x.reshape(1, taps), test_y.T)])
        out = shape((pairs, rows, cols), F32)
        sub, ger = pl.pallas_call(
            functools.partial(edge_kernel, margin),
            out_shape=(out, out),
            in_specs=[vmem] * 15,
            out_specs=(anywhere, anywhere),
            scratch_shapes=[
                pltpu.VMEM((pairs, 2, margin, cols), F32),
                pltpu.VMEM((pairs, 2, width, cols), F32),
                pltpu.SemaphoreType.DMA((2 * pairs + 4,)),
            ],
            compiler_params=pltpu.CompilerParams(vmem_limit_bytes=48 << 20),
            name="edge",
        )(*parts)
        subs.append(jnp.swapaxes(sub, 1, 2))
        gers.append(jnp.swapaxes(ger, 1, 2))
    return jnp.stack(subs, axis=1), jnp.stack(gers, axis=1)


def solution(mesh):
    nx, ny = mesh.shape["gx"], mesh.shape["gy"]
    field = P(None, None, "gy", "gx")
    return jax.shard_map(
        functools.partial(local, nx, ny),
        mesh=mesh,
        in_specs=(field, P(), P("gy", None), P(), P("gy", None)),
        out_specs=(field, field),
        check_vma=False,
    )
```

```python
import functools

import jax
import jax.numpy as jnp
from jax import lax
from jax.experimental import pallas as pl
from jax.experimental.pallas import tpu as pltpu
from jax.sharding import PartitionSpec as P

MESH = pl.DeviceIdType.MESH
LANES = 128
SUB = 8
BF = jnp.bfloat16
F32 = jnp.float32


def round_up(value, unit):
    return (value + unit - 1) // unit * unit


def split(value):
    high = value.astype(BF)
    return high, (value - high.astype(F32)).astype(BF)


def dot(a, b):
    return jnp.dot(a, b, preferred_element_type=F32)


def x_weights(w_ref, step, out, edge):
    taps = w_ref.shape[1]
    w = jnp.concatenate([w_ref[...], jnp.zeros((1, LANES - taps), F32)], axis=1)
    w = w / jnp.sum(w)
    band = pltpu.roll(jnp.broadcast_to(w, (LANES, LANES)), 0, 1, stride=1, stride_axis=0)
    high, low = split(band[0:step])
    out[:, 0:LANES] = high
    out[:, LANES:2 * LANES] = high
    out[:, 2 * LANES:] = low
    width = edge.shape[0] // 2
    high, low = split(band[0:width])
    high = high.astype(F32)
    edge[0:width] = (high + pltpu.roll(high, 2 * width, 1)).astype(BF)
    edge[width:] = low


def y_weights(table, taps, first_row, total, cols, main, edge=None, tiles=None):
    margin = (taps - 1) // 2
    width = 2 * margin
    lanes = table.shape[1]
    wide = cols + LANES
    k = lax.broadcasted_iota(jnp.int32, (LANES, lanes), 0)
    lane = lax.broadcasted_iota(jnp.int32, (LANES, lanes), 1)
    y = first_row + jnp.where(lane < cols + LANES // 2, lane, lane - wide)
    source = y + k - margin
    keep = (k < taps) & (source >= 0) & (source < total) & (y >= 0) & (y < total)
    w = jnp.where(keep, jnp.concatenate(
        [table, jnp.zeros((LANES - table.shape[0], lanes), F32)], axis=0), 0.0)
    s = jnp.sum(w, axis=0, keepdims=True)
    w = (w / jnp.where(s > 0.0, s, 1.0)).T
    zeros = jnp.zeros((LANES, cols), F32)
    for t in (range(lanes // LANES) if tiles is None else tiles):
        at = slice(t * LANES, (t + 1) * LANES)
        tile = jnp.concatenate([w[at], zeros], axis=1)
        band = pltpu.roll(tile, (t * LANES - margin) % wide, 1, stride=1, stride_axis=0)
        if t * LANES < cols:
            own, halo = band[:, 0:cols].T, band[:, cols:]
            own_high, own_low = split(own)
            main[0:cols, at] = own_high
            main[cols:2 * cols, at] = own_low
            main[2 * cols:3 * cols, at] = own_high
            high = halo.astype(BF).astype(F32)
            packed = high + pltpu.roll(high, 2 * margin, 1) + pltpu.roll(halo - high, 4 * margin, 1)
            main[3 * cols:, at] = packed.T.astype(BF)
        else:
            low_own, high_own, halo = band[:, 0:LANES].T, band[:, cols - LANES:cols].T, band[:, cols:].T
            near = jnp.concatenate([
                halo[0:width], low_own[0:LANES // 2 - width], high_own[LANES // 2 + width:],
                halo[LANES - width:]], axis=0)
            high, low = split(near)
            edge[0:LANES] = high
            edge[LANES:2 * LANES] = high
            edge[2 * LANES:] = low


def y_own(value, cols, main):
    high, low = split(value)
    return dot(jnp.concatenate([high, high, low], axis=1), main[0:3 * cols])


def packed_halo(halo, margin):
    lane = lax.broadcasted_iota(jnp.int32, halo.shape, 1)
    near = jnp.where((lane < margin) | (lane >= LANES - margin), halo, 0.0)
    high = near.astype(BF).astype(F32)
    return (high + pltpu.roll(near - high, 2 * margin, 1) + pltpu.roll(high, 4 * margin, 1)).astype(BF)


def y_halo(halo, margin, cols, main):
    return dot(packed_halo(halo, margin), main[3 * cols:])


def y_filter(value, margin, cols, main):
    high, low = split(value[:, 0:cols])
    return dot(jnp.concatenate([high, high, low, packed_halo(value[:, cols:], margin)], axis=1), main[...])


def y_ends(value, margin, cols, edge):
    width = 2 * margin
    halo = value[:, cols:]
    lane = lax.broadcasted_iota(jnp.int32, halo.shape, 1)
    own = jnp.where(lane < LANES // 2, pltpu.roll(value[:, 0:LANES], width, 1),
                    pltpu.roll(value[:, cols - LANES:cols], LANES - width, 1))
    high, low = split(jnp.where((lane < width) | (lane >= LANES - width), halo, own))
    return dot(jnp.concatenate([high, low, high], axis=1), edge[...])


def side_lanes(up, down, q, width):
    lane = lax.broadcasted_iota(jnp.int32, up.shape, 1)
    low = pltpu.roll(up, (LANES - q * width) % LANES, 1)
    high = pltpu.roll(down, (LANES - (q + 1) * width) % LANES, 1)
    return jnp.where(lane < width, low, jnp.where(lane >= LANES - width, high, 0.0))


def x_filter(zh, zl, count, weights, put):
    step = weights.shape[0]
    for s in range(0, count, step):
        size = min(step, count - s)
        at = slice(s, s + LANES)
        high = zh[at]
        put(slice(s, s + size), dot(weights[0:size], jnp.concatenate([high, zl[at], high], axis=0)))


def stacked(values):
    return jnp.concatenate(values, axis=0)


def interior_kernel(nx, ny, width, v_hbm, t_hbm, gx_hbm, tx_hbm, ty_hbm,
                    halo, corners, z1h, z1l, zph, zpl, z2h, z2l, sub, ger, gxe, txe, gym, gye, tym,
                    ext, t_ref, gx_ref, tx_ref, ty_ref, text_ref, gxw, txw,
                    pack_d, pack_u, from_d, from_u, t_low, t_high,
                    own_v, own_p, coarse, tested, load_sem, send_sem, recv_sem, ready):
    comps, rows, _ = ext.shape
    taps, cols = t_ref.shape
    margin = width // 2
    pairs, inner, _ = sub.shape
    innermost = ger.shape[1]
    me_x, me_y = lax.axis_index("gx"), lax.axis_index("gy")
    first, last = me_x == 0, me_x == nx - 1
    not_first, not_last = me_x > 0, me_x < nx - 1
    has_up, has_down = me_y < ny - 1, me_y > 0
    vertical = jnp.where(has_up, 1, 0) + jnp.where(has_down, 1, 0)
    sides = ((1, has_up), (-1, has_down))
    columns = ((0, None), (1, has_up), (-1, has_down))

    def device(dx, dy):
        return {"gx": lax.rem(me_x + dx + nx, nx), "gy": lax.rem(me_y + dy + ny, ny)}

    def signal(sem, dx, dy):
        pl.semaphore_signal(sem, inc=1, device_id=device(dx, dy), device_id_type=MESH)

    def column(condition, act):
        for dy, present in columns:
            pl.when(condition if present is None else condition & present)(lambda dy=dy: act(dy))

    barrier = pltpu.get_barrier_semaphore()
    pl.when(has_up)(lambda: signal(barrier, 0, 1))
    column(not_last, lambda dy: signal(barrier, 1, dy))
    column(first, lambda dy: signal(barrier, -1, dy))

    own = slice(0, cols)
    order = [(i, j) for i in range(comps) for j in range(i, comps)]
    loads = [pltpu.make_async_copy(src, dst, load_sem.at[i]) for i, (src, dst) in enumerate((
        (t_hbm, t_ref), (gx_hbm, gx_ref), (tx_hbm, tx_ref), (ty_hbm, ty_ref),
        (v_hbm, ext.at[:, :, own])))]
    for load in loads:
        load.start()

    per = LANES // width
    groups = rows // width
    head, tail = pl.ds(0, SUB), pl.ds((groups - 1) * SUB, SUB)
    low_x, high_x = v_hbm.at[:, pl.ds(0, width), :], v_hbm.at[:, pl.ds(rows - width, width), :]
    copies = {}

    def remote(key, src, dst, dx, dy):
        n = len(copies)
        copies[key] = pltpu.make_async_remote_copy(
            src_ref=src, dst_ref=dst, send_sem=send_sem.at[n], recv_sem=recv_sem.at[n],
            device_id=device(dx, dy), device_id_type=MESH)

    remote((1, 0), high_x, halo.at[0], 1, 0)
    remote((-1, 0), low_x, halo.at[1], -1, 0)
    remote((1, 1), pack_u.at[:, tail, :], corners.at[0], 1, 1)
    remote((-1, 1), pack_u.at[:, head, :], corners.at[1], -1, 1)
    remote((1, -1), pack_d.at[:, tail, :], corners.at[2], 1, -1)
    remote((-1, -1), pack_d.at[:, head, :], corners.at[3], -1, -1)
    remote(("t", 1), t_ref.at[:, pl.ds(cols - LANES, LANES)], t_low, 0, 1)
    remote(("t", -1), t_ref.at[:, pl.ds(0, LANES)], t_high, 0, -1)
    for c in range(comps):
        remote((c, "v", 1), pack_u.at[c], from_d.at[c], 0, 1)
        remote((c, "v", -1), pack_d.at[c], from_u.at[c], 0, -1)

    @pl.when(last)
    def _():
        pl.semaphore_wait(barrier, jnp.where(has_down, 1, 0) + jnp.where(first, 0, 1 + vertical) + 1 + vertical)
        copies[1, 0].start()

    column(last, lambda dy: signal(ready.at[1 - dy], 1, dy))

    text_ref[...] = jnp.zeros_like(text_ref)
    for z, full in ((z1h, rows), (z1l, rows), (zph, rows), (zpl, rows), (z2h, inner), (z2l, inner)):
        if z.shape[1] > full:
            z[:, full:, :] = jnp.zeros((z.shape[0], z.shape[1] - full, z.shape[2]), BF)
    for sign, present, mid in ((1, has_up, from_u), (-1, has_down, from_d)):
        @pl.when(jnp.logical_not(present))
        def _(sign=sign, mid=mid):
            mid[...] = jnp.zeros_like(mid)
            for side in range(2):
                corners[side + (2 if sign > 0 else 0)] = jnp.zeros(corners.shape[1:], F32)

    for load in loads[:4]:
        load.wait()
    text_ref[0:taps, 0:cols] = t_ref[...]
    first_row, total = me_y * cols, cols * ny
    own_tiles = range(cols // LANES)
    y_weights(t_ref[...], taps, first_row, total, cols, gym, tiles=own_tiles)

    @pl.when(not_last & (not_first | has_down))
    def _():
        pl.semaphore_wait(barrier, jnp.where(has_down, 1, 0) + jnp.where(first, 0, 1 + vertical))

    pl.when(not_first)(lambda: copies[-1, 0].start())
    pl.when(has_down)(lambda: signal(ready.at[3], 0, -1))
    column(not_first, lambda dy: signal(ready.at[5 - dy], -1, dy))

    loads[4].wait()
    for c in range(comps):
        for g in range(groups):
            for q in range(per):
                src = pl.ds(g * width + q * SUB, SUB)
                dst = pl.ds(g * SUB, SUB)
                pack_u[c, dst, q * width:(q + 1) * width] = ext[c, src, cols - width:cols]
                pack_d[c, dst, q * width:(q + 1) * width] = ext[c, src, 0:width]

    def wall(sign):
        copies["t", sign].start()
        for c in range(comps):
            copies[c, "v", sign].start()

    own_v[0] = y_own(ext[0, :, own], cols, gym)
    pl.when(has_down)(lambda: wall(-1))
    for dy, present in sides:
        pl.when(last & present)(lambda dy=dy: copies[1, dy].start())
        pl.when(not_first & present)(lambda dy=dy: copies[-1, dy].start())

    for c in range(1, comps):
        own_v[c] = y_own(ext[c, :, own], cols, gym)

    @pl.when(has_up)
    def _():
        pl.semaphore_wait(ready.at[3], 1)
        wall(1)

    def forward(dx, dy):
        pl.semaphore_wait(ready.at[(5 if dx > 0 else 1) + dy], 1)
        copies[dx, dy].start()

    x_weights(gx_ref, gxw.shape[0], gxw, gxe)
    x_weights(tx_ref, txw.shape[0], txw, txe)
    y_weights(ty_ref[...], taps, first_row, total, cols, tym, tiles=own_tiles)
    for p, (i, j) in enumerate(order):
        own_p[p] = y_own(ext[i, :, own] * ext[j, :, own], cols, gym)
    column(not_last, lambda dy: forward(1, dy))

    for sign, present, tile, at in ((1, has_down, t_low, LANES - margin), (-1, has_up, t_high, 0)):
        @pl.when(present)
        def _(sign=sign, tile=tile, at=at):
            copies["t", sign].wait_recv()
            text_ref[0:taps, cols + at:cols + at + margin] = tile[:, at:at + margin]

    y_weights(text_ref[...], taps, first_row, total, cols, gym, gye, tiles=(cols // LANES,))

    def store(high, low, index, lanes, z):
        high[index, 0:z.shape[0], lanes], low[index, 0:z.shape[0], lanes] = split(z)

    def unpack(c):
        for g in range(groups):
            at = pl.ds(g * SUB, SUB)
            up, down = from_u[c, at, :], from_d[c, at, :]
            for q in range(per):
                ext[c, pl.ds(g * width + q * SUB, SUB), cols:] = side_lanes(up, down, q, width)

    def y_grid(c):
        store(z1h, z1l, c, own, own_v[c] + y_halo(ext[c, :, cols:], margin, cols, gym))
        store(z1h, z1l, c, slice(cols, cols + LANES), y_ends(ext[c], margin, cols, gye))

    def x_grid(c):
        def put(at, value):
            coarse[c, at, :] = value

        x_filter(z1h.at[c], z1l.at[c], inner, gxw, put)

    def y_pair(p):
        i, j = order[p]
        store(zph, zpl, p, own, own_p[p] + y_halo(ext[i, :, cols:] * ext[j, :, cols:], margin, cols, gym))

    def y_test(c):
        store(z2h, z2l, c, own, y_filter(coarse[c], margin, cols, tym))

    def x_test(c):
        def put(at, value):
            tested[c, at, :] = value

        x_filter(z2h.at[c], z2l.at[c], innermost, txw, put)

    def y_resolved(p):
        i, j = order[p]
        store(z2h, z2l, comps + p, own, y_filter(coarse[i] * coarse[j], margin, cols, tym))

    def x_sub(p):
        i, j = order[p]

        def put(at, value):
            sub[p, at, :] = value - coarse[i, at, own] * coarse[j, at, own]

        x_filter(zph.at[p], zpl.at[p], inner, gxw, put)

    def x_ger(p):
        i, j = order[p]

        def put(at, value):
            ger[p, at, :] = value - tested[i, at, :] * tested[j, at, :]

        x_filter(z2h.at[comps + p], z2l.at[comps + p], innermost, txw, put)

    def arrive(c):
        for sign, present in ((1, has_down), (-1, has_up)):
            pl.when(present)(lambda sign=sign: copies[c, "v", sign].wait_recv())

    for c in range(comps):
        arrive(c)
        unpack(c)
        y_grid(c)
        for p, (i, j) in enumerate(order):
            if j == c:
                y_pair(p)
        if c > 0:
            x_grid(c - 1)
    column(first, lambda dy: forward(-1, dy))
    x_grid(comps - 1)
    for c in range(comps):
        y_test(c)
        x_sub(c)
    for c in range(comps):
        y_resolved(c)
        x_test(c)

    for p in range(comps, pairs):
        y_resolved(p)
        x_sub(p)
        x_ger(p - comps)
    for p in range(pairs - comps, pairs):
        x_ger(p)

    copies[1, 0].wait_recv()
    copies[-1, 0].wait_recv()
    for sign, present in ((1, has_down), (-1, has_up)):
        @pl.when(present)
        def _(sign=sign):
            copies[1, sign].wait_recv()
            copies[-1, sign].wait_recv()

    copies[1, 0].wait_send()
    copies[-1, 0].wait_send()
    for sign, present in sides:
        @pl.when(present)
        def _(sign=sign):
            copies[1, sign].wait_send()
            copies[-1, sign].wait_send()
            copies["t", sign].wait_send()
            for c in range(comps):
                copies[c, "v", sign].wait_send()


def edge_kernel(margin, halo, corners, z1h, z1l, zph, zpl, z2h, z2l, sub_in, ger_in,
                gxe, txe, gym, gye, tym, sub_ref, ger_ref, sub_e, ger_e, sems):
    comps, cols = halo.shape[1], halo.shape[3]
    pairs, rows, _ = sub_ref.shape
    width = 2 * margin
    inner, innermost = sub_in.shape[1], ger_in.shape[1]
    order = [(i, j) for i in range(comps) for j in range(i, comps)]
    outs = []

    def leave(source, target):
        copy = pltpu.make_async_copy(source, target, sems.at[len(outs)])
        copy.start()
        outs.append(copy)

    for p in range(pairs):
        leave(sub_in.at[p], sub_ref.at[p, pl.ds(margin, inner), :])
        leave(ger_in.at[p], ger_ref.at[p, pl.ds(width, innermost), :])

    def ends(side, c):
        up, down = corners[2 + side, c], corners[side, c]
        blocks = [side_lanes(up, down, q, width) for q in range(width // SUB)]
        return jnp.concatenate([halo[side, c], jnp.concatenate(blocks, axis=0)], axis=1)

    def pieces(z, size, count):
        high, low = split(z)
        return [(high[n * size:(n + 1) * size], low[n * size:(n + 1) * size]) for n in range(count)]

    def x_ends(side, late, high, low, n, count, size, weights):
        at = slice(0, size) if side == 0 else slice(count - size, count)
        h = (late[0], high[n, at]) if side == 0 else (high[n, at], late[0])
        l = (late[1], low[n, at]) if side == 0 else (low[n, at], late[1])
        r = dot(weights, stacked(h + l))
        half = weights.shape[0] // 2
        return r[0:half] + r[half:]

    both = [(c, side) for c in range(comps) for side in range(2)]
    every = [(p, side) for p in range(pairs) for side in range(2)]
    near = (slice(width - margin, width), slice(0, margin))
    ext = {key: ends(key[1], key[0]) for key in both}
    values = stacked([ext[key] for key in both])
    products = stacked([ext[order[p][0], side][near[side]] * ext[order[p][1], side][near[side]] for p, side in every])
    z = y_filter(stacked([values, products]), margin, cols, gym)
    count = len(both) * width
    late = pieces(jnp.concatenate([z[0:count], y_ends(values, margin, cols, gye)], axis=1), width, len(both))
    coarse = {}
    for (c, side), part in zip(both, late):
        coarse[c, side] = x_ends(side, part, z1h, z1l, c, rows, width, gxe[...])
    late = pieces(z[count:], margin, len(every))
    for (p, side), part in zip(every, late):
        weights = stacked([gxe[0:margin], gxe[width:width + margin]] if side == 0 else
                          [gxe[width - margin:width], gxe[2 * width - margin:]])
        value = x_ends(side, part, zph, zpl, p, rows, width + margin, weights)
        i, j = order[p]
        sub_e[p, side] = value - coarse[i, side][near[side], 0:cols] * coarse[j, side][near[side], 0:cols]
    leave(sub_e.at[:, 0], sub_ref.at[:, pl.ds(0, margin), :])
    leave(sub_e.at[:, 1], sub_ref.at[:, pl.ds(rows - margin, margin), :])
    z = y_filter(stacked([coarse[key] for key in both]
                         + [coarse[order[p][0], side] * coarse[order[p][1], side] for p, side in every]),
                 margin, cols, tym)
    late = pieces(z, width, len(both) + len(every))
    tested = {}
    for (c, side), part in zip(both, late):
        tested[c, side] = x_ends(side, part, z2h, z2l, c, inner, width, txe[...])
    for (p, side), part in zip(every, late[len(both):]):
        value = x_ends(side, part, z2h, z2l, comps + p, inner, width, txe[...])
        i, j = order[p]
        ger_e[p, side] = value - tested[i, side] * tested[j, side]
    leave(ger_e.at[:, 0], ger_ref.at[:, pl.ds(0, width), :])
    leave(ger_e.at[:, 1], ger_ref.at[:, pl.ds(rows - width, width), :])
    for copy in outs:
        copy.wait()


def local(nx, ny, velocity, grid_x, grid_y, test_x, test_y):
    comps, planes, cols, rows = velocity.shape
    taps = grid_x.shape[0]
    margin = (taps - 1) // 2
    width = 2 * margin
    wide = cols + LANES
    step = LANES - width
    pairs = comps * (comps + 1) // 2
    vmem = pl.BlockSpec(memory_space=pltpu.VMEM)
    anywhere = pl.BlockSpec(memory_space=pl.ANY)
    packed = rows // width * SUB
    inner, innermost = rows - width, rows - 2 * width

    def filled(count):
        return round_up(count, step) + width

    fields = comps + pairs
    subs, gers = [], []
    shape = jax.ShapeDtypeStruct
    for plane in range(planes):
        v = jnp.swapaxes(velocity[:, plane], 1, 2)
        parts = pl.pallas_call(
            functools.partial(interior_kernel, nx, ny, width),
            out_shape=(
                shape((2, comps, width, cols), F32),
                shape((4, comps, SUB, LANES), F32),
                shape((comps, max(rows, filled(inner)), wide), BF),
                shape((comps, max(rows, filled(inner)), wide), BF),
                shape((pairs, max(rows, filled(inner)), cols), BF),
                shape((pairs, max(rows, filled(inner)), cols), BF),
                shape((fields, max(inner, filled(innermost)), cols), BF),
                shape((fields, max(inner, filled(innermost)), cols), BF),
                shape((pairs, inner, cols), F32),
                shape((pairs, innermost, cols), F32),
                shape((2 * width, LANES), BF),
                shape((2 * width, LANES), BF),
                shape((3 * cols + LANES, cols), BF),
                shape((3 * LANES, LANES), BF),
                shape((3 * cols + LANES, cols), BF),
            ),
            in_specs=[pl.BlockSpec(memory_space=pltpu.HBM)] * 5,
            out_specs=(vmem,) * 15,
            scratch_shapes=[
                pltpu.VMEM((comps, rows, wide), F32),
                pltpu.VMEM((taps, cols), F32),
                pltpu.VMEM((1, taps), F32),
                pltpu.VMEM((1, taps), F32),
                pltpu.VMEM((taps, cols), F32),
                pltpu.VMEM((round_up(taps, SUB), wide), F32),
                pltpu.VMEM((step, 3 * LANES), BF),
                pltpu.VMEM((step, 3 * LANES), BF),
                pltpu.VMEM((comps, packed, LANES), F32),
                pltpu.VMEM((comps, packed, LANES), F32),
                pltpu.VMEM((comps, packed, LANES), F32),
                pltpu.VMEM((comps, packed, LANES), F32),
                pltpu.VMEM((taps, LANES), F32),
                pltpu.VMEM((taps, LANES), F32),
                pltpu.VMEM((comps, rows, cols), F32),
                pltpu.VMEM((pairs, rows, cols), F32),
                pltpu.VMEM((comps, inner, wide), F32),
                pltpu.VMEM((comps, innermost, cols), F32),
                pltpu.SemaphoreType.DMA((5,)),
                pltpu.SemaphoreType.DMA((8 + 2 * comps,)),
                pltpu.SemaphoreType.DMA((8 + 2 * comps,)),
                pltpu.SemaphoreType.REGULAR((7,)),
            ],
            compiler_params=pltpu.CompilerParams(
                collective_id=plane, has_side_effects=True, vmem_limit_bytes=20 << 20),
            name="interior",
        )(*[pltpu.with_memory_space_constraint(x, pltpu.HBM) for x in (
            v, grid_y.T, grid_x.reshape(1, taps), test_x.reshape(1, taps), test_y.T)])
        out = shape((pairs, rows, cols), F32)
        sub, ger = pl.pallas_call(
            functools.partial(edge_kernel, margin),
            out_shape=(out, out),
            in_specs=[vmem] * 15,
            out_specs=(anywhere, anywhere),
            scratch_shapes=[
                pltpu.VMEM((pairs, 2, margin, cols), F32),
                pltpu.VMEM((pairs, 2, width, cols), F32),
                pltpu.SemaphoreType.DMA((2 * pairs + 4,)),
            ],
            compiler_params=pltpu.CompilerParams(vmem_limit_bytes=8 << 20),
            name="edge",
        )(*parts)
        subs.append(jnp.swapaxes(sub, 1, 2))
        gers.append(jnp.swapaxes(ger, 1, 2))
    return jnp.stack(subs, axis=1), jnp.stack(gers, axis=1)


def solution(mesh):
    nx, ny = mesh.shape["gx"], mesh.shape["gy"]
    field = P(None, None, "gy", "gx")
    return jax.shard_map(
        functools.partial(local, nx, ny),
        mesh=mesh,
        in_specs=(field, P(), P("gy", None), P(), P("gy", None)),
        out_specs=(field, field),
        check_vma=False,
    )
```

```python
import functools

import jax
import jax.numpy as jnp
from jax import lax
from jax.experimental import pallas as pl
from jax.experimental.pallas import tpu as pltpu
from jax.sharding import PartitionSpec as P

MESH = pl.DeviceIdType.MESH
LANES = 128
SUB = 8
BF = jnp.bfloat16
F32 = jnp.float32


def round_up(value, unit):
    return (value + unit - 1) // unit * unit


def split(value):
    high = value.astype(BF)
    return high, (value - high.astype(F32)).astype(BF)


def dot(a, b):
    return jnp.dot(a, b, preferred_element_type=F32)


def x_weights(w_ref, step, out, edge):
    taps = w_ref.shape[1]
    w = jnp.concatenate([w_ref[...], jnp.zeros((1, LANES - taps), F32)], axis=1)
    w = w / jnp.sum(w)
    band = pltpu.roll(jnp.broadcast_to(w, (LANES, LANES)), 0, 1, stride=1, stride_axis=0)
    high, low = split(band[0:step])
    out[:, 0:LANES] = high
    out[:, LANES:2 * LANES] = high
    out[:, 2 * LANES:] = low
    width = edge.shape[0] // 2
    high, low = split(band[0:width])
    high = high.astype(F32)
    edge[0:width] = (high + pltpu.roll(high, 2 * width, 1)).astype(BF)
    edge[width:] = low


def spread(value, margin):
    lane = lax.broadcasted_iota(jnp.int32, value.shape, 1)
    near = jnp.where((lane < margin) | (lane >= LANES - margin), value, 0.0)
    return pltpu.roll(jnp.where(lane < LANES // 2, near, 0.0), margin, 1) + pltpu.roll(
        jnp.where(lane < LANES // 2, 0.0, near), LANES - margin, 1)


def y_weights(table, taps, first_row, total, cols, main, edge=None, tiles=None):
    margin = (taps - 1) // 2
    width = 2 * margin
    lanes = table.shape[1]
    wide = cols + LANES
    k = lax.broadcasted_iota(jnp.int32, (LANES, lanes), 0)
    lane = lax.broadcasted_iota(jnp.int32, (LANES, lanes), 1)
    y = first_row + jnp.where(lane < cols + LANES // 2, lane, lane - wide)
    source = y + k - margin
    keep = (k < taps) & (source >= 0) & (source < total) & (y >= 0) & (y < total)
    w = jnp.where(keep, jnp.concatenate(
        [table, jnp.zeros((LANES - table.shape[0], lanes), F32)], axis=0), 0.0)
    s = jnp.sum(w, axis=0, keepdims=True)
    w = (w / jnp.where(s > 0.0, s, 1.0)).T
    zeros = jnp.zeros((LANES, cols), F32)
    for t in (range(lanes // LANES) if tiles is None else tiles):
        at = slice(t * LANES, (t + 1) * LANES)
        tile = jnp.concatenate([w[at], zeros], axis=1)
        band = pltpu.roll(tile, (t * LANES - margin) % wide, 1, stride=1, stride_axis=0)
        if t * LANES < cols:
            own, halo = band[:, 0:cols].T, band[:, cols:]
            own_high, own_low = split(own)
            main[0:cols, at] = own_high
            main[cols:2 * cols, at] = own_low
            main[2 * cols:3 * cols, at] = own_high
            halo = spread(halo, margin)
            high = halo.astype(BF).astype(F32)
            packed = high + pltpu.roll(high, width, 1) + pltpu.roll(halo - high, 2 * width, 1)
            main[3 * cols:, at] = packed.T.astype(BF)
        else:
            low_own, high_own, halo = band[:, 0:LANES].T, band[:, cols - LANES:cols].T, band[:, cols:].T
            near = jnp.concatenate([
                low_own[0:margin], halo[0:width], jnp.zeros((LANES - 2 * margin - 2 * width, LANES), F32),
                halo[LANES - width:], high_own[LANES - margin:]], axis=0)
            near = spread(near, margin)
            near = near + pltpu.roll(near, width, 1) + pltpu.roll(near, 2 * width, 1)
            high, low = split(near)
            edge[0:LANES] = high
            edge[LANES:2 * LANES] = high
            edge[2 * LANES:] = low


def y_own(value, cols, main):
    high, low = split(value)
    return dot(jnp.concatenate([high, high, low], axis=1), main[0:3 * cols])


def second(shape, width):
    lane = lax.broadcasted_iota(jnp.int32, shape, 1)
    return (lane < width // 2) | ((lane >= width + width // 2) & (lane < 2 * width))


def thrice(halo, width):
    lane = lax.broadcasted_iota(jnp.int32, halo.shape, 1)
    margin = width // 2
    home = ((lane >= margin) & (lane < width)) | ((lane >= LANES - width) & (lane < LANES - margin))
    return jnp.where(home, halo, jnp.where(
        second(halo.shape, width), pltpu.roll(halo, width, 1), pltpu.roll(halo, 2 * width, 1)))


def packed_halo(halo, margin):
    high = halo.astype(BF).astype(F32)
    return jnp.where(second(halo.shape, 2 * margin), halo - high, high).astype(BF)


def y_halo(halo, margin, cols, main):
    return dot(packed_halo(halo, margin), main[3 * cols:])


def y_filter(value, margin, cols, main):
    high, low = split(value[:, 0:cols])
    return dot(jnp.concatenate([high, high, low, packed_halo(value[:, cols:], margin)], axis=1), main[...])


def y_ends(own, halo, margin, edge):
    lane = lax.broadcasted_iota(jnp.int32, halo.shape, 1)
    ends = jnp.where(lane < margin, own[:, 0:LANES],
                     jnp.where(lane >= LANES - margin, own[:, own.shape[1] - LANES:], halo))
    high, low = split(ends)
    return dot(jnp.concatenate([high, low, high], axis=1), edge[...])


def side_lanes(up, down, q, width):
    lane = lax.broadcasted_iota(jnp.int32, up.shape, 1)
    margin = width // 2
    return jnp.where(lane < LANES // 2, pltpu.roll(up, (LANES + margin - q * width) % LANES, 1),
                     pltpu.roll(down, (2 * LANES - margin - (q + 1) * width) % LANES, 1))


def x_filter(zh, zl, count, weights, put):
    step = weights.shape[0]
    for s in range(0, count, step):
        size = min(step, count - s)
        at = slice(s, s + LANES)
        high = zh[at]
        put(slice(s, s + size), dot(weights[0:size], jnp.concatenate([high, zl[at], high], axis=0)))


def stacked(values):
    return jnp.concatenate(values, axis=0)


def interior_kernel(nx, ny, width, v_hbm, t_hbm, gx_hbm, tx_hbm, ty_hbm,
                    halo, corners, z1h, z1l, zph, zpl, z2h, z2l, sub, ger, gxe, txe, gym, gye, tym,
                    ext, t_ref, gx_ref, tx_ref, ty_ref, text_ref, gxw, txw,
                    pack_d, pack_u, from_d, from_u, t_low, t_high,
                    own_v, own_p, coarse, tested, load_sem, send_sem, recv_sem, ready):
    comps, rows, _ = ext.shape
    taps, cols = t_ref.shape
    margin = width // 2
    pairs, inner, _ = sub.shape
    innermost = ger.shape[1]
    me_x, me_y = lax.axis_index("gx"), lax.axis_index("gy")
    first, last = me_x == 0, me_x == nx - 1
    not_first, not_last = me_x > 0, me_x < nx - 1
    has_up, has_down = me_y < ny - 1, me_y > 0
    vertical = jnp.where(has_up, 1, 0) + jnp.where(has_down, 1, 0)
    sides = ((1, has_up), (-1, has_down))
    columns = ((0, None), (1, has_up), (-1, has_down))

    def device(dx, dy):
        return {"gx": lax.rem(me_x + dx + nx, nx), "gy": lax.rem(me_y + dy + ny, ny)}

    def signal(sem, dx, dy):
        pl.semaphore_signal(sem, inc=1, device_id=device(dx, dy), device_id_type=MESH)

    def column(condition, act):
        for dy, present in columns:
            pl.when(condition if present is None else condition & present)(lambda dy=dy: act(dy))

    barrier = pltpu.get_barrier_semaphore()
    pl.when(has_up)(lambda: signal(barrier, 0, 1))
    column(not_last, lambda dy: signal(barrier, 1, dy))
    column(first, lambda dy: signal(barrier, -1, dy))

    own = slice(0, cols)
    order = [(i, j) for i in range(comps) for j in range(i, comps)]
    loads = [pltpu.make_async_copy(src, dst, load_sem.at[i]) for i, (src, dst) in enumerate((
        (t_hbm, t_ref), (gx_hbm, gx_ref), (tx_hbm, tx_ref), (ty_hbm, ty_ref),
        (v_hbm, ext.at[:, :, own])))]
    for load in loads:
        load.start()

    per = LANES // width
    groups = rows // width
    head, tail = pl.ds(0, SUB), pl.ds((groups - 1) * SUB, SUB)
    low_x, high_x = v_hbm.at[:, pl.ds(0, width), :], v_hbm.at[:, pl.ds(rows - width, width), :]
    copies = {}

    def remote(key, src, dst, dx, dy):
        n = len(copies)
        copies[key] = pltpu.make_async_remote_copy(
            src_ref=src, dst_ref=dst, send_sem=send_sem.at[n], recv_sem=recv_sem.at[n],
            device_id=device(dx, dy), device_id_type=MESH)

    remote((1, 0), high_x, halo.at[0], 1, 0)
    remote((-1, 0), low_x, halo.at[1], -1, 0)
    remote((1, 1), pack_u.at[:, tail, :], corners.at[0], 1, 1)
    remote((-1, 1), pack_u.at[:, head, :], corners.at[1], -1, 1)
    remote((1, -1), pack_d.at[:, tail, :], corners.at[2], 1, -1)
    remote((-1, -1), pack_d.at[:, head, :], corners.at[3], -1, -1)
    remote(("t", 1), t_ref.at[:, pl.ds(cols - LANES, LANES)], t_low, 0, 1)
    remote(("t", -1), t_ref.at[:, pl.ds(0, LANES)], t_high, 0, -1)
    for c in range(comps):
        remote((c, "v", 1), pack_u.at[c], from_d.at[c], 0, 1)
        remote((c, "v", -1), pack_d.at[c], from_u.at[c], 0, -1)

    @pl.when(last)
    def _():
        pl.semaphore_wait(barrier, jnp.where(has_down, 1, 0) + jnp.where(first, 0, 1 + vertical) + 1 + vertical)
        copies[1, 0].start()

    column(last, lambda dy: signal(ready.at[1 - dy], 1, dy))

    text_ref[...] = jnp.zeros_like(text_ref)
    for z, full in ((z1h, rows), (z1l, rows), (zph, rows), (zpl, rows), (z2h, inner), (z2l, inner)):
        if z.shape[1] > full:
            z[:, full:, :] = jnp.zeros((z.shape[0], z.shape[1] - full, z.shape[2]), BF)
    for sign, present, mid in ((1, has_up, from_u), (-1, has_down, from_d)):
        @pl.when(jnp.logical_not(present))
        def _(sign=sign, mid=mid):
            mid[...] = jnp.zeros_like(mid)
            for side in range(2):
                corners[side + (2 if sign > 0 else 0)] = jnp.zeros(corners.shape[1:], F32)

    for load in loads[:4]:
        load.wait()
    text_ref[0:taps, 0:cols] = t_ref[...]
    first_row, total = me_y * cols, cols * ny
    own_tiles = range(cols // LANES)
    y_weights(t_ref[...], taps, first_row, total, cols, gym, tiles=own_tiles)

    @pl.when(not_last & (not_first | has_down))
    def _():
        pl.semaphore_wait(barrier, jnp.where(has_down, 1, 0) + jnp.where(first, 0, 1 + vertical))

    pl.when(not_first)(lambda: copies[-1, 0].start())
    pl.when(has_down)(lambda: signal(ready.at[3], 0, -1))
    column(not_first, lambda dy: signal(ready.at[5 - dy], -1, dy))

    loads[4].wait()
    for c in range(comps):
        for g in range(groups):
            for q in range(per):
                src = pl.ds(g * width + q * SUB, SUB)
                dst = pl.ds(g * SUB, SUB)
                pack_u[c, dst, q * width:(q + 1) * width] = ext[c, src, cols - width:cols]
                pack_d[c, dst, q * width:(q + 1) * width] = ext[c, src, 0:width]

    def wall(sign):
        copies["t", sign].start()
        for c in range(comps):
            copies[c, "v", sign].start()

    own_v[0] = y_own(ext[0, :, own], cols, gym)
    pl.when(has_down)(lambda: wall(-1))
    for dy, present in sides:
        pl.when(last & present)(lambda dy=dy: copies[1, dy].start())
        pl.when(not_first & present)(lambda dy=dy: copies[-1, dy].start())

    def own_pair(p):
        i, j = order[p]
        own_p[p] = y_own(ext[i, :, own] * ext[j, :, own], cols, gym)

    for c in range(1, comps):
        own_v[c] = y_own(ext[c, :, own], cols, gym)
    early = pairs // 2
    for p in range(early):
        own_pair(p)

    @pl.when(has_up)
    def _():
        pl.semaphore_wait(ready.at[3], 1)
        wall(1)

    def forward(dx, dy):
        pl.semaphore_wait(ready.at[(5 if dx > 0 else 1) + dy], 1)
        copies[dx, dy].start()

    pl.when(not_last)(lambda: forward(1, 0))
    x_weights(gx_ref, gxw.shape[0], gxw, gxe)
    x_weights(tx_ref, txw.shape[0], txw, txe)
    y_weights(ty_ref[...], taps, first_row, total, cols, tym, tiles=own_tiles)
    for p in range(early, pairs):
        own_pair(p)
    for dy, present in sides:
        pl.when(not_last & present)(lambda dy=dy: forward(1, dy))

    for sign, present, tile, at in ((1, has_down, t_low, LANES - margin), (-1, has_up, t_high, 0)):
        @pl.when(present)
        def _(sign=sign, tile=tile, at=at):
            copies["t", sign].wait_recv()
            text_ref[0:taps, cols + at:cols + at + margin] = tile[:, at:at + margin]

    y_weights(text_ref[...], taps, first_row, total, cols, gym, gye, tiles=(cols // LANES,))

    def store(high, low, index, lanes, z):
        high[index, 0:z.shape[0], lanes], low[index, 0:z.shape[0], lanes] = split(z)

    def y_grid(c):
        blocks = []
        for g in range(groups):
            at = pl.ds(g * SUB, SUB)
            up, down = from_u[c, at, :], from_d[c, at, :]
            blocks += [side_lanes(up, down, q, width) for q in range(per)]
        halo = stacked(blocks)
        spread_halo = thrice(halo, width)
        ext[c, :, cols:] = spread_halo
        store(z1h, z1l, c, own, own_v[c] + y_halo(spread_halo, margin, cols, gym))
        store(z1h, z1l, c, slice(cols, cols + LANES), y_ends(ext[c, :, own], halo, margin, gye))

    def x_grid(c):
        def put(at, value):
            coarse[c, at, :] = value

        x_filter(z1h.at[c], z1l.at[c], inner, gxw, put)

    def y_pair(p):
        i, j = order[p]
        store(zph, zpl, p, own, own_p[p] + y_halo(ext[i, :, cols:] * ext[j, :, cols:], margin, cols, gym))

    def y_test(c):
        store(z2h, z2l, c, own, y_filter(coarse[c], margin, cols, tym))

    def x_test(c):
        def put(at, value):
            tested[c, at, :] = value

        x_filter(z2h.at[c], z2l.at[c], innermost, txw, put)

    def y_resolved(p):
        i, j = order[p]
        store(z2h, z2l, comps + p, own, y_filter(coarse[i] * coarse[j], margin, cols, tym))

    def x_sub(p):
        i, j = order[p]

        def put(at, value):
            sub[p, at, :] = value - coarse[i, at, own] * coarse[j, at, own]

        x_filter(zph.at[p], zpl.at[p], inner, gxw, put)

    def x_ger(p):
        i, j = order[p]

        def put(at, value):
            ger[p, at, :] = value - tested[i, at, :] * tested[j, at, :]

        x_filter(z2h.at[comps + p], z2l.at[comps + p], innermost, txw, put)

    def arrive(c):
        for sign, present in ((1, has_down), (-1, has_up)):
            pl.when(present)(lambda sign=sign: copies[c, "v", sign].wait_recv())

    for c in range(comps):
        arrive(c)
        y_grid(c)
        for p, (i, j) in enumerate(order):
            if j == c:
                y_pair(p)
        if c > 0:
            x_grid(c - 1)
    column(first, lambda dy: forward(-1, dy))
    x_grid(comps - 1)
    for c in range(comps):
        y_test(c)
        x_sub(c)
    for c in range(comps):
        y_resolved(c)
        x_test(c)

    for p in range(comps, pairs):
        y_resolved(p)
        x_sub(p)
        x_ger(p - comps)
    for p in range(pairs - comps, pairs):
        x_ger(p)

    copies[1, 0].wait_recv()
    copies[-1, 0].wait_recv()
    for sign, present in ((1, has_down), (-1, has_up)):
        @pl.when(present)
        def _(sign=sign):
            copies[1, sign].wait_recv()
            copies[-1, sign].wait_recv()

    copies[1, 0].wait_send()
    copies[-1, 0].wait_send()
    for sign, present in sides:
        @pl.when(present)
        def _(sign=sign):
            copies[1, sign].wait_send()
            copies[-1, sign].wait_send()
            copies["t", sign].wait_send()
            for c in range(comps):
                copies[c, "v", sign].wait_send()


def edge_kernel(margin, halo, corners, z1h, z1l, zph, zpl, z2h, z2l, sub_in, ger_in,
                gxe, txe, gym, gye, tym, sub_ref, ger_ref, sub_e, ger_e, sems):
    comps, cols = halo.shape[1], halo.shape[3]
    pairs, rows, _ = sub_ref.shape
    width = 2 * margin
    inner, innermost = sub_in.shape[1], ger_in.shape[1]
    order = [(i, j) for i in range(comps) for j in range(i, comps)]
    outs = []

    def leave(source, target):
        copy = pltpu.make_async_copy(source, target, sems.at[len(outs)])
        copy.start()
        outs.append(copy)

    for p in range(pairs):
        leave(sub_in.at[p], sub_ref.at[p, pl.ds(margin, inner), :])
        leave(ger_in.at[p], ger_ref.at[p, pl.ds(width, innermost), :])

    def ends(side, c):
        up, down = corners[2 + side, c], corners[side, c]
        return halo[side, c], stacked([side_lanes(up, down, q, width) for q in range(width // SUB)])

    def pieces(z, size, count):
        high, low = split(z)
        return [(high[n * size:(n + 1) * size], low[n * size:(n + 1) * size]) for n in range(count)]

    def x_ends(side, late, high, low, n, count, size, weights):
        at = slice(0, size) if side == 0 else slice(count - size, count)
        h = (late[0], high[n, at]) if side == 0 else (high[n, at], late[0])
        l = (late[1], low[n, at]) if side == 0 else (low[n, at], late[1])
        r = dot(weights, stacked(h + l))
        half = weights.shape[0] // 2
        return r[0:half] + r[half:]

    near = (slice(width - margin, width), slice(0, margin))
    everywhere = range(pairs)

    def grid(side):
        parts = [ends(side, c) for c in range(comps)]
        rows_own, rows_halo = stacked([part[0] for part in parts]), stacked([part[1] for part in parts])
        values = jnp.concatenate([rows_own, thrice(rows_halo, width)], axis=1)
        ext = [values[c * width:(c + 1) * width] for c in range(comps)]
        products = stacked([ext[i][near[side]] * ext[j][near[side]] for i, j in order])
        z = y_filter(stacked([values, products]), margin, cols, gym)
        count = comps * width
        late = pieces(jnp.concatenate([z[0:count], y_ends(rows_own, rows_halo, margin, gye)], axis=1), width, comps)
        return late, pieces(z[count:], margin, pairs)

    def coarsen(side, late):
        return [x_ends(side, part, z1h, z1l, c, rows, width, gxe[...]) for c, part in enumerate(late)]

    def stress(side, coarse, late):
        weights = stacked([gxe[0:margin], gxe[width:width + margin]] if side == 0 else
                          [gxe[width - margin:width], gxe[2 * width - margin:]])
        for p, part in enumerate(late):
            value = x_ends(side, part, zph, zpl, p, rows, width + margin, weights)
            i, j = order[p]
            sub_e[p, side] = value - coarse[i][near[side], 0:cols] * coarse[j][near[side], 0:cols]

    def test(side, coarse):
        z = y_filter(stacked(coarse + [coarse[i] * coarse[j] for i, j in order]), margin, cols, tym)
        return pieces(z, width, comps + pairs)

    def resolve(side, late):
        tested = [x_ends(side, part, z2h, z2l, c, inner, width, txe[...]) for c, part in enumerate(late[0:comps])]
        for p, part in enumerate(late[comps:]):
            i, j = order[p]
            ger_e[p, side] = (x_ends(side, part, z2h, z2l, comps + p, inner, width, txe[...])
                              - tested[i] * tested[j])

    late = [grid(side) for side in range(2)]
    coarse = [coarsen(side, late[side][0]) for side in range(2)]
    tests = []
    for side in range(2):
        tests.append(test(side, coarse[side]))
        stress(side, coarse[side], late[side][1])
    leave(sub_e.at[:, 0], sub_ref.at[:, pl.ds(0, margin), :])
    leave(sub_e.at[:, 1], sub_ref.at[:, pl.ds(rows - margin, margin), :])
    resolve(0, tests[0])
    leave(ger_e.at[:, 0], ger_ref.at[:, pl.ds(0, width), :])
    resolve(1, tests[1])
    leave(ger_e.at[:, 1], ger_ref.at[:, pl.ds(rows - width, width), :])
    for copy in outs:
        copy.wait()


def local(nx, ny, velocity, grid_x, grid_y, test_x, test_y):
    comps, planes, cols, rows = velocity.shape
    taps = grid_x.shape[0]
    margin = (taps - 1) // 2
    width = 2 * margin
    wide = cols + LANES
    step = LANES - width
    pairs = comps * (comps + 1) // 2
    vmem = pl.BlockSpec(memory_space=pltpu.VMEM)
    anywhere = pl.BlockSpec(memory_space=pl.ANY)
    packed = rows // width * SUB
    inner, innermost = rows - width, rows - 2 * width

    def filled(count):
        return round_up(count, step) + width

    fields = comps + pairs
    subs, gers = [], []
    shape = jax.ShapeDtypeStruct
    for plane in range(planes):
        v = jnp.swapaxes(velocity[:, plane], 1, 2)
        parts = pl.pallas_call(
            functools.partial(interior_kernel, nx, ny, width),
            out_shape=(
                shape((2, comps, width, cols), F32),
                shape((4, comps, SUB, LANES), F32),
                shape((comps, max(rows, filled(inner)), wide), BF),
                shape((comps, max(rows, filled(inner)), wide), BF),
                shape((pairs, max(rows, filled(inner)), cols), BF),
                shape((pairs, max(rows, filled(inner)), cols), BF),
                shape((fields, max(inner, filled(innermost)), cols), BF),
                shape((fields, max(inner, filled(innermost)), cols), BF),
                shape((pairs, inner, cols), F32),
                shape((pairs, innermost, cols), F32),
                shape((2 * width, LANES), BF),
                shape((2 * width, LANES), BF),
                shape((3 * cols + LANES, cols), BF),
                shape((3 * LANES, LANES), BF),
                shape((3 * cols + LANES, cols), BF),
            ),
            in_specs=[pl.BlockSpec(memory_space=pltpu.HBM)] * 5,
            out_specs=(vmem,) * 15,
            scratch_shapes=[
                pltpu.VMEM((comps, rows, wide), F32),
                pltpu.VMEM((taps, cols), F32),
                pltpu.VMEM((1, taps), F32),
                pltpu.VMEM((1, taps), F32),
                pltpu.VMEM((taps, cols), F32),
                pltpu.VMEM((round_up(taps, SUB), wide), F32),
                pltpu.VMEM((step, 3 * LANES), BF),
                pltpu.VMEM((step, 3 * LANES), BF),
                pltpu.VMEM((comps, packed, LANES), F32),
                pltpu.VMEM((comps, packed, LANES), F32),
                pltpu.VMEM((comps, packed, LANES), F32),
                pltpu.VMEM((comps, packed, LANES), F32),
                pltpu.VMEM((taps, LANES), F32),
                pltpu.VMEM((taps, LANES), F32),
                pltpu.VMEM((comps, rows, cols), F32),
                pltpu.VMEM((pairs, rows, cols), F32),
                pltpu.VMEM((comps, inner, wide), F32),
                pltpu.VMEM((comps, innermost, cols), F32),
                pltpu.SemaphoreType.DMA((5,)),
                pltpu.SemaphoreType.DMA((8 + 2 * comps,)),
                pltpu.SemaphoreType.DMA((8 + 2 * comps,)),
                pltpu.SemaphoreType.REGULAR((7,)),
            ],
            compiler_params=pltpu.CompilerParams(
                collective_id=plane, has_side_effects=True, vmem_limit_bytes=20 << 20),
            name="interior",
        )(*[pltpu.with_memory_space_constraint(x, pltpu.HBM) for x in (
            v, grid_y.T, grid_x.reshape(1, taps), test_x.reshape(1, taps), test_y.T)])
        out = shape((pairs, rows, cols), F32)
        sub, ger = pl.pallas_call(
            functools.partial(edge_kernel, margin),
            out_shape=(out, out),
            in_specs=[vmem] * 15,
            out_specs=(anywhere, anywhere),
            scratch_shapes=[
                pltpu.VMEM((pairs, 2, margin, cols), F32),
                pltpu.VMEM((pairs, 2, width, cols), F32),
                pltpu.SemaphoreType.DMA((2 * pairs + 4,)),
            ],
            compiler_params=pltpu.CompilerParams(vmem_limit_bytes=8 << 20),
            name="edge",
        )(*parts)
        subs.append(jnp.swapaxes(sub, 1, 2))
        gers.append(jnp.swapaxes(ger, 1, 2))
    return jnp.stack(subs, axis=1), jnp.stack(gers, axis=1)


def solution(mesh):
    nx, ny = mesh.shape["gx"], mesh.shape["gy"]
    field = P(None, None, "gy", "gx")
    return jax.shard_map(
        functools.partial(local, nx, ny),
        mesh=mesh,
        in_specs=(field, P(), P("gy", None), P(), P("gy", None)),
        out_specs=(field, field),
        check_vma=False,
    )
```

```python
import functools

import jax
import jax.numpy as jnp
from jax import lax
from jax.experimental import pallas as pl
from jax.experimental.pallas import tpu as pltpu
from jax.sharding import PartitionSpec as P

MESH = pl.DeviceIdType.MESH
LANES = 128
SUB = 8
BF = jnp.bfloat16
F32 = jnp.float32


def round_up(value, unit):
    return (value + unit - 1) // unit * unit


def split(value):
    high = value.astype(BF)
    return high, (value - high.astype(F32)).astype(BF)


def dot(a, b):
    return jnp.dot(a, b, preferred_element_type=F32)


def x_weights(w_ref, step, out, edge):
    taps = w_ref.shape[1]
    w = jnp.concatenate([w_ref[...], jnp.zeros((1, LANES - taps), F32)], axis=1)
    w = w / jnp.sum(w)
    band = pltpu.roll(jnp.broadcast_to(w, (LANES, LANES)), 0, 1, stride=1, stride_axis=0)
    high, low = split(band[0:step])
    out[:, 0:LANES] = high
    out[:, LANES:2 * LANES] = high
    out[:, 2 * LANES:] = low
    width = edge.shape[0] // 2
    high, low = split(band[0:width])
    high = high.astype(F32)
    edge[0:width] = (high + pltpu.roll(high, 2 * width, 1)).astype(BF)
    edge[width:] = low


def spread(value, margin):
    lane = lax.broadcasted_iota(jnp.int32, value.shape, 1)
    near = jnp.where((lane < margin) | (lane >= LANES - margin), value, 0.0)
    return pltpu.roll(jnp.where(lane < LANES // 2, near, 0.0), margin, 1) + pltpu.roll(
        jnp.where(lane < LANES // 2, 0.0, near), LANES - margin, 1)


def y_weights(table, taps, first_row, total, cols, main, edge=None, tiles=None):
    margin = (taps - 1) // 2
    width = 2 * margin
    lanes = table.shape[1]
    wide = cols + LANES
    k = lax.broadcasted_iota(jnp.int32, (LANES, lanes), 0)
    lane = lax.broadcasted_iota(jnp.int32, (LANES, lanes), 1)
    y = first_row + jnp.where(lane < cols + LANES // 2, lane, lane - wide)
    source = y + k - margin
    keep = (k < taps) & (source >= 0) & (source < total) & (y >= 0) & (y < total)
    w = jnp.where(keep, jnp.concatenate(
        [table, jnp.zeros((LANES - table.shape[0], lanes), F32)], axis=0), 0.0)
    s = jnp.sum(w, axis=0, keepdims=True)
    w = (w / jnp.where(s > 0.0, s, 1.0)).T
    zeros = jnp.zeros((LANES, cols), F32)
    for t in (range(lanes // LANES) if tiles is None else tiles):
        at = slice(t * LANES, (t + 1) * LANES)
        tile = jnp.concatenate([w[at], zeros], axis=1)
        band = pltpu.roll(tile, (t * LANES - margin) % wide, 1, stride=1, stride_axis=0)
        if t * LANES < cols:
            own, halo = band[:, 0:cols].T, band[:, cols:]
            own_high, own_low = split(own)
            main[0:cols, at] = own_high
            main[cols:2 * cols, at] = own_low
            main[2 * cols:3 * cols, at] = own_high
            halo = spread(halo, margin)
            high = halo.astype(BF).astype(F32)
            packed = high + pltpu.roll(high, width, 1) + pltpu.roll(halo - high, 2 * width, 1)
            main[3 * cols:, at] = packed.T.astype(BF)
        else:
            low_own, high_own, halo = band[:, 0:LANES].T, band[:, cols - LANES:cols].T, band[:, cols:].T
            near = jnp.concatenate([
                low_own[0:margin], halo[0:width], jnp.zeros((LANES - 2 * margin - 2 * width, LANES), F32),
                halo[LANES - width:], high_own[LANES - margin:]], axis=0)
            near = spread(near, margin)
            near = near + pltpu.roll(near, width, 1) + pltpu.roll(near, 2 * width, 1)
            high, low = split(near)
            edge[0:LANES] = high
            edge[LANES:2 * LANES] = high
            edge[2 * LANES:] = low


def y_own(value, cols, main):
    high, low = split(value)
    return dot(jnp.concatenate([high, high, low], axis=1), main[0:3 * cols])


def second(shape, width):
    lane = lax.broadcasted_iota(jnp.int32, shape, 1)
    return (lane < width // 2) | ((lane >= width + width // 2) & (lane < 2 * width))


def thrice(halo, width):
    lane = lax.broadcasted_iota(jnp.int32, halo.shape, 1)
    margin = width // 2
    home = ((lane >= margin) & (lane < width)) | ((lane >= LANES - width) & (lane < LANES - margin))
    return jnp.where(home, halo, jnp.where(
        second(halo.shape, width), pltpu.roll(halo, width, 1), pltpu.roll(halo, 2 * width, 1)))


def packed_halo(halo, margin):
    high = halo.astype(BF).astype(F32)
    return jnp.where(second(halo.shape, 2 * margin), halo - high, high).astype(BF)


def y_halo(halo, margin, cols, main):
    return dot(packed_halo(halo, margin), main[3 * cols:])


def y_filter(value, margin, cols, main):
    high, low = split(value[:, 0:cols])
    return dot(jnp.concatenate([high, high, low, packed_halo(value[:, cols:], margin)], axis=1), main[...])


def y_ends(own, halo, margin, edge):
    lane = lax.broadcasted_iota(jnp.int32, halo.shape, 1)
    ends = jnp.where(lane < margin, own[:, 0:LANES],
                     jnp.where(lane >= LANES - margin, own[:, own.shape[1] - LANES:], halo))
    high, low = split(ends)
    return dot(jnp.concatenate([high, low, high], axis=1), edge[...])


def side_lanes(up, down, q, width):
    lane = lax.broadcasted_iota(jnp.int32, up.shape, 1)
    margin = width // 2
    return jnp.where(lane < LANES // 2, pltpu.roll(up, (LANES + margin - q * width) % LANES, 1),
                     pltpu.roll(down, (2 * LANES - margin - (q + 1) * width) % LANES, 1))


def x_filter(zh, zl, count, weights, put):
    step = weights.shape[0]
    for s in range(0, count, step):
        size = min(step, count - s)
        at = slice(s, s + LANES)
        high = zh[at]
        put(slice(s, s + size), dot(weights[0:size], jnp.concatenate([high, zl[at], high], axis=0)))


def stacked(values):
    return jnp.concatenate(values, axis=0)


def interior_kernel(nx, ny, width, v_hbm, t_hbm, gx_hbm, tx_hbm, ty_hbm,
                    halo, corners, z1h, z1l, zph, zpl, z2h, z2l, sub, ger, gxe, txe, gym, gye, tym,
                    ext, t_ref, gx_ref, tx_ref, ty_ref, text_ref, gxw, txw,
                    pack_d, pack_u, from_d, from_u, t_low, t_high,
                    own_v, own_p, coarse, tested, load_sem, send_sem, recv_sem, ready):
    comps, rows, _ = ext.shape
    taps, cols = t_ref.shape
    margin = width // 2
    pairs, inner, _ = sub.shape
    innermost = ger.shape[1]
    me_x, me_y = lax.axis_index("gx"), lax.axis_index("gy")
    first, last = me_x == 0, me_x == nx - 1
    not_first, not_last = me_x > 0, me_x < nx - 1
    has_up, has_down = me_y < ny - 1, me_y > 0
    vertical = jnp.where(has_up, 1, 0) + jnp.where(has_down, 1, 0)
    sides = ((1, has_up), (-1, has_down))
    columns = ((0, None), (1, has_up), (-1, has_down))

    def device(dx, dy):
        return {"gx": lax.rem(me_x + dx + nx, nx), "gy": lax.rem(me_y + dy + ny, ny)}

    def signal(sem, dx, dy):
        pl.semaphore_signal(sem, inc=1, device_id=device(dx, dy), device_id_type=MESH)

    def column(condition, act):
        for dy, present in columns:
            pl.when(condition if present is None else condition & present)(lambda dy=dy: act(dy))

    barrier = pltpu.get_barrier_semaphore()
    pl.when(has_up)(lambda: signal(barrier, 0, 1))
    column(not_last, lambda dy: signal(barrier, 1, dy))
    column(first, lambda dy: signal(barrier, -1, dy))

    own = slice(0, cols)
    order = [(i, j) for i in range(comps) for j in range(i, comps)]
    loads = [pltpu.make_async_copy(src, dst, load_sem.at[i]) for i, (src, dst) in enumerate((
        (v_hbm, ext.at[:, :, own]), (t_hbm, t_ref), (gx_hbm, gx_ref), (tx_hbm, tx_ref), (ty_hbm, ty_ref)))]
    for load in loads:
        load.start()

    per = LANES // width
    groups = rows // width
    head, tail = pl.ds(0, SUB), pl.ds((groups - 1) * SUB, SUB)
    low_x, high_x = v_hbm.at[:, pl.ds(0, width), :], v_hbm.at[:, pl.ds(rows - width, width), :]
    copies = {}

    def remote(key, src, dst, dx, dy):
        n = len(copies)
        copies[key] = pltpu.make_async_remote_copy(
            src_ref=src, dst_ref=dst, send_sem=send_sem.at[n], recv_sem=recv_sem.at[n],
            device_id=device(dx, dy), device_id_type=MESH)

    remote((1, 0), high_x, halo.at[0], 1, 0)
    remote((-1, 0), low_x, halo.at[1], -1, 0)
    remote((1, 1), pack_u.at[:, tail, :], corners.at[0], 1, 1)
    remote((-1, 1), pack_u.at[:, head, :], corners.at[1], -1, 1)
    remote((1, -1), pack_d.at[:, tail, :], corners.at[2], 1, -1)
    remote((-1, -1), pack_d.at[:, head, :], corners.at[3], -1, -1)
    remote(("t", 1), t_ref.at[:, pl.ds(cols - LANES, LANES)], t_low, 0, 1)
    remote(("t", -1), t_ref.at[:, pl.ds(0, LANES)], t_high, 0, -1)
    for c in range(comps):
        remote((c, "v", 1), pack_u.at[c], from_d.at[c], 0, 1)
        remote((c, "v", -1), pack_d.at[c], from_u.at[c], 0, -1)

    @pl.when(last)
    def _():
        pl.semaphore_wait(barrier, jnp.where(has_down, 1, 0) + jnp.where(first, 0, 1 + vertical) + 1 + vertical)
        copies[1, 0].start()

    column(last, lambda dy: signal(ready.at[1 - dy], 1, dy))

    @pl.when(not_last & (not_first | has_down))
    def _():
        pl.semaphore_wait(barrier, jnp.where(has_down, 1, 0) + jnp.where(first, 0, 1 + vertical))

    pl.when(not_first)(lambda: copies[-1, 0].start())
    pl.when(has_down)(lambda: signal(ready.at[3], 0, -1))
    column(not_first, lambda dy: signal(ready.at[5 - dy], -1, dy))

    loads[0].wait()
    for c in range(comps):
        for g in range(groups):
            for q in range(per):
                src = pl.ds(g * width + q * SUB, SUB)
                dst = pl.ds(g * SUB, SUB)
                pack_u[c, dst, q * width:(q + 1) * width] = ext[c, src, cols - width:cols]
                pack_d[c, dst, q * width:(q + 1) * width] = ext[c, src, 0:width]

    text_ref[...] = jnp.zeros_like(text_ref)
    for z, full in ((z1h, rows), (z1l, rows), (zph, rows), (zpl, rows), (z2h, inner), (z2l, inner)):
        if z.shape[1] > full:
            z[:, full:, :] = jnp.zeros((z.shape[0], z.shape[1] - full, z.shape[2]), BF)
    for sign, present, mid in ((1, has_up, from_u), (-1, has_down, from_d)):
        @pl.when(jnp.logical_not(present))
        def _(sign=sign, mid=mid):
            mid[...] = jnp.zeros_like(mid)
            for side in range(2):
                corners[side + (2 if sign > 0 else 0)] = jnp.zeros(corners.shape[1:], F32)

    def wall(sign):
        copies["t", sign].start()
        for c in range(comps):
            copies[c, "v", sign].start()

    loads[1].wait()
    pl.when(has_down)(lambda: wall(-1))
    @pl.when(has_up)
    def _():
        pl.semaphore_wait(ready.at[3], 1)
        wall(1)

    for dy, present in sides:
        pl.when(last & present)(lambda dy=dy: copies[1, dy].start())
        pl.when(not_first & present)(lambda dy=dy: copies[-1, dy].start())

    for load in loads[2:]:
        load.wait()
    text_ref[0:taps, 0:cols] = t_ref[...]
    first_row, total = me_y * cols, cols * ny
    own_tiles = range(cols // LANES)
    y_weights(t_ref[...], taps, first_row, total, cols, gym, tiles=own_tiles)

    def own_pair(p):
        i, j = order[p]
        own_p[p] = y_own(ext[i, :, own] * ext[j, :, own], cols, gym)

    def forward(dx, dy):
        pl.semaphore_wait(ready.at[(5 if dx > 0 else 1) + dy], 1)
        copies[dx, dy].start()

    for c in range(comps):
        own_v[c] = y_own(ext[c, :, own], cols, gym)
    for p in range(0):
        own_pair(p)
    pl.when(not_last)(lambda: forward(1, 0))
    x_weights(gx_ref, gxw.shape[0], gxw, gxe)
    x_weights(tx_ref, txw.shape[0], txw, txe)
    y_weights(ty_ref[...], taps, first_row, total, cols, tym, tiles=own_tiles)
    for p in range(0, pairs):
        own_pair(p)
    for dy, present in sides:
        pl.when(not_last & present)(lambda dy=dy: forward(1, dy))

    for sign, present, tile, at in ((1, has_down, t_low, LANES - margin), (-1, has_up, t_high, 0)):
        @pl.when(present)
        def _(sign=sign, tile=tile, at=at):
            copies["t", sign].wait_recv()
            text_ref[0:taps, cols + at:cols + at + margin] = tile[:, at:at + margin]

    y_weights(text_ref[...], taps, first_row, total, cols, gym, gye, tiles=(cols // LANES,))

    def store(high, low, index, lanes, z):
        high[index, 0:z.shape[0], lanes], low[index, 0:z.shape[0], lanes] = split(z)

    def y_grid(c):
        blocks = []
        for g in range(groups):
            at = pl.ds(g * SUB, SUB)
            up, down = from_u[c, at, :], from_d[c, at, :]
            blocks += [side_lanes(up, down, q, width) for q in range(per)]
        halo = stacked(blocks)
        spread_halo = thrice(halo, width)
        ext[c, :, cols:] = spread_halo
        store(z1h, z1l, c, own, own_v[c] + y_halo(spread_halo, margin, cols, gym))
        store(z1h, z1l, c, slice(cols, cols + LANES), y_ends(ext[c, :, own], halo, margin, gye))

    def x_grid(c):
        def put(at, value):
            coarse[c, at, :] = value

        x_filter(z1h.at[c], z1l.at[c], inner, gxw, put)

    def y_pair(p):
        i, j = order[p]
        store(zph, zpl, p, own, own_p[p] + y_halo(ext[i, :, cols:] * ext[j, :, cols:], margin, cols, gym))

    def y_test(c):
        store(z2h, z2l, c, own, y_filter(coarse[c], margin, cols, tym))

    def x_test(c):
        def put(at, value):
            tested[c, at, :] = value

        x_filter(z2h.at[c], z2l.at[c], innermost, txw, put)

    def y_resolved(p):
        i, j = order[p]
        store(z2h, z2l, comps + p, own, y_filter(coarse[i] * coarse[j], margin, cols, tym))

    def x_sub(p):
        i, j = order[p]

        def put(at, value):
            sub[p, at, :] = value - coarse[i, at, own] * coarse[j, at, own]

        x_filter(zph.at[p], zpl.at[p], inner, gxw, put)

    def x_ger(p):
        i, j = order[p]

        def put(at, value):
            ger[p, at, :] = value - tested[i, at, :] * tested[j, at, :]

        x_filter(z2h.at[comps + p], z2l.at[comps + p], innermost, txw, put)

    def arrive(c):
        for sign, present in ((1, has_down), (-1, has_up)):
            pl.when(present)(lambda sign=sign: copies[c, "v", sign].wait_recv())

    for c in range(comps):
        arrive(c)
        y_grid(c)
        for p, (i, j) in enumerate(order):
            if j == c:
                y_pair(p)
        if c > 0:
            x_grid(c - 1)
    column(first, lambda dy: forward(-1, dy))
    x_grid(comps - 1)
    for c in range(comps):
        y_test(c)
        x_sub(c)
    for c in range(comps):
        y_resolved(c)
        x_test(c)

    for p in range(comps, pairs):
        y_resolved(p)
        x_sub(p)
        x_ger(p - comps)
    for p in range(pairs - comps, pairs):
        x_ger(p)

    copies[1, 0].wait_recv()
    copies[-1, 0].wait_recv()
    for sign, present in ((1, has_down), (-1, has_up)):
        @pl.when(present)
        def _(sign=sign):
            copies[1, sign].wait_recv()
            copies[-1, sign].wait_recv()

    copies[1, 0].wait_send()
    copies[-1, 0].wait_send()
    for sign, present in sides:
        @pl.when(present)
        def _(sign=sign):
            copies[1, sign].wait_send()
            copies[-1, sign].wait_send()
            copies["t", sign].wait_send()
            for c in range(comps):
                copies[c, "v", sign].wait_send()


def edge_kernel(margin, halo, corners, z1h, z1l, zph, zpl, z2h, z2l, sub_in, ger_in,
                gxe, txe, gym, gye, tym, sub_ref, ger_ref, sub_e, ger_e, sems):
    comps, cols = halo.shape[1], halo.shape[3]
    pairs, rows, _ = sub_ref.shape
    width = 2 * margin
    inner, innermost = sub_in.shape[1], ger_in.shape[1]
    order = [(i, j) for i in range(comps) for j in range(i, comps)]
    outs = []

    def leave(source, target):
        copy = pltpu.make_async_copy(source, target, sems.at[len(outs)])
        copy.start()
        outs.append(copy)

    for p in range(pairs):
        leave(sub_in.at[p], sub_ref.at[p, pl.ds(margin, inner), :])
        leave(ger_in.at[p], ger_ref.at[p, pl.ds(width, innermost), :])

    def ends(side, c):
        up, down = corners[2 + side, c], corners[side, c]
        return halo[side, c], stacked([side_lanes(up, down, q, width) for q in range(width // SUB)])

    def pieces(z, size, count):
        high, low = split(z)
        return [(high[n * size:(n + 1) * size], low[n * size:(n + 1) * size]) for n in range(count)]

    def x_ends(side, late, high, low, n, count, size, weights):
        at = slice(0, size) if side == 0 else slice(count - size, count)
        h = (late[0], high[n, at]) if side == 0 else (high[n, at], late[0])
        l = (late[1], low[n, at]) if side == 0 else (low[n, at], late[1])
        r = dot(weights, stacked(h + l))
        half = weights.shape[0] // 2
        return r[0:half] + r[half:]

    near = (slice(width - margin, width), slice(0, margin))
    everywhere = range(pairs)

    def grid(side):
        parts = [ends(side, c) for c in range(comps)]
        rows_own, rows_halo = stacked([part[0] for part in parts]), stacked([part[1] for part in parts])
        values = jnp.concatenate([rows_own, thrice(rows_halo, width)], axis=1)
        ext = [values[c * width:(c + 1) * width] for c in range(comps)]
        products = stacked([ext[i][near[side]] * ext[j][near[side]] for i, j in order])
        z = y_filter(stacked([values, products]), margin, cols, gym)
        count = comps * width
        late = pieces(jnp.concatenate([z[0:count], y_ends(rows_own, rows_halo, margin, gye)], axis=1), width, comps)
        return late, pieces(z[count:], margin, pairs)

    def coarsen(side, late):
        return [x_ends(side, part, z1h, z1l, c, rows, width, gxe[...]) for c, part in enumerate(late)]

    def stress(side, coarse, late):
        weights = stacked([gxe[0:margin], gxe[width:width + margin]] if side == 0 else
                          [gxe[width - margin:width], gxe[2 * width - margin:]])
        for p, part in enumerate(late):
            value = x_ends(side, part, zph, zpl, p, rows, width + margin, weights)
            i, j = order[p]
            sub_e[p, side] = value - coarse[i][near[side], 0:cols] * coarse[j][near[side], 0:cols]

    def test(side, coarse):
        z = y_filter(stacked(coarse + [coarse[i] * coarse[j] for i, j in order]), margin, cols, tym)
        return pieces(z, width, comps + pairs)

    def resolve(side, late):
        tested = [x_ends(side, part, z2h, z2l, c, inner, width, txe[...]) for c, part in enumerate(late[0:comps])]
        for p, part in enumerate(late[comps:]):
            i, j = order[p]
            ger_e[p, side] = (x_ends(side, part, z2h, z2l, comps + p, inner, width, txe[...])
                              - tested[i] * tested[j])

    late = [grid(side) for side in range(2)]
    coarse = [coarsen(side, late[side][0]) for side in range(2)]
    tests = []
    for side in range(2):
        tests.append(test(side, coarse[side]))
        stress(side, coarse[side], late[side][1])
    leave(sub_e.at[:, 0], sub_ref.at[:, pl.ds(0, margin), :])
    leave(sub_e.at[:, 1], sub_ref.at[:, pl.ds(rows - margin, margin), :])
    resolve(0, tests[0])
    leave(ger_e.at[:, 0], ger_ref.at[:, pl.ds(0, width), :])
    resolve(1, tests[1])
    leave(ger_e.at[:, 1], ger_ref.at[:, pl.ds(rows - width, width), :])
    for copy in outs:
        copy.wait()


def local(nx, ny, velocity, grid_x, grid_y, test_x, test_y):
    comps, planes, cols, rows = velocity.shape
    taps = grid_x.shape[0]
    margin = (taps - 1) // 2
    width = 2 * margin
    wide = cols + LANES
    step = LANES - width
    pairs = comps * (comps + 1) // 2
    vmem = pl.BlockSpec(memory_space=pltpu.VMEM)
    anywhere = pl.BlockSpec(memory_space=pl.ANY)
    packed = rows // width * SUB
    inner, innermost = rows - width, rows - 2 * width

    def filled(count):
        return round_up(count, step) + width

    fields = comps + pairs
    subs, gers = [], []
    shape = jax.ShapeDtypeStruct
    for plane in range(planes):
        v = jnp.swapaxes(velocity[:, plane], 1, 2)
        parts = pl.pallas_call(
            functools.partial(interior_kernel, nx, ny, width),
            out_shape=(
                shape((2, comps, width, cols), F32),
                shape((4, comps, SUB, LANES), F32),
                shape((comps, max(rows, filled(inner)), wide), BF),
                shape((comps, max(rows, filled(inner)), wide), BF),
                shape((pairs, max(rows, filled(inner)), cols), BF),
                shape((pairs, max(rows, filled(inner)), cols), BF),
                shape((fields, max(inner, filled(innermost)), cols), BF),
                shape((fields, max(inner, filled(innermost)), cols), BF),
                shape((pairs, inner, cols), F32),
                shape((pairs, innermost, cols), F32),
                shape((2 * width, LANES), BF),
                shape((2 * width, LANES), BF),
                shape((3 * cols + LANES, cols), BF),
                shape((3 * LANES, LANES), BF),
                shape((3 * cols + LANES, cols), BF),
            ),
            in_specs=[pl.BlockSpec(memory_space=pltpu.HBM)] * 5,
            out_specs=(vmem,) * 15,
            scratch_shapes=[
                pltpu.VMEM((comps, rows, wide), F32),
                pltpu.VMEM((taps, cols), F32),
                pltpu.VMEM((1, taps), F32),
                pltpu.VMEM((1, taps), F32),
                pltpu.VMEM((taps, cols), F32),
                pltpu.VMEM((round_up(taps, SUB), wide), F32),
                pltpu.VMEM((step, 3 * LANES), BF),
                pltpu.VMEM((step, 3 * LANES), BF),
                pltpu.VMEM((comps, packed, LANES), F32),
                pltpu.VMEM((comps, packed, LANES), F32),
                pltpu.VMEM((comps, packed, LANES), F32),
                pltpu.VMEM((comps, packed, LANES), F32),
                pltpu.VMEM((taps, LANES), F32),
                pltpu.VMEM((taps, LANES), F32),
                pltpu.VMEM((comps, rows, cols), F32),
                pltpu.VMEM((pairs, rows, cols), F32),
                pltpu.VMEM((comps, inner, wide), F32),
                pltpu.VMEM((comps, innermost, cols), F32),
                pltpu.SemaphoreType.DMA((5,)),
                pltpu.SemaphoreType.DMA((8 + 2 * comps,)),
                pltpu.SemaphoreType.DMA((8 + 2 * comps,)),
                pltpu.SemaphoreType.REGULAR((7,)),
            ],
            compiler_params=pltpu.CompilerParams(
                collective_id=plane, has_side_effects=True, vmem_limit_bytes=20 << 20),
            name="interior",
        )(*[pltpu.with_memory_space_constraint(x, pltpu.HBM) for x in (
            v, grid_y.T, grid_x.reshape(1, taps), test_x.reshape(1, taps), test_y.T)])
        out = shape((pairs, rows, cols), F32)
        sub, ger = pl.pallas_call(
            functools.partial(edge_kernel, margin),
            out_shape=(out, out),
            in_specs=[vmem] * 15,
            out_specs=(anywhere, anywhere),
            scratch_shapes=[
                pltpu.VMEM((pairs, 2, margin, cols), F32),
                pltpu.VMEM((pairs, 2, width, cols), F32),
                pltpu.SemaphoreType.DMA((2 * pairs + 4,)),
            ],
            compiler_params=pltpu.CompilerParams(vmem_limit_bytes=8 << 20),
            name="edge",
        )(*parts)
        subs.append(jnp.swapaxes(sub, 1, 2))
        gers.append(jnp.swapaxes(ger, 1, 2))
    return jnp.stack(subs, axis=1), jnp.stack(gers, axis=1)


def solution(mesh):
    nx, ny = mesh.shape["gx"], mesh.shape["gy"]
    field = P(None, None, "gy", "gx")
    return jax.shard_map(
        functools.partial(local, nx, ny),
        mesh=mesh,
        in_specs=(field, P(), P("gy", None), P(), P("gy", None)),
        out_specs=(field, field),
        check_vma=False,
    )
```

```python
import functools

import jax
import jax.numpy as jnp
from jax import lax
from jax.experimental import pallas as pl
from jax.experimental.pallas import tpu as pltpu
from jax.sharding import PartitionSpec as P

MESH = pl.DeviceIdType.MESH
LANES = 128
SUB = 8
BF = jnp.bfloat16
F32 = jnp.float32


def round_up(value, unit):
    return (value + unit - 1) // unit * unit


def split(value):
    high = value.astype(BF)
    return high, (value - high.astype(F32)).astype(BF)


def dot(a, b):
    return jnp.dot(a, b, preferred_element_type=F32)


def x_weights(w_ref, step, out, edge):
    taps = w_ref.shape[1]
    w = jnp.concatenate([w_ref[...], jnp.zeros((1, LANES - taps), F32)], axis=1)
    w = w / jnp.sum(w)
    band = pltpu.roll(jnp.broadcast_to(w, (LANES, LANES)), 0, 1, stride=1, stride_axis=0)
    high, low = split(band[0:step])
    out[:, 0:LANES] = high
    out[:, LANES:2 * LANES] = high
    out[:, 2 * LANES:] = low
    width = edge.shape[0] // 2
    high, low = split(band[0:width])
    high = high.astype(F32)
    edge[0:width] = (high + pltpu.roll(high, 2 * width, 1)).astype(BF)
    edge[width:] = low


def spread(value, margin):
    lane = lax.broadcasted_iota(jnp.int32, value.shape, 1)
    near = jnp.where((lane < margin) | (lane >= LANES - margin), value, 0.0)
    return pltpu.roll(jnp.where(lane < LANES // 2, near, 0.0), margin, 1) + pltpu.roll(
        jnp.where(lane < LANES // 2, 0.0, near), LANES - margin, 1)


def y_weights(table, taps, first_row, total, cols, main, edge=None, tiles=None):
    margin = (taps - 1) // 2
    width = 2 * margin
    lanes = table.shape[1]
    wide = cols + LANES
    k = lax.broadcasted_iota(jnp.int32, (LANES, lanes), 0)
    lane = lax.broadcasted_iota(jnp.int32, (LANES, lanes), 1)
    y = first_row + jnp.where(lane < cols + LANES // 2, lane, lane - wide)
    source = y + k - margin
    keep = (k < taps) & (source >= 0) & (source < total) & (y >= 0) & (y < total)
    w = jnp.where(keep, jnp.concatenate(
        [table, jnp.zeros((LANES - table.shape[0], lanes), F32)], axis=0), 0.0)
    s = jnp.sum(w, axis=0, keepdims=True)
    w = (w / jnp.where(s > 0.0, s, 1.0)).T
    zeros = jnp.zeros((LANES, cols), F32)
    for t in (range(lanes // LANES) if tiles is None else tiles):
        at = slice(t * LANES, (t + 1) * LANES)
        tile = jnp.concatenate([w[at], zeros], axis=1)
        band = pltpu.roll(tile, (t * LANES - margin) % wide, 1, stride=1, stride_axis=0)
        if t * LANES < cols:
            own, halo = band[:, 0:cols].T, band[:, cols:]
            own_high, own_low = split(own)
            main[0:cols, at] = own_high
            main[cols:2 * cols, at] = own_low
            main[2 * cols:3 * cols, at] = own_high
            halo = spread(halo, margin)
            high = halo.astype(BF).astype(F32)
            packed = high + pltpu.roll(high, width, 1) + pltpu.roll(halo - high, 2 * width, 1)
            main[3 * cols:, at] = packed.T.astype(BF)
        else:
            low_own, high_own, halo = band[:, 0:LANES].T, band[:, cols - LANES:cols].T, band[:, cols:].T
            near = jnp.concatenate([
                low_own[0:margin], halo[0:width], jnp.zeros((LANES - 2 * margin - 2 * width, LANES), F32),
                halo[LANES - width:], high_own[LANES - margin:]], axis=0)
            near = spread(near, margin)
            near = near + pltpu.roll(near, width, 1) + pltpu.roll(near, 2 * width, 1)
            high, low = split(near)
            edge[0:LANES] = high
            edge[LANES:2 * LANES] = high
            edge[2 * LANES:] = low


def y_own(value, cols, main):
    high, low = split(value)
    return dot(jnp.concatenate([high, high, low], axis=1), main[0:3 * cols])


def second(shape, width):
    lane = lax.broadcasted_iota(jnp.int32, shape, 1)
    return (lane < width // 2) | ((lane >= width + width // 2) & (lane < 2 * width))


def thrice(halo, width):
    lane = lax.broadcasted_iota(jnp.int32, halo.shape, 1)
    margin = width // 2
    home = ((lane >= margin) & (lane < width)) | ((lane >= LANES - width) & (lane < LANES - margin))
    return jnp.where(home, halo, jnp.where(
        second(halo.shape, width), pltpu.roll(halo, width, 1), pltpu.roll(halo, 2 * width, 1)))


def packed_halo(halo, margin):
    high = halo.astype(BF).astype(F32)
    return jnp.where(second(halo.shape, 2 * margin), halo - high, high).astype(BF)


def y_halo(halo, margin, cols, main):
    return dot(packed_halo(halo, margin), main[3 * cols:])


def y_filter(value, margin, cols, main):
    high, low = split(value[:, 0:cols])
    return dot(jnp.concatenate([high, high, low, packed_halo(value[:, cols:], margin)], axis=1), main[...])


def y_ends(own, halo, margin, edge):
    lane = lax.broadcasted_iota(jnp.int32, halo.shape, 1)
    ends = jnp.where(lane < margin, own[:, 0:LANES],
                     jnp.where(lane >= LANES - margin, own[:, own.shape[1] - LANES:], halo))
    high, low = split(ends)
    return dot(jnp.concatenate([high, low, high], axis=1), edge[...])


def side_lanes(up, down, q, width):
    lane = lax.broadcasted_iota(jnp.int32, up.shape, 1)
    margin = width // 2
    return jnp.where(lane < LANES // 2, pltpu.roll(up, (LANES + margin - q * width) % LANES, 1),
                     pltpu.roll(down, (2 * LANES - margin - (q + 1) * width) % LANES, 1))


def x_filter(zh, zl, count, weights, put):
    step = weights.shape[0]
    for s in range(0, count, step):
        size = min(step, count - s)
        at = slice(s, s + LANES)
        high = zh[at]
        put(slice(s, s + size), dot(weights[0:size], jnp.concatenate([high, zl[at], high], axis=0)))


def stacked(values):
    return jnp.concatenate(values, axis=0)


def interior_kernel(nx, ny, width, v_hbm, t_hbm, gx_hbm, tx_hbm, ty_hbm,
                    halo, corners, z1h, z1l, zph, zpl, z2h, z2l, sub, ger, gxe, txe, gym, gye, tym,
                    ext, t_ref, gx_ref, tx_ref, ty_ref, text_ref, gxw, txw,
                    pack_d, pack_u, from_d, from_u, t_low, t_high,
                    own_v, own_p, coarse, tested, load_sem, send_sem, recv_sem, ready):
    comps, rows, _ = ext.shape
    taps, cols = t_ref.shape
    margin = width // 2
    pairs, inner, _ = sub.shape
    innermost = ger.shape[1]
    me_x, me_y = lax.axis_index("gx"), lax.axis_index("gy")
    first, last = me_x == 0, me_x == nx - 1
    not_first, not_last = me_x > 0, me_x < nx - 1
    has_up, has_down = me_y < ny - 1, me_y > 0
    vertical = jnp.where(has_up, 1, 0) + jnp.where(has_down, 1, 0)
    sides = ((1, has_up), (-1, has_down))
    columns = ((0, None), (1, has_up), (-1, has_down))

    def device(dx, dy):
        return {"gx": lax.rem(me_x + dx + nx, nx), "gy": lax.rem(me_y + dy + ny, ny)}

    def signal(sem, dx, dy):
        pl.semaphore_signal(sem, inc=1, device_id=device(dx, dy), device_id_type=MESH)

    def column(condition, act):
        for dy, present in columns:
            pl.when(condition if present is None else condition & present)(lambda dy=dy: act(dy))

    barrier = pltpu.get_barrier_semaphore()
    pl.when(has_up)(lambda: signal(barrier, 0, 1))
    column(not_last, lambda dy: signal(barrier, 1, dy))
    column(first, lambda dy: signal(barrier, -1, dy))

    own = slice(0, cols)
    order = [(i, j) for i in range(comps) for j in range(i, comps)]
    loads = [pltpu.make_async_copy(src, dst, load_sem.at[i]) for i, (src, dst) in enumerate(
        [(v_hbm.at[0], ext.at[0, :, own]), (t_hbm, t_ref)]
        + [(v_hbm.at[c], ext.at[c, :, own]) for c in range(1, comps)]
        + [(gx_hbm, gx_ref), (tx_hbm, tx_ref), (ty_hbm, ty_ref)])]
    for load in loads:
        load.start()

    per = LANES // width
    groups = rows // width
    head, tail = pl.ds(0, SUB), pl.ds((groups - 1) * SUB, SUB)
    low_x, high_x = v_hbm.at[:, pl.ds(0, width), :], v_hbm.at[:, pl.ds(rows - width, width), :]
    copies = {}

    def remote(key, src, dst, dx, dy):
        n = len(copies)
        copies[key] = pltpu.make_async_remote_copy(
            src_ref=src, dst_ref=dst, send_sem=send_sem.at[n], recv_sem=recv_sem.at[n],
            device_id=device(dx, dy), device_id_type=MESH)

    remote((1, 0), high_x, halo.at[0], 1, 0)
    remote((-1, 0), low_x, halo.at[1], -1, 0)
    remote((1, 1), pack_u.at[:, tail, :], corners.at[0], 1, 1)
    remote((-1, 1), pack_u.at[:, head, :], corners.at[1], -1, 1)
    remote((1, -1), pack_d.at[:, tail, :], corners.at[2], 1, -1)
    remote((-1, -1), pack_d.at[:, head, :], corners.at[3], -1, -1)
    remote(("t", 1), t_ref.at[:, pl.ds(cols - LANES, LANES)], t_low, 0, 1)
    remote(("t", -1), t_ref.at[:, pl.ds(0, LANES)], t_high, 0, -1)
    for c in range(comps):
        remote((c, "v", 1), pack_u.at[c], from_d.at[c], 0, 1)
        remote((c, "v", -1), pack_d.at[c], from_u.at[c], 0, -1)

    @pl.when(last)
    def _():
        pl.semaphore_wait(barrier, jnp.where(has_down, 1, 0) + jnp.where(first, 0, 1 + vertical) + 1 + vertical)
        copies[1, 0].start()

    column(last, lambda dy: signal(ready.at[1 - dy], 1, dy))

    @pl.when(not_last & (not_first | has_down))
    def _():
        pl.semaphore_wait(barrier, jnp.where(has_down, 1, 0) + jnp.where(first, 0, 1 + vertical))

    pl.when(not_first)(lambda: copies[-1, 0].start())
    pl.when(has_down)(lambda: signal(ready.at[3], 0, -1))
    column(not_first, lambda dy: signal(ready.at[5 - dy], -1, dy))

    def pack(c):
        for g in range(groups):
            for q in range(per):
                src = pl.ds(g * width + q * SUB, SUB)
                dst = pl.ds(g * SUB, SUB)
                pack_u[c, dst, q * width:(q + 1) * width] = ext[c, src, cols - width:cols]
                pack_d[c, dst, q * width:(q + 1) * width] = ext[c, src, 0:width]

    for c in range(comps):
        loads[c + (c > 0)].wait()
        pack(c)
        if c == 0:
            loads[1].wait()
            pl.when(has_down)(lambda: copies["t", -1].start())
        else:
            pl.when(has_down)(lambda c=c: copies[c - 1, "v", -1].start())

    text_ref[...] = jnp.zeros_like(text_ref)
    for z, full in ((z1h, rows), (z1l, rows), (zph, rows), (zpl, rows), (z2h, inner), (z2l, inner)):
        if z.shape[1] > full:
            z[:, full:, :] = jnp.zeros((z.shape[0], z.shape[1] - full, z.shape[2]), BF)
    for sign, present, mid in ((1, has_up, from_u), (-1, has_down, from_d)):
        @pl.when(jnp.logical_not(present))
        def _(sign=sign, mid=mid):
            mid[...] = jnp.zeros_like(mid)
            for side in range(2):
                corners[side + (2 if sign > 0 else 0)] = jnp.zeros(corners.shape[1:], F32)

    pl.when(has_down)(lambda: copies[comps - 1, "v", -1].start())

    @pl.when(has_up)
    def _():
        pl.semaphore_wait(ready.at[3], 1)
        copies["t", 1].start()
        for c in range(comps):
            copies[c, "v", 1].start()

    for dy, present in sides:
        pl.when(last & present)(lambda dy=dy: copies[1, dy].start())
        pl.when(not_first & present)(lambda dy=dy: copies[-1, dy].start())

    for load in loads[comps + 1:]:
        load.wait()
    text_ref[0:taps, 0:cols] = t_ref[...]
    first_row, total = me_y * cols, cols * ny
    own_tiles = range(cols // LANES)
    y_weights(t_ref[...], taps, first_row, total, cols, gym, tiles=own_tiles)

    def own_pair(p):
        i, j = order[p]
        own_p[p] = y_own(ext[i, :, own] * ext[j, :, own], cols, gym)

    def forward(dx, dy):
        pl.semaphore_wait(ready.at[(5 if dx > 0 else 1) + dy], 1)
        copies[dx, dy].start()

    for c in range(comps):
        own_v[c] = y_own(ext[c, :, own], cols, gym)
    for p in range(0):
        own_pair(p)
    pl.when(not_last)(lambda: forward(1, 0))
    x_weights(gx_ref, gxw.shape[0], gxw, gxe)
    x_weights(tx_ref, txw.shape[0], txw, txe)
    y_weights(ty_ref[...], taps, first_row, total, cols, tym, tiles=own_tiles)
    for p in range(0, pairs):
        own_pair(p)
    for dy, present in sides:
        pl.when(not_last & present)(lambda dy=dy: forward(1, dy))

    for sign, present, tile, at in ((1, has_down, t_low, LANES - margin), (-1, has_up, t_high, 0)):
        @pl.when(present)
        def _(sign=sign, tile=tile, at=at):
            copies["t", sign].wait_recv()
            text_ref[0:taps, cols + at:cols + at + margin] = tile[:, at:at + margin]

    y_weights(text_ref[...], taps, first_row, total, cols, gym, gye, tiles=(cols // LANES,))

    def store(high, low, index, lanes, z):
        high[index, 0:z.shape[0], lanes], low[index, 0:z.shape[0], lanes] = split(z)

    def y_grid(c):
        blocks = []
        for g in range(groups):
            at = pl.ds(g * SUB, SUB)
            up, down = from_u[c, at, :], from_d[c, at, :]
            blocks += [side_lanes(up, down, q, width) for q in range(per)]
        halo = stacked(blocks)
        spread_halo = thrice(halo, width)
        ext[c, :, cols:] = spread_halo
        store(z1h, z1l, c, own, own_v[c] + y_halo(spread_halo, margin, cols, gym))
        store(z1h, z1l, c, slice(cols, cols + LANES), y_ends(ext[c, :, own], halo, margin, gye))

    def x_grid(c):
        def put(at, value):
            coarse[c, at, :] = value

        x_filter(z1h.at[c], z1l.at[c], inner, gxw, put)

    def y_pair(p):
        i, j = order[p]
        store(zph, zpl, p, own, own_p[p] + y_halo(ext[i, :, cols:] * ext[j, :, cols:], margin, cols, gym))

    def y_test(c):
        store(z2h, z2l, c, own, y_filter(coarse[c], margin, cols, tym))

    def x_test(c):
        def put(at, value):
            tested[c, at, :] = value

        x_filter(z2h.at[c], z2l.at[c], innermost, txw, put)

    def y_resolved(p):
        i, j = order[p]
        store(z2h, z2l, comps + p, own, y_filter(coarse[i] * coarse[j], margin, cols, tym))

    def x_sub(p):
        i, j = order[p]

        def put(at, value):
            sub[p, at, :] = value - coarse[i, at, own] * coarse[j, at, own]

        x_filter(zph.at[p], zpl.at[p], inner, gxw, put)

    def x_ger(p):
        i, j = order[p]

        def put(at, value):
            ger[p, at, :] = value - tested[i, at, :] * tested[j, at, :]

        x_filter(z2h.at[comps + p], z2l.at[comps + p], innermost, txw, put)

    def arrive(c):
        for sign, present in ((1, has_down), (-1, has_up)):
            pl.when(present)(lambda sign=sign: copies[c, "v", sign].wait_recv())

    for c in range(comps):
        arrive(c)
        y_grid(c)
        for p, (i, j) in enumerate(order):
            if j == c:
                y_pair(p)
        if c > 0:
            x_grid(c - 1)
    x_grid(comps - 1)
    for c in range(comps):
        if c == 1:
            column(first, lambda dy: forward(-1, dy))
        y_test(c)
        x_sub(c)
    for c in range(comps):
        y_resolved(c)
        x_test(c)

    for p in range(comps, pairs):
        y_resolved(p)
        x_sub(p)
        x_ger(p - comps)
    for p in range(pairs - comps, pairs):
        x_ger(p)

    copies[1, 0].wait_recv()
    copies[-1, 0].wait_recv()
    for sign, present in ((1, has_down), (-1, has_up)):
        @pl.when(present)
        def _(sign=sign):
            copies[1, sign].wait_recv()
            copies[-1, sign].wait_recv()

    copies[1, 0].wait_send()
    copies[-1, 0].wait_send()
    for sign, present in sides:
        @pl.when(present)
        def _(sign=sign):
            copies[1, sign].wait_send()
            copies[-1, sign].wait_send()
            copies["t", sign].wait_send()
            for c in range(comps):
                copies[c, "v", sign].wait_send()


def edge_kernel(margin, halo, corners, z1h, z1l, zph, zpl, z2h, z2l, sub_in, ger_in,
                gxe, txe, gym, gye, tym, sub_ref, ger_ref, sub_e, ger_e, sems):
    comps, cols = halo.shape[1], halo.shape[3]
    pairs, rows, _ = sub_ref.shape
    width = 2 * margin
    inner, innermost = sub_in.shape[1], ger_in.shape[1]
    order = [(i, j) for i in range(comps) for j in range(i, comps)]
    outs = []

    def leave(source, target):
        copy = pltpu.make_async_copy(source, target, sems.at[len(outs)])
        copy.start()
        outs.append(copy)

    for p in range(pairs):
        leave(sub_in.at[p], sub_ref.at[p, pl.ds(margin, inner), :])
        leave(ger_in.at[p], ger_ref.at[p, pl.ds(width, innermost), :])

    def ends(side, c):
        up, down = corners[2 + side, c], corners[side, c]
        return halo[side, c], stacked([side_lanes(up, down, q, width) for q in range(width // SUB)])

    def pieces(z, size, count):
        high, low = split(z)
        return [(high[n * size:(n + 1) * size], low[n * size:(n + 1) * size]) for n in range(count)]

    def x_ends(side, late, high, low, n, count, size, weights):
        at = slice(0, size) if side == 0 else slice(count - size, count)
        h = (late[0], high[n, at]) if side == 0 else (high[n, at], late[0])
        l = (late[1], low[n, at]) if side == 0 else (low[n, at], late[1])
        r = dot(weights, stacked(h + l))
        half = weights.shape[0] // 2
        return r[0:half] + r[half:]

    near = (slice(width - margin, width), slice(0, margin))
    everywhere = range(pairs)

    def grid(side):
        parts = [ends(side, c) for c in range(comps)]
        rows_own, rows_halo = stacked([part[0] for part in parts]), stacked([part[1] for part in parts])
        values = jnp.concatenate([rows_own, thrice(rows_halo, width)], axis=1)
        ext = [values[c * width:(c + 1) * width] for c in range(comps)]
        products = stacked([ext[i][near[side]] * ext[j][near[side]] for i, j in order])
        z = y_filter(stacked([values, products]), margin, cols, gym)
        count = comps * width
        late = pieces(jnp.concatenate([z[0:count], y_ends(rows_own, rows_halo, margin, gye)], axis=1), width, comps)
        return late, pieces(z[count:], margin, pairs)

    def coarsen(side, late):
        return [x_ends(side, part, z1h, z1l, c, rows, width, gxe[...]) for c, part in enumerate(late)]

    def stress(side, coarse, late):
        weights = stacked([gxe[0:margin], gxe[width:width + margin]] if side == 0 else
                          [gxe[width - margin:width], gxe[2 * width - margin:]])
        for p, part in enumerate(late):
            value = x_ends(side, part, zph, zpl, p, rows, width + margin, weights)
            i, j = order[p]
            sub_e[p, side] = value - coarse[i][near[side], 0:cols] * coarse[j][near[side], 0:cols]

    def test(side, coarse):
        z = y_filter(stacked(coarse + [coarse[i] * coarse[j] for i, j in order]), margin, cols, tym)
        return pieces(z, width, comps + pairs)

    def resolve(side, late):
        tested = [x_ends(side, part, z2h, z2l, c, inner, width, txe[...]) for c, part in enumerate(late[0:comps])]
        for p, part in enumerate(late[comps:]):
            i, j = order[p]
            ger_e[p, side] = (x_ends(side, part, z2h, z2l, comps + p, inner, width, txe[...])
                              - tested[i] * tested[j])

    late = [grid(side) for side in range(2)]
    coarse = [coarsen(side, late[side][0]) for side in range(2)]
    tests = []
    for side in range(2):
        tests.append(test(side, coarse[side]))
        stress(side, coarse[side], late[side][1])
    leave(sub_e.at[:, 0], sub_ref.at[:, pl.ds(0, margin), :])
    leave(sub_e.at[:, 1], sub_ref.at[:, pl.ds(rows - margin, margin), :])
    resolve(0, tests[0])
    leave(ger_e.at[:, 0], ger_ref.at[:, pl.ds(0, width), :])
    resolve(1, tests[1])
    leave(ger_e.at[:, 1], ger_ref.at[:, pl.ds(rows - width, width), :])
    for copy in outs:
        copy.wait()


def local(nx, ny, velocity, grid_x, grid_y, test_x, test_y):
    comps, planes, cols, rows = velocity.shape
    taps = grid_x.shape[0]
    margin = (taps - 1) // 2
    width = 2 * margin
    wide = cols + LANES
    step = LANES - width
    pairs = comps * (comps + 1) // 2
    vmem = pl.BlockSpec(memory_space=pltpu.VMEM)
    anywhere = pl.BlockSpec(memory_space=pl.ANY)
    packed = rows // width * SUB
    inner, innermost = rows - width, rows - 2 * width

    def filled(count):
        return round_up(count, step) + width

    fields = comps + pairs
    subs, gers = [], []
    shape = jax.ShapeDtypeStruct
    for plane in range(planes):
        v = jnp.swapaxes(velocity[:, plane], 1, 2)
        parts = pl.pallas_call(
            functools.partial(interior_kernel, nx, ny, width),
            out_shape=(
                shape((2, comps, width, cols), F32),
                shape((4, comps, SUB, LANES), F32),
                shape((comps, max(rows, filled(inner)), wide), BF),
                shape((comps, max(rows, filled(inner)), wide), BF),
                shape((pairs, max(rows, filled(inner)), cols), BF),
                shape((pairs, max(rows, filled(inner)), cols), BF),
                shape((fields, max(inner, filled(innermost)), cols), BF),
                shape((fields, max(inner, filled(innermost)), cols), BF),
                shape((pairs, inner, cols), F32),
                shape((pairs, innermost, cols), F32),
                shape((2 * width, LANES), BF),
                shape((2 * width, LANES), BF),
                shape((3 * cols + LANES, cols), BF),
                shape((3 * LANES, LANES), BF),
                shape((3 * cols + LANES, cols), BF),
            ),
            in_specs=[pl.BlockSpec(memory_space=pltpu.HBM)] * 5,
            out_specs=(vmem,) * 15,
            scratch_shapes=[
                pltpu.VMEM((comps, rows, wide), F32),
                pltpu.VMEM((taps, cols), F32),
                pltpu.VMEM((1, taps), F32),
                pltpu.VMEM((1, taps), F32),
                pltpu.VMEM((taps, cols), F32),
                pltpu.VMEM((round_up(taps, SUB), wide), F32),
                pltpu.VMEM((step, 3 * LANES), BF),
                pltpu.VMEM((step, 3 * LANES), BF),
                pltpu.VMEM((comps, packed, LANES), F32),
                pltpu.VMEM((comps, packed, LANES), F32),
                pltpu.VMEM((comps, packed, LANES), F32),
                pltpu.VMEM((comps, packed, LANES), F32),
                pltpu.VMEM((taps, LANES), F32),
                pltpu.VMEM((taps, LANES), F32),
                pltpu.VMEM((comps, rows, cols), F32),
                pltpu.VMEM((pairs, rows, cols), F32),
                pltpu.VMEM((comps, inner, wide), F32),
                pltpu.VMEM((comps, innermost, cols), F32),
                pltpu.SemaphoreType.DMA((4 + comps,)),
                pltpu.SemaphoreType.DMA((8 + 2 * comps,)),
                pltpu.SemaphoreType.DMA((8 + 2 * comps,)),
                pltpu.SemaphoreType.REGULAR((7,)),
            ],
            compiler_params=pltpu.CompilerParams(
                collective_id=plane, has_side_effects=True, vmem_limit_bytes=20 << 20),
            name="interior",
        )(*[pltpu.with_memory_space_constraint(x, pltpu.HBM) for x in (
            v, grid_y.T, grid_x.reshape(1, taps), test_x.reshape(1, taps), test_y.T)])
        out = shape((pairs, rows, cols), F32)
        sub, ger = pl.pallas_call(
            functools.partial(edge_kernel, margin),
            out_shape=(out, out),
            in_specs=[vmem] * 15,
            out_specs=(anywhere, anywhere),
            scratch_shapes=[
                pltpu.VMEM((pairs, 2, margin, cols), F32),
                pltpu.VMEM((pairs, 2, width, cols), F32),
                pltpu.SemaphoreType.DMA((2 * pairs + 4,)),
            ],
            compiler_params=pltpu.CompilerParams(
                vmem_limit_bytes=8 << 20),
            name="edge",
        )(*parts)
        subs.append(jnp.swapaxes(sub, 1, 2))
        gers.append(jnp.swapaxes(ger, 1, 2))
    return jnp.stack(subs, axis=1), jnp.stack(gers, axis=1)


def solution(mesh):
    nx, ny = mesh.shape["gx"], mesh.shape["gy"]
    field = P(None, None, "gy", "gx")
    return jax.shard_map(
        functools.partial(local, nx, ny),
        mesh=mesh,
        in_specs=(field, P(), P("gy", None), P(), P("gy", None)),
        out_specs=(field, field),
        check_vma=False,
    )
```

```python
import functools

import jax
import jax.numpy as jnp
from jax import lax
from jax.experimental import pallas as pl
from jax.experimental.pallas import tpu as pltpu
from jax.sharding import PartitionSpec as P

MESH = pl.DeviceIdType.MESH
LANES = 128
SUB = 8
BF = jnp.bfloat16
F32 = jnp.float32


def round_up(value, unit):
    return (value + unit - 1) // unit * unit


def split(value):
    high = value.astype(BF)
    return high, (value - high.astype(F32)).astype(BF)


def dot(a, b):
    return jnp.dot(a, b, preferred_element_type=F32)


def x_weights(w_ref, step, out, edge):
    taps = w_ref.shape[1]
    w = jnp.concatenate([w_ref[...], jnp.zeros((1, LANES - taps), F32)], axis=1)
    w = w / jnp.sum(w)
    band = pltpu.roll(jnp.broadcast_to(w, (LANES, LANES)), 0, 1, stride=1, stride_axis=0)
    high, low = split(band[0:step])
    out[:, 0:LANES] = high
    out[:, LANES:2 * LANES] = high
    out[:, 2 * LANES:] = low
    width = edge.shape[0] // 2
    high, low = split(band[0:width])
    high = high.astype(F32)
    edge[0:width] = (high + pltpu.roll(high, 2 * width, 1)).astype(BF)
    edge[width:] = low


def spread(value, margin):
    lane = lax.broadcasted_iota(jnp.int32, value.shape, 1)
    near = jnp.where((lane < margin) | (lane >= LANES - margin), value, 0.0)
    return pltpu.roll(jnp.where(lane < LANES // 2, near, 0.0), margin, 1) + pltpu.roll(
        jnp.where(lane < LANES // 2, 0.0, near), LANES - margin, 1)


def y_weights(table, taps, first_row, total, cols, main, edge=None, tiles=None):
    margin = (taps - 1) // 2
    width = 2 * margin
    lanes = table.shape[1]
    wide = cols + LANES
    k = lax.broadcasted_iota(jnp.int32, (LANES, lanes), 0)
    lane = lax.broadcasted_iota(jnp.int32, (LANES, lanes), 1)
    y = first_row + jnp.where(lane < cols + LANES // 2, lane, lane - wide)
    source = y + k - margin
    keep = (k < taps) & (source >= 0) & (source < total) & (y >= 0) & (y < total)
    w = jnp.where(keep, jnp.concatenate(
        [table, jnp.zeros((LANES - table.shape[0], lanes), F32)], axis=0), 0.0)
    s = jnp.sum(w, axis=0, keepdims=True)
    w = (w / jnp.where(s > 0.0, s, 1.0)).T
    zeros = jnp.zeros((LANES, cols), F32)
    for t in (range(lanes // LANES) if tiles is None else tiles):
        at = slice(t * LANES, (t + 1) * LANES)
        tile = jnp.concatenate([w[at], zeros], axis=1)
        band = pltpu.roll(tile, (t * LANES - margin) % wide, 1, stride=1, stride_axis=0)
        if t * LANES < cols:
            own, halo = band[:, 0:cols].T, band[:, cols:]
            own_high, own_low = split(own)
            main[0:cols, at] = own_high
            main[cols:2 * cols, at] = own_low
            main[2 * cols:3 * cols, at] = own_high
            halo = spread(halo, margin)
            high = halo.astype(BF).astype(F32)
            packed = high + pltpu.roll(high, width, 1) + pltpu.roll(halo - high, 2 * width, 1)
            main[3 * cols:, at] = packed.T.astype(BF)
        else:
            low_own, high_own, halo = band[:, 0:LANES].T, band[:, cols - LANES:cols].T, band[:, cols:].T
            near = jnp.concatenate([
                low_own[0:margin], halo[0:width], jnp.zeros((LANES - 2 * margin - 2 * width, LANES), F32),
                halo[LANES - width:], high_own[LANES - margin:]], axis=0)
            near = spread(near, margin)
            near = near + pltpu.roll(near, width, 1) + pltpu.roll(near, 2 * width, 1)
            high, low = split(near)
            edge[0:LANES] = high
            edge[LANES:2 * LANES] = high
            edge[2 * LANES:] = low


def y_own(value, cols, main):
    high, low = split(value)
    return dot(jnp.concatenate([high, high, low], axis=1), main[0:3 * cols])


def second(shape, width):
    lane = lax.broadcasted_iota(jnp.int32, shape, 1)
    return (lane < width // 2) | ((lane >= width + width // 2) & (lane < 2 * width))


def thrice(halo, width):
    lane = lax.broadcasted_iota(jnp.int32, halo.shape, 1)
    margin = width // 2
    home = ((lane >= margin) & (lane < width)) | ((lane >= LANES - width) & (lane < LANES - margin))
    return jnp.where(home, halo, jnp.where(
        second(halo.shape, width), pltpu.roll(halo, width, 1), pltpu.roll(halo, 2 * width, 1)))


def packed_halo(halo, margin):
    high = halo.astype(BF).astype(F32)
    return jnp.where(second(halo.shape, 2 * margin), halo - high, high).astype(BF)


def y_halo(halo, margin, cols, main):
    return dot(packed_halo(halo, margin), main[3 * cols:])


def y_filter(value, margin, cols, main):
    high, low = split(value[:, 0:cols])
    return dot(jnp.concatenate([high, high, low, packed_halo(value[:, cols:], margin)], axis=1), main[...])


def y_ends(own, halo, margin, edge):
    lane = lax.broadcasted_iota(jnp.int32, halo.shape, 1)
    ends = jnp.where(lane < margin, own[:, 0:LANES],
                     jnp.where(lane >= LANES - margin, own[:, own.shape[1] - LANES:], halo))
    high, low = split(ends)
    return dot(jnp.concatenate([high, low, high], axis=1), edge[...])


def side_lanes(up, down, q, width):
    lane = lax.broadcasted_iota(jnp.int32, up.shape, 1)
    margin = width // 2
    return jnp.where(lane < LANES // 2, pltpu.roll(up, (LANES + margin - q * width) % LANES, 1),
                     pltpu.roll(down, (2 * LANES - margin - (q + 1) * width) % LANES, 1))


def x_filter(zh, zl, count, weights, put):
    step = weights.shape[0]
    for s in range(0, count, step):
        size = min(step, count - s)
        at = slice(s, s + LANES)
        high = zh[at]
        put(slice(s, s + size), dot(weights[0:size], jnp.concatenate([high, zl[at], high], axis=0)))


def stacked(values):
    return jnp.concatenate(values, axis=0)


def interior_kernel(nx, ny, width, v_hbm, t_hbm, gx_hbm, tx_hbm, ty_hbm,
                    halo, corners, z1h, z1l, zph, zpl, z2h, z2l, sub, ger, gxe, txe, gym, gye, tym,
                    ext, t_ref, gx_ref, tx_ref, ty_ref, text_ref, gxw, txw,
                    pack_d, pack_u, from_d, from_u, t_low, t_high,
                    own_v, own_p, coarse, tested, load_sem, send_sem, recv_sem, ready):
    comps, rows, _ = ext.shape
    taps, cols = t_ref.shape
    margin = width // 2
    pairs, inner, _ = sub.shape
    innermost = ger.shape[1]
    me_x, me_y = lax.axis_index("gx"), lax.axis_index("gy")
    first, last = me_x == 0, me_x == nx - 1
    not_first, not_last = me_x > 0, me_x < nx - 1
    has_up, has_down = me_y < ny - 1, me_y > 0
    vertical = jnp.where(has_up, 1, 0) + jnp.where(has_down, 1, 0)
    sides = ((1, has_up), (-1, has_down))
    columns = ((0, None), (1, has_up), (-1, has_down))

    def device(dx, dy):
        return {"gx": lax.rem(me_x + dx + nx, nx), "gy": lax.rem(me_y + dy + ny, ny)}

    def signal(sem, dx, dy):
        pl.semaphore_signal(sem, inc=1, device_id=device(dx, dy), device_id_type=MESH)

    def column(condition, act):
        for dy, present in columns:
            pl.when(condition if present is None else condition & present)(lambda dy=dy: act(dy))

    barrier = pltpu.get_barrier_semaphore()
    pl.when(has_up)(lambda: signal(barrier, 0, 1))
    column(not_last, lambda dy: signal(barrier, 1, dy))
    column(first, lambda dy: signal(barrier, -1, dy))

    own = slice(0, cols)
    order = [(i, j) for i in range(comps) for j in range(i, comps)]
    loads = [pltpu.make_async_copy(src, dst, load_sem.at[i]) for i, (src, dst) in enumerate(
        [(v_hbm.at[0], ext.at[0, :, own]), (t_hbm, t_ref)]
        + [(v_hbm.at[c], ext.at[c, :, own]) for c in range(1, comps)]
        + [(gx_hbm, gx_ref), (tx_hbm, tx_ref), (ty_hbm, ty_ref)])]
    for load in loads:
        load.start()

    per = LANES // width
    groups = rows // width
    head, tail = pl.ds(0, SUB), pl.ds((groups - 1) * SUB, SUB)
    low_x, high_x = v_hbm.at[:, pl.ds(0, width), :], v_hbm.at[:, pl.ds(rows - width, width), :]
    copies = {}

    def remote(key, src, dst, dx, dy):
        n = len(copies)
        copies[key] = pltpu.make_async_remote_copy(
            src_ref=src, dst_ref=dst, send_sem=send_sem.at[n], recv_sem=recv_sem.at[n],
            device_id=device(dx, dy), device_id_type=MESH)

    remote((1, 0), high_x, halo.at[0], 1, 0)
    remote((-1, 0), low_x, halo.at[1], -1, 0)
    remote((1, 1), pack_u.at[:, tail, :], corners.at[0], 1, 1)
    remote((-1, 1), pack_u.at[:, head, :], corners.at[1], -1, 1)
    remote((1, -1), pack_d.at[:, tail, :], corners.at[2], 1, -1)
    remote((-1, -1), pack_d.at[:, head, :], corners.at[3], -1, -1)
    remote(("t", 1), t_ref.at[:, pl.ds(cols - LANES, LANES)], t_low, 0, 1)
    remote(("t", -1), t_ref.at[:, pl.ds(0, LANES)], t_high, 0, -1)
    for c in range(comps):
        remote((c, "v", 1), pack_u.at[c], from_d.at[c], 0, 1)
        remote((c, "v", -1), pack_d.at[c], from_u.at[c], 0, -1)

    @pl.when(last)
    def _():
        pl.semaphore_wait(barrier, jnp.where(has_down, 1, 0) + jnp.where(first, 0, 1 + vertical) + 1 + vertical)
        copies[1, 0].start()

    column(last, lambda dy: signal(ready.at[1 - dy], 1, dy))

    @pl.when(not_last & (not_first | has_down))
    def _():
        pl.semaphore_wait(barrier, jnp.where(has_down, 1, 0) + jnp.where(first, 0, 1 + vertical))

    pl.when(not_first)(lambda: copies[-1, 0].start())
    pl.when(has_down)(lambda: signal(ready.at[3], 0, -1))
    column(not_first, lambda dy: signal(ready.at[5 - dy], -1, dy))

    def pack(c):
        for g in range(groups):
            for q in range(per):
                src = pl.ds(g * width + q * SUB, SUB)
                dst = pl.ds(g * SUB, SUB)
                pack_u[c, dst, q * width:(q + 1) * width] = ext[c, src, cols - width:cols]
                pack_d[c, dst, q * width:(q + 1) * width] = ext[c, src, 0:width]

    for c in range(comps):
        loads[c + (c > 0)].wait()
        pack(c)
        if c == 0:
            loads[1].wait()
            pl.when(has_down)(lambda: copies["t", -1].start())
        else:
            pl.when(has_down)(lambda c=c: copies[c - 1, "v", -1].start())

    text_ref[...] = jnp.zeros_like(text_ref)
    for z, full in ((z1h, rows), (z1l, rows), (zph, rows), (zpl, rows), (z2h, inner), (z2l, inner)):
        if z.shape[1] > full:
            z[:, full:, :] = jnp.zeros((z.shape[0], z.shape[1] - full, z.shape[2]), BF)
    for sign, present, mid in ((1, has_up, from_u), (-1, has_down, from_d)):
        @pl.when(jnp.logical_not(present))
        def _(sign=sign, mid=mid):
            mid[...] = jnp.zeros_like(mid)
            for side in range(2):
                corners[side + (2 if sign > 0 else 0)] = jnp.zeros(corners.shape[1:], F32)

    pl.when(has_down)(lambda: copies[comps - 1, "v", -1].start())

    @pl.when(has_up)
    def _():
        pl.semaphore_wait(ready.at[3], 1)
        copies["t", 1].start()
        for c in range(comps):
            copies[c, "v", 1].start()

    for dy, present in sides:
        pl.when(last & present)(lambda dy=dy: copies[1, dy].start())
        pl.when(not_first & present)(lambda dy=dy: copies[-1, dy].start())

    for load in loads[comps + 1:]:
        load.wait()
    text_ref[0:taps, 0:cols] = t_ref[...]
    first_row, total = me_y * cols, cols * ny
    own_tiles = range(cols // LANES)
    y_weights(t_ref[...], taps, first_row, total, cols, gym, tiles=own_tiles)

    def own_pair(p):
        i, j = order[p]
        own_p[p] = y_own(ext[i, :, own] * ext[j, :, own], cols, gym)

    def forward(dx, dy):
        pl.semaphore_wait(ready.at[(5 if dx > 0 else 1) + dy], 1)
        copies[dx, dy].start()

    for c in range(comps):
        own_v[c] = y_own(ext[c, :, own], cols, gym)
    for p in range(0):
        own_pair(p)
    pl.when(not_last)(lambda: forward(1, 0))
    x_weights(gx_ref, gxw.shape[0], gxw, gxe)
    x_weights(tx_ref, txw.shape[0], txw, txe)
    y_weights(ty_ref[...], taps, first_row, total, cols, tym, tiles=own_tiles)
    for p in range(0, pairs):
        own_pair(p)
    for dy, present in sides:
        pl.when(not_last & present)(lambda dy=dy: forward(1, dy))

    for sign, present, tile, at in ((1, has_down, t_low, LANES - margin), (-1, has_up, t_high, 0)):
        @pl.when(present)
        def _(sign=sign, tile=tile, at=at):
            copies["t", sign].wait_recv()
            text_ref[0:taps, cols + at:cols + at + margin] = tile[:, at:at + margin]

    y_weights(text_ref[...], taps, first_row, total, cols, gym, gye, tiles=(cols // LANES,))

    def store(high, low, index, lanes, z):
        high[index, 0:z.shape[0], lanes], low[index, 0:z.shape[0], lanes] = split(z)

    def y_grid(c):
        blocks = []
        for g in range(groups):
            at = pl.ds(g * SUB, SUB)
            up, down = from_u[c, at, :], from_d[c, at, :]
            blocks += [side_lanes(up, down, q, width) for q in range(per)]
        halo = stacked(blocks)
        spread_halo = thrice(halo, width)
        ext[c, :, cols:] = spread_halo
        store(z1h, z1l, c, own, own_v[c] + y_halo(spread_halo, margin, cols, gym))
        store(z1h, z1l, c, slice(cols, cols + LANES), y_ends(ext[c, :, own], halo, margin, gye))

    def x_grid(c):
        def put(at, value):
            coarse[c, at, :] = value

        x_filter(z1h.at[c], z1l.at[c], inner, gxw, put)

    def y_pair(p):
        i, j = order[p]
        store(zph, zpl, p, own, own_p[p] + y_halo(ext[i, :, cols:] * ext[j, :, cols:], margin, cols, gym))

    def y_test(c):
        store(z2h, z2l, c, own, y_filter(coarse[c], margin, cols, tym))

    def x_test(c):
        def put(at, value):
            tested[c, at, :] = value

        x_filter(z2h.at[c], z2l.at[c], innermost, txw, put)

    def y_resolved(p):
        i, j = order[p]
        store(z2h, z2l, comps + p, own, y_filter(coarse[i] * coarse[j], margin, cols, tym))

    def x_sub(p):
        i, j = order[p]

        def put(at, value):
            sub[p, at, :] = value - coarse[i, at, own] * coarse[j, at, own]

        x_filter(zph.at[p], zpl.at[p], inner, gxw, put)

    def x_ger(p):
        i, j = order[p]

        def put(at, value):
            ger[p, at, :] = value - tested[i, at, :] * tested[j, at, :]

        x_filter(z2h.at[comps + p], z2l.at[comps + p], innermost, txw, put)

    def arrive(c):
        for sign, present in ((1, has_down), (-1, has_up)):
            pl.when(present)(lambda sign=sign: copies[c, "v", sign].wait_recv())

    for c in range(comps):
        if c < 2:
            arrive(c)
        if c == 1:
            for n in range(2, comps):
                arrive(n)
        y_grid(c)
        for p, (i, j) in enumerate(order):
            if j == c:
                y_pair(p)
        if c > 0:
            x_grid(c - 1)
    x_grid(comps - 1)
    for c in range(comps):
        if c == 1:
            column(first, lambda dy: forward(-1, dy))
        y_test(c)
        x_sub(c)
    for c in range(comps):
        y_resolved(c)
        x_test(c)

    for p in range(comps, pairs):
        y_resolved(p)
        x_sub(p)
        x_ger(p - comps)
    for p in range(pairs - comps, pairs):
        x_ger(p)

    copies[1, 0].wait_recv()
    copies[-1, 0].wait_recv()
    for sign, present in ((1, has_down), (-1, has_up)):
        @pl.when(present)
        def _(sign=sign):
            copies[1, sign].wait_recv()
            copies[-1, sign].wait_recv()

    copies[1, 0].wait_send()
    copies[-1, 0].wait_send()
    for sign, present in sides:
        @pl.when(present)
        def _(sign=sign):
            copies[1, sign].wait_send()
            copies[-1, sign].wait_send()
            copies["t", sign].wait_send()
            for c in range(comps):
                copies[c, "v", sign].wait_send()


def edge_kernel(margin, halo, corners, z1h, z1l, zph, zpl, z2h, z2l, sub_in, ger_in,
                gxe, txe, gym, gye, tym, sub_ref, ger_ref, sub_e, ger_e, sems):
    comps, cols = halo.shape[1], halo.shape[3]
    pairs, rows, _ = sub_ref.shape
    width = 2 * margin
    inner, innermost = sub_in.shape[1], ger_in.shape[1]
    order = [(i, j) for i in range(comps) for j in range(i, comps)]
    outs = []

    def leave(source, target):
        copy = pltpu.make_async_copy(source, target, sems.at[len(outs)])
        copy.start()
        outs.append(copy)

    for p in range(pairs):
        leave(sub_in.at[p], sub_ref.at[p, pl.ds(margin, inner), :])
        leave(ger_in.at[p], ger_ref.at[p, pl.ds(width, innermost), :])

    def ends(side, c):
        up, down = corners[2 + side, c], corners[side, c]
        return halo[side, c], stacked([side_lanes(up, down, q, width) for q in range(width // SUB)])

    def pieces(z, size, count):
        high, low = split(z)
        return [(high[n * size:(n + 1) * size], low[n * size:(n + 1) * size]) for n in range(count)]

    def x_ends(side, late, high, low, n, count, size, weights):
        at = slice(0, size) if side == 0 else slice(count - size, count)
        h = (late[0], high[n, at]) if side == 0 else (high[n, at], late[0])
        l = (late[1], low[n, at]) if side == 0 else (low[n, at], late[1])
        r = dot(weights, stacked(h + l))
        half = weights.shape[0] // 2
        return r[0:half] + r[half:]

    near = (slice(width - margin, width), slice(0, margin))
    everywhere = range(pairs)

    def grid(side):
        parts = [ends(side, c) for c in range(comps)]
        rows_own, rows_halo = stacked([part[0] for part in parts]), stacked([part[1] for part in parts])
        values = jnp.concatenate([rows_own, thrice(rows_halo, width)], axis=1)
        ext = [values[c * width:(c + 1) * width] for c in range(comps)]
        products = stacked([ext[i][near[side]] * ext[j][near[side]] for i, j in order])
        z = y_filter(stacked([values, products]), margin, cols, gym)
        count = comps * width
        late = pieces(jnp.concatenate([z[0:count], y_ends(rows_own, rows_halo, margin, gye)], axis=1), width, comps)
        return late, pieces(z[count:], margin, pairs)

    def coarsen(side, late):
        return [x_ends(side, part, z1h, z1l, c, rows, width, gxe[...]) for c, part in enumerate(late)]

    def stress(side, coarse, late):
        weights = stacked([gxe[0:margin], gxe[width:width + margin]] if side == 0 else
                          [gxe[width - margin:width], gxe[2 * width - margin:]])
        for p, part in enumerate(late):
            value = x_ends(side, part, zph, zpl, p, rows, width + margin, weights)
            i, j = order[p]
            sub_e[p, side] = value - coarse[i][near[side], 0:cols] * coarse[j][near[side], 0:cols]

    def test(side, coarse):
        z = y_filter(stacked(coarse + [coarse[i] * coarse[j] for i, j in order]), margin, cols, tym)
        return pieces(z, width, comps + pairs)

    def resolve(side, late):
        tested = [x_ends(side, part, z2h, z2l, c, inner, width, txe[...]) for c, part in enumerate(late[0:comps])]
        for p, part in enumerate(late[comps:]):
            i, j = order[p]
            ger_e[p, side] = (x_ends(side, part, z2h, z2l, comps + p, inner, width, txe[...])
                              - tested[i] * tested[j])

    late = [grid(side) for side in range(2)]
    coarse = [coarsen(side, late[side][0]) for side in range(2)]
    tests = []
    for side in range(2):
        tests.append(test(side, coarse[side]))
        stress(side, coarse[side], late[side][1])
    leave(sub_e.at[:, 0], sub_ref.at[:, pl.ds(0, margin), :])
    leave(sub_e.at[:, 1], sub_ref.at[:, pl.ds(rows - margin, margin), :])
    resolve(0, tests[0])
    leave(ger_e.at[:, 0], ger_ref.at[:, pl.ds(0, width), :])
    resolve(1, tests[1])
    leave(ger_e.at[:, 1], ger_ref.at[:, pl.ds(rows - width, width), :])
    for copy in outs:
        copy.wait()


def local(nx, ny, velocity, grid_x, grid_y, test_x, test_y):
    comps, planes, cols, rows = velocity.shape
    taps = grid_x.shape[0]
    margin = (taps - 1) // 2
    width = 2 * margin
    wide = cols + LANES
    step = LANES - width
    pairs = comps * (comps + 1) // 2
    vmem = pl.BlockSpec(memory_space=pltpu.VMEM)
    anywhere = pl.BlockSpec(memory_space=pl.ANY)
    packed = rows // width * SUB
    inner, innermost = rows - width, rows - 2 * width

    def filled(count):
        return round_up(count, step) + width

    fields = comps + pairs
    subs, gers = [], []
    shape = jax.ShapeDtypeStruct
    for plane in range(planes):
        v = jnp.swapaxes(velocity[:, plane], 1, 2)
        parts = pl.pallas_call(
            functools.partial(interior_kernel, nx, ny, width),
            out_shape=(
                shape((2, comps, width, cols), F32),
                shape((4, comps, SUB, LANES), F32),
                shape((comps, max(rows, filled(inner)), wide), BF),
                shape((comps, max(rows, filled(inner)), wide), BF),
                shape((pairs, max(rows, filled(inner)), cols), BF),
                shape((pairs, max(rows, filled(inner)), cols), BF),
                shape((fields, max(inner, filled(innermost)), cols), BF),
                shape((fields, max(inner, filled(innermost)), cols), BF),
                shape((pairs, inner, cols), F32),
                shape((pairs, innermost, cols), F32),
                shape((2 * width, LANES), BF),
                shape((2 * width, LANES), BF),
                shape((3 * cols + LANES, cols), BF),
                shape((3 * LANES, LANES), BF),
                shape((3 * cols + LANES, cols), BF),
            ),
            in_specs=[pl.BlockSpec(memory_space=pltpu.HBM)] * 5,
            out_specs=(vmem,) * 15,
            scratch_shapes=[
                pltpu.VMEM((comps, rows, wide), F32),
                pltpu.VMEM((taps, cols), F32),
                pltpu.VMEM((1, taps), F32),
                pltpu.VMEM((1, taps), F32),
                pltpu.VMEM((taps, cols), F32),
                pltpu.VMEM((round_up(taps, SUB), wide), F32),
                pltpu.VMEM((step, 3 * LANES), BF),
                pltpu.VMEM((step, 3 * LANES), BF),
                pltpu.VMEM((comps, packed, LANES), F32),
                pltpu.VMEM((comps, packed, LANES), F32),
                pltpu.VMEM((comps, packed, LANES), F32),
                pltpu.VMEM((comps, packed, LANES), F32),
                pltpu.VMEM((taps, LANES), F32),
                pltpu.VMEM((taps, LANES), F32),
                pltpu.VMEM((comps, rows, cols), F32),
                pltpu.VMEM((pairs, rows, cols), F32),
                pltpu.VMEM((comps, inner, wide), F32),
                pltpu.VMEM((comps, innermost, cols), F32),
                pltpu.SemaphoreType.DMA((4 + comps,)),
                pltpu.SemaphoreType.DMA((8 + 2 * comps,)),
                pltpu.SemaphoreType.DMA((8 + 2 * comps,)),
                pltpu.SemaphoreType.REGULAR((7,)),
            ],
            compiler_params=pltpu.CompilerParams(
                collective_id=plane, has_side_effects=True, vmem_limit_bytes=20 << 20),
            name="interior",
        )(*[pltpu.with_memory_space_constraint(x, pltpu.HBM) for x in (
            v, grid_y.T, grid_x.reshape(1, taps), test_x.reshape(1, taps), test_y.T)])
        out = shape((pairs, rows, cols), F32)
        sub, ger = pl.pallas_call(
            functools.partial(edge_kernel, margin),
            out_shape=(out, out),
            in_specs=[vmem] * 15,
            out_specs=(anywhere, anywhere),
            scratch_shapes=[
                pltpu.VMEM((pairs, 2, margin, cols), F32),
                pltpu.VMEM((pairs, 2, width, cols), F32),
                pltpu.SemaphoreType.DMA((2 * pairs + 4,)),
            ],
            compiler_params=pltpu.CompilerParams(
                vmem_limit_bytes=8 << 20),
            name="edge",
        )(*parts)
        subs.append(jnp.swapaxes(sub, 1, 2))
        gers.append(jnp.swapaxes(ger, 1, 2))
    return jnp.stack(subs, axis=1), jnp.stack(gers, axis=1)


def solution(mesh):
    nx, ny = mesh.shape["gx"], mesh.shape["gy"]
    field = P(None, None, "gy", "gx")
    return jax.shard_map(
        functools.partial(local, nx, ny),
        mesh=mesh,
        in_specs=(field, P(), P("gy", None), P(), P("gy", None)),
        out_specs=(field, field),
        check_vma=False,
    )
```

```python
import functools

import jax
import jax.numpy as jnp
from jax import lax
from jax.experimental import pallas as pl
from jax.experimental.pallas import tpu as pltpu
from jax.sharding import PartitionSpec as P

MESH = pl.DeviceIdType.MESH
LANES = 128
SUB = 8
BF = jnp.bfloat16
F32 = jnp.float32


def round_up(value, unit):
    return (value + unit - 1) // unit * unit


def split(value):
    high = value.astype(BF)
    return high, (value - high.astype(F32)).astype(BF)


def dot(a, b):
    return jnp.dot(a, b, preferred_element_type=F32)


def x_weights(w_ref, step, out, edge):
    taps = w_ref.shape[1]
    w = jnp.concatenate([w_ref[...], jnp.zeros((1, LANES - taps), F32)], axis=1)
    w = w / jnp.sum(w)
    band = pltpu.roll(jnp.broadcast_to(w, (LANES, LANES)), 0, 1, stride=1, stride_axis=0)
    high, low = split(band[0:step])
    out[0:step, 0:LANES] = high
    out[0:step, LANES:] = high
    out[step:, 0:LANES] = low
    out[step:, LANES:] = jnp.zeros((step, LANES), BF)
    width = edge.shape[0] // 2
    high, low = split(band[0:width])
    high = high.astype(F32)
    edge[0:width] = (high + pltpu.roll(high, 2 * width, 1)).astype(BF)
    edge[width:] = low


def spread(value, margin):
    lane = lax.broadcasted_iota(jnp.int32, value.shape, 1)
    near = jnp.where((lane < margin) | (lane >= LANES - margin), value, 0.0)
    return pltpu.roll(jnp.where(lane < LANES // 2, near, 0.0), margin, 1) + pltpu.roll(
        jnp.where(lane < LANES // 2, 0.0, near), LANES - margin, 1)


def y_weights(table, taps, first_row, total, cols, main, edge=None, tiles=None):
    margin = (taps - 1) // 2
    width = 2 * margin
    lanes = table.shape[1]
    wide = cols + LANES
    k = lax.broadcasted_iota(jnp.int32, (LANES, lanes), 0)
    lane = lax.broadcasted_iota(jnp.int32, (LANES, lanes), 1)
    y = first_row + jnp.where(lane < cols + LANES // 2, lane, lane - wide)
    source = y + k - margin
    keep = (k < taps) & (source >= 0) & (source < total) & (y >= 0) & (y < total)
    w = jnp.where(keep, jnp.concatenate(
        [table, jnp.zeros((LANES - table.shape[0], lanes), F32)], axis=0), 0.0)
    s = jnp.sum(w, axis=0, keepdims=True)
    w = (w / jnp.where(s > 0.0, s, 1.0)).T
    zeros = jnp.zeros((LANES, cols), F32)
    for t in (range(lanes // LANES) if tiles is None else tiles):
        at = slice(t * LANES, (t + 1) * LANES)
        tile = jnp.concatenate([w[at], zeros], axis=1)
        band = pltpu.roll(tile, (t * LANES - margin) % wide, 1, stride=1, stride_axis=0)
        if t * LANES < cols:
            own, halo = band[:, 0:cols].T, band[:, cols:]
            own_high, own_low = split(own)
            main[0:cols, at] = own_high
            main[cols:2 * cols, at] = own_low
            main[2 * cols:3 * cols, at] = own_high
            halo = spread(halo, margin)
            high = halo.astype(BF).astype(F32)
            packed = high + pltpu.roll(high, width, 1) + pltpu.roll(halo - high, 2 * width, 1)
            main[3 * cols:, at] = packed.T.astype(BF)
        else:
            low_own, high_own, halo = band[:, 0:LANES].T, band[:, cols - LANES:cols].T, band[:, cols:].T
            near = jnp.concatenate([
                low_own[0:margin], halo[0:width], jnp.zeros((LANES - 2 * margin - 2 * width, LANES), F32),
                halo[LANES - width:], high_own[LANES - margin:]], axis=0)
            near = spread(near, margin)
            near = near + pltpu.roll(near, width, 1) + pltpu.roll(near, 2 * width, 1)
            high, low = split(near)
            edge[0:LANES] = high
            edge[LANES:2 * LANES] = high
            edge[2 * LANES:] = low


def y_own(value, cols, main):
    high, low = split(value)
    return dot(jnp.concatenate([high, high, low], axis=1), main[0:3 * cols])


def second(shape, width):
    lane = lax.broadcasted_iota(jnp.int32, shape, 1)
    return (lane < width // 2) | ((lane >= width + width // 2) & (lane < 2 * width))


def thrice(halo, width):
    lane = lax.broadcasted_iota(jnp.int32, halo.shape, 1)
    margin = width // 2
    home = ((lane >= margin) & (lane < width)) | ((lane >= LANES - width) & (lane < LANES - margin))
    return jnp.where(home, halo, jnp.where(
        second(halo.shape, width), pltpu.roll(halo, width, 1), pltpu.roll(halo, 2 * width, 1)))


def packed_halo(halo, margin):
    high = halo.astype(BF).astype(F32)
    return jnp.where(second(halo.shape, 2 * margin), halo - high, high).astype(BF)


def y_halo(halo, margin, cols, main):
    return dot(packed_halo(halo, margin), main[3 * cols:])


def y_filter(value, margin, cols, main):
    high, low = split(value[:, 0:cols])
    return dot(jnp.concatenate([high, high, low, packed_halo(value[:, cols:], margin)], axis=1), main[...])


def y_ends(own, halo, margin, edge):
    lane = lax.broadcasted_iota(jnp.int32, halo.shape, 1)
    ends = jnp.where(lane < margin, own[:, 0:LANES],
                     jnp.where(lane >= LANES - margin, own[:, own.shape[1] - LANES:], halo))
    high, low = split(ends)
    return dot(jnp.concatenate([high, low, high], axis=1), edge[...])


def side_lanes(up, down, q, width):
    lane = lax.broadcasted_iota(jnp.int32, up.shape, 1)
    margin = width // 2
    return jnp.where(lane < LANES // 2, pltpu.roll(up, (LANES + margin - q * width) % LANES, 1),
                     pltpu.roll(down, (2 * LANES - margin - (q + 1) * width) % LANES, 1))


def x_filter(zh, zl, count, weights, put):
    step = weights.shape[0] // 2
    for s in range(0, count, step):
        size = min(step, count - s)
        at = slice(s, s + LANES)
        w = weights[...] if size == step else stacked([weights[0:size], weights[step:step + size]])
        r = dot(w, jnp.concatenate([zh[at], zl[at]], axis=0))
        put(slice(s, s + size), r[0:size] + r[size:])


def stacked(values):
    return jnp.concatenate(values, axis=0)


def interior_kernel(nx, ny, width, v_hbm, t_hbm, gx_hbm, tx_hbm, ty_hbm,
                    halo, corners, z1h, z1l, zph, zpl, z2h, z2l, sub, ger, gxe, txe, gym, gye, tym,
                    ext, t_ref, gx_ref, tx_ref, ty_ref, text_ref, gxw, txw,
                    pack_d, pack_u, from_d, from_u, t_low, t_high,
                    own_v, own_p, coarse, tested, tail_v, corner_u, corner_d, load_sem, send_sem, recv_sem, ready):
    comps, rows, _ = ext.shape
    taps, cols = t_ref.shape
    margin = width // 2
    pairs, inner, _ = sub.shape
    innermost = ger.shape[1]
    me_x, me_y = lax.axis_index("gx"), lax.axis_index("gy")
    first, last = me_x == 0, me_x == nx - 1
    not_first, not_last = me_x > 0, me_x < nx - 1
    has_up, has_down = me_y < ny - 1, me_y > 0
    vertical = jnp.where(has_up, 1, 0) + jnp.where(has_down, 1, 0)
    sides = ((1, has_up), (-1, has_down))
    columns = ((0, None), (1, has_up), (-1, has_down))

    def device(dx, dy):
        return {"gx": lax.rem(me_x + dx + nx, nx), "gy": lax.rem(me_y + dy + ny, ny)}

    def signal(sem, dx, dy):
        pl.semaphore_signal(sem, inc=1, device_id=device(dx, dy), device_id_type=MESH)

    def column(condition, act):
        for dy, present in columns:
            pl.when(condition if present is None else condition & present)(lambda dy=dy: act(dy))

    barrier = pltpu.get_barrier_semaphore()
    pl.when(has_up)(lambda: signal(barrier, 0, 1))
    column(not_last, lambda dy: signal(barrier, 1, dy))
    column(first, lambda dy: signal(barrier, -1, dy))

    own = slice(0, cols)
    order = [(i, j) for i in range(comps) for j in range(i, comps)]
    loads = [pltpu.make_async_copy(src, dst, load_sem.at[i]) for i, (src, dst) in enumerate(
        [(v_hbm.at[0], ext.at[0, :, own]), (t_hbm, t_ref)]
        + [(v_hbm.at[c], ext.at[c, :, own]) for c in range(1, comps)]
        + [(gx_hbm, gx_ref), (tx_hbm, tx_ref), (ty_hbm, ty_ref)])]
    ahead = pltpu.make_async_copy(v_hbm.at[:, pl.ds(rows - width, width), :], tail_v, load_sem.at[4 + comps])
    pl.when(last)(lambda: ahead.start())
    for load in loads:
        load.start()

    per = LANES // width
    groups = rows // width
    head, tail = pl.ds(0, SUB), pl.ds((groups - 1) * SUB, SUB)
    low_x, high_x = v_hbm.at[:, pl.ds(0, width), :], v_hbm.at[:, pl.ds(rows - width, width), :]
    copies = {}

    def remote(key, src, dst, dx, dy):
        n = len(copies)
        copies[key] = pltpu.make_async_remote_copy(
            src_ref=src, dst_ref=dst, send_sem=send_sem.at[n], recv_sem=recv_sem.at[n],
            device_id=device(dx, dy), device_id_type=MESH)

    remote((1, 0), high_x, halo.at[0], 1, 0)
    remote((-1, 0), low_x, halo.at[1], -1, 0)
    remote((1, 1), pack_u.at[:, tail, :], corners.at[0], 1, 1)
    remote((-1, 1), pack_u.at[:, head, :], corners.at[1], -1, 1)
    remote((1, -1), pack_d.at[:, tail, :], corners.at[2], 1, -1)
    remote((-1, -1), pack_d.at[:, head, :], corners.at[3], -1, -1)
    remote(("t", 1), t_ref.at[:, pl.ds(cols - LANES, LANES)], t_low, 0, 1)
    remote(("t", -1), t_ref.at[:, pl.ds(0, LANES)], t_high, 0, -1)
    for c in range(comps):
        remote((c, "v", 1), pack_u.at[c], from_d.at[c], 0, 1)
        remote((c, "v", -1), pack_d.at[c], from_u.at[c], 0, -1)

    @pl.when(last)
    def _():
        pl.semaphore_wait(barrier, jnp.where(has_down, 1, 0) + jnp.where(first, 0, 1 + vertical) + 1 + vertical)
        copies[1, 0].start()

    column(last, lambda dy: signal(ready.at[1 - dy], 1, dy))

    @pl.when(last)
    def _():
        ahead.wait()
        for c in range(comps):
            for q in range(per):
                at = slice(q * SUB, (q + 1) * SUB)
                corner_u[c, :, q * width:(q + 1) * width] = tail_v[c, at, cols - width:cols]
                corner_d[c, :, q * width:(q + 1) * width] = tail_v[c, at, 0:width]

    @pl.when(not_last & (not_first | has_down))
    def _():
        pl.semaphore_wait(barrier, jnp.where(has_down, 1, 0) + jnp.where(first, 0, 1 + vertical))

    pl.when(not_first)(lambda: copies[-1, 0].start())
    pl.when(has_down)(lambda: signal(ready.at[3], 0, -1))
    column(not_first, lambda dy: signal(ready.at[5 - dy], -1, dy))

    for n, dy, src, present in ((2, 1, corner_u, has_up), (4, -1, corner_d, has_down)):
        wrapped = pltpu.make_async_remote_copy(
            src_ref=src, dst_ref=corners.at[n - 2], send_sem=send_sem.at[n],
            recv_sem=recv_sem.at[n], device_id=device(1, dy), device_id_type=MESH)
        pl.when(last & present)(lambda wrapped=wrapped: wrapped.start())

    def pack(c):
        for g in range(groups):
            for q in range(per):
                src = pl.ds(g * width + q * SUB, SUB)
                dst = pl.ds(g * SUB, SUB)
                pack_u[c, dst, q * width:(q + 1) * width] = ext[c, src, cols - width:cols]
                pack_d[c, dst, q * width:(q + 1) * width] = ext[c, src, 0:width]

    for c in range(comps):
        loads[c + (c > 0)].wait()
        pack(c)
        if c == 0:
            loads[1].wait()
            pl.when(has_down)(lambda: copies["t", -1].start())
        else:
            pl.when(has_down)(lambda c=c: copies[c - 1, "v", -1].start())

    text_ref[...] = jnp.zeros_like(text_ref)
    for z, full in ((z1h, rows), (z1l, rows), (zph, rows), (zpl, rows), (z2h, inner), (z2l, inner)):
        if z.shape[1] > full:
            z[:, full:, :] = jnp.zeros((z.shape[0], z.shape[1] - full, z.shape[2]), BF)
    for sign, present, mid in ((1, has_up, from_u), (-1, has_down, from_d)):
        @pl.when(jnp.logical_not(present))
        def _(sign=sign, mid=mid):
            mid[...] = jnp.zeros_like(mid)
            for side in range(2):
                corners[side + (2 if sign > 0 else 0)] = jnp.zeros(corners.shape[1:], F32)

    pl.when(has_down)(lambda: copies[comps - 1, "v", -1].start())

    @pl.when(has_up)
    def _():
        pl.semaphore_wait(ready.at[3], 1)
        copies["t", 1].start()
        for c in range(comps):
            copies[c, "v", 1].start()

    for dy, present in sides:
        pl.when(not_first & present)(lambda dy=dy: copies[-1, dy].start())

    for load in loads[comps + 1:]:
        load.wait()
    text_ref[0:taps, 0:cols] = t_ref[...]
    first_row, total = me_y * cols, cols * ny
    own_tiles = range(cols // LANES)
    y_weights(t_ref[...], taps, first_row, total, cols, gym, tiles=own_tiles)

    def own_pair(p):
        i, j = order[p]
        own_p[p] = y_own(ext[i, :, own] * ext[j, :, own], cols, gym)

    held = {}
    for n, dx, at in ((0, 1, rows - width), (1, -1, 0)):
        held[dx, 0] = pltpu.make_async_remote_copy(
            src_ref=ext.at[:, pl.ds(at, width), own], dst_ref=halo.at[n], send_sem=send_sem.at[n],
            recv_sem=recv_sem.at[n], device_id=device(dx, 0), device_id_type=MESH)

    def forward(dx, dy):
        pl.semaphore_wait(ready.at[(5 if dx > 0 else 1) + dy], 1)
        held.get((dx, dy), copies[dx, dy]).start()

    for c in range(comps):
        own_v[c] = y_own(ext[c, :, own], cols, gym)
    for p in range(0):
        own_pair(p)
    pl.when(not_last)(lambda: forward(1, 0))
    x_weights(gx_ref, gxw.shape[0] // 2, gxw, gxe)
    x_weights(tx_ref, txw.shape[0] // 2, txw, txe)
    y_weights(ty_ref[...], taps, first_row, total, cols, tym, tiles=own_tiles)
    for p in range(0, pairs):
        own_pair(p)
    for dy, present in sides:
        pl.when(not_last & present)(lambda dy=dy: forward(1, dy))

    for sign, present, tile, at in ((1, has_down, t_low, LANES - margin), (-1, has_up, t_high, 0)):
        @pl.when(present)
        def _(sign=sign, tile=tile, at=at):
            copies["t", sign].wait_recv()
            text_ref[0:taps, cols + at:cols + at + margin] = tile[:, at:at + margin]

    y_weights(text_ref[...], taps, first_row, total, cols, gym, gye, tiles=(cols // LANES,))

    def store(high, low, index, lanes, z):
        high[index, 0:z.shape[0], lanes], low[index, 0:z.shape[0], lanes] = split(z)

    def y_grid(c):
        blocks = []
        for g in range(groups):
            at = pl.ds(g * SUB, SUB)
            up, down = from_u[c, at, :], from_d[c, at, :]
            blocks += [side_lanes(up, down, q, width) for q in range(per)]
        halo = stacked(blocks)
        spread_halo = thrice(halo, width)
        ext[c, :, cols:] = spread_halo
        store(z1h, z1l, c, own, own_v[c] + y_halo(spread_halo, margin, cols, gym))
        store(z1h, z1l, c, slice(cols, cols + LANES), y_ends(ext[c, :, own], halo, margin, gye))

    def x_grid(c):
        def put(at, value):
            coarse[c, at, :] = value

        x_filter(z1h.at[c], z1l.at[c], inner, gxw, put)

    def y_pair(p):
        i, j = order[p]
        store(zph, zpl, p, own, own_p[p] + y_halo(ext[i, :, cols:] * ext[j, :, cols:], margin, cols, gym))

    def y_test(c):
        store(z2h, z2l, c, own, y_filter(coarse[c], margin, cols, tym))

    def x_test(c):
        def put(at, value):
            tested[c, at, :] = value

        x_filter(z2h.at[c], z2l.at[c], innermost, txw, put)

    def y_resolved(p):
        i, j = order[p]
        store(z2h, z2l, comps + p, own, y_filter(coarse[i] * coarse[j], margin, cols, tym))

    def x_sub(p):
        i, j = order[p]

        def put(at, value):
            sub[p, at, :] = value - coarse[i, at, own] * coarse[j, at, own]

        x_filter(zph.at[p], zpl.at[p], inner, gxw, put)

    def x_ger(p):
        i, j = order[p]

        def put(at, value):
            ger[p, at, :] = value - tested[i, at, :] * tested[j, at, :]

        x_filter(z2h.at[comps + p], z2l.at[comps + p], innermost, txw, put)

    def arrive(c):
        for sign, present in ((1, has_down), (-1, has_up)):
            pl.when(present)(lambda sign=sign: copies[c, "v", sign].wait_recv())

    for c in range(comps):
        if c < 2:
            arrive(c)
        if c == 1:
            for n in range(2, comps):
                arrive(n)
        y_grid(c)
        for p, (i, j) in enumerate(order):
            if j == c:
                y_pair(p)
        if c > 0:
            x_grid(c - 1)
    x_grid(comps - 1)
    for c in range(comps):
        if c == 1:
            column(first, lambda dy: forward(-1, dy))
        y_test(c)
        x_sub(c)
    for c in range(comps):
        y_resolved(c)
        x_test(c)

    for p in range(comps, pairs):
        y_resolved(p)
        x_sub(p)
        x_ger(p - comps)
    for p in range(pairs - comps, pairs):
        x_ger(p)

    copies[1, 0].wait_recv()
    copies[-1, 0].wait_recv()
    for sign, present in ((1, has_down), (-1, has_up)):
        @pl.when(present)
        def _(sign=sign):
            copies[1, sign].wait_recv()
            copies[-1, sign].wait_recv()

    copies[1, 0].wait_send()
    copies[-1, 0].wait_send()
    for sign, present in sides:
        @pl.when(present)
        def _(sign=sign):
            copies[1, sign].wait_send()
            copies[-1, sign].wait_send()
            copies["t", sign].wait_send()
            for c in range(comps):
                copies[c, "v", sign].wait_send()


def edge_kernel(margin, halo, corners, z1h, z1l, zph, zpl, z2h, z2l, sub_in, ger_in,
                gxe, txe, gym, gye, tym, sub_ref, ger_ref, sub_e, ger_e, sems):
    comps, cols = halo.shape[1], halo.shape[3]
    pairs, rows, _ = sub_ref.shape
    width = 2 * margin
    inner, innermost = sub_in.shape[1], ger_in.shape[1]
    order = [(i, j) for i in range(comps) for j in range(i, comps)]
    outs = []

    def leave(source, target):
        copy = pltpu.make_async_copy(source, target, sems.at[len(outs)])
        copy.start()
        outs.append(copy)

    for p in range(pairs):
        leave(sub_in.at[p], sub_ref.at[p, pl.ds(margin, inner), :])
        leave(ger_in.at[p], ger_ref.at[p, pl.ds(width, innermost), :])

    def ends(side, c):
        up, down = corners[2 + side, c], corners[side, c]
        return halo[side, c], stacked([side_lanes(up, down, q, width) for q in range(width // SUB)])

    def pieces(z, size, count):
        high, low = split(z)
        return [(high[n * size:(n + 1) * size], low[n * size:(n + 1) * size]) for n in range(count)]

    def x_ends(side, late, high, low, n, count, size, weights):
        at = slice(0, size) if side == 0 else slice(count - size, count)
        h = (late[0], high[n, at]) if side == 0 else (high[n, at], late[0])
        l = (late[1], low[n, at]) if side == 0 else (low[n, at], late[1])
        r = dot(weights, stacked(h + l))
        half = weights.shape[0] // 2
        return r[0:half] + r[half:]

    near = (slice(width - margin, width), slice(0, margin))
    everywhere = range(pairs)

    def grid(side):
        parts = [ends(side, c) for c in range(comps)]
        rows_own, rows_halo = stacked([part[0] for part in parts]), stacked([part[1] for part in parts])
        values = jnp.concatenate([rows_own, thrice(rows_halo, width)], axis=1)
        ext = [values[c * width:(c + 1) * width] for c in range(comps)]
        products = stacked([ext[i][near[side]] * ext[j][near[side]] for i, j in order])
        z = y_filter(stacked([values, products]), margin, cols, gym)
        count = comps * width
        late = pieces(jnp.concatenate([z[0:count], y_ends(rows_own, rows_halo, margin, gye)], axis=1), width, comps)
        return late, pieces(z[count:], margin, pairs)

    def coarsen(side, late):
        return [x_ends(side, part, z1h, z1l, c, rows, width, gxe[...]) for c, part in enumerate(late)]

    def stress(side, coarse, late):
        weights = stacked([gxe[0:margin], gxe[width:width + margin]] if side == 0 else
                          [gxe[width - margin:width], gxe[2 * width - margin:]])
        for p, part in enumerate(late):
            value = x_ends(side, part, zph, zpl, p, rows, width + margin, weights)
            i, j = order[p]
            sub_e[p, side] = value - coarse[i][near[side], 0:cols] * coarse[j][near[side], 0:cols]

    def test(side, coarse):
        z = y_filter(stacked(coarse + [coarse[i] * coarse[j] for i, j in order]), margin, cols, tym)
        return pieces(z, width, comps + pairs)

    def resolve(side, late):
        tested = [x_ends(side, part, z2h, z2l, c, inner, width, txe[...]) for c, part in enumerate(late[0:comps])]
        for p, part in enumerate(late[comps:]):
            i, j = order[p]
            ger_e[p, side] = (x_ends(side, part, z2h, z2l, comps + p, inner, width, txe[...])
                              - tested[i] * tested[j])

    late = [grid(side) for side in range(2)]
    coarse = [coarsen(side, late[side][0]) for side in range(2)]
    tests = []
    for side in range(2):
        tests.append(test(side, coarse[side]))
        stress(side, coarse[side], late[side][1])
    leave(sub_e.at[:, 0], sub_ref.at[:, pl.ds(0, margin), :])
    leave(sub_e.at[:, 1], sub_ref.at[:, pl.ds(rows - margin, margin), :])
    resolve(0, tests[0])
    leave(ger_e.at[:, 0], ger_ref.at[:, pl.ds(0, width), :])
    resolve(1, tests[1])
    leave(ger_e.at[:, 1], ger_ref.at[:, pl.ds(rows - width, width), :])
    for copy in outs:
        copy.wait()


def local(nx, ny, velocity, grid_x, grid_y, test_x, test_y):
    comps, planes, cols, rows = velocity.shape
    taps = grid_x.shape[0]
    margin = (taps - 1) // 2
    width = 2 * margin
    wide = cols + LANES
    step = LANES - width
    pairs = comps * (comps + 1) // 2
    vmem = pl.BlockSpec(memory_space=pltpu.VMEM)
    anywhere = pl.BlockSpec(memory_space=pl.ANY)
    packed = rows // width * SUB
    inner, innermost = rows - width, rows - 2 * width

    def filled(count):
        return round_up(count, step) + width

    fields = comps + pairs
    subs, gers = [], []
    shape = jax.ShapeDtypeStruct
    for plane in range(planes):
        v = jnp.swapaxes(velocity[:, plane], 1, 2)
        parts = pl.pallas_call(
            functools.partial(interior_kernel, nx, ny, width),
            out_shape=(
                shape((2, comps, width, cols), F32),
                shape((4, comps, SUB, LANES), F32),
                shape((comps, max(rows, filled(inner)), wide), BF),
                shape((comps, max(rows, filled(inner)), wide), BF),
                shape((pairs, max(rows, filled(inner)), cols), BF),
                shape((pairs, max(rows, filled(inner)), cols), BF),
                shape((fields, max(inner, filled(innermost)), cols), BF),
                shape((fields, max(inner, filled(innermost)), cols), BF),
                shape((pairs, inner, cols), F32),
                shape((pairs, innermost, cols), F32),
                shape((2 * width, LANES), BF),
                shape((2 * width, LANES), BF),
                shape((3 * cols + LANES, cols), BF),
                shape((3 * LANES, LANES), BF),
                shape((3 * cols + LANES, cols), BF),
            ),
            in_specs=[pl.BlockSpec(memory_space=pltpu.HBM)] * 5,
            out_specs=(vmem,) * 15,
            scratch_shapes=[
                pltpu.VMEM((comps, rows, wide), F32),
                pltpu.VMEM((taps, cols), F32),
                pltpu.VMEM((1, taps), F32),
                pltpu.VMEM((1, taps), F32),
                pltpu.VMEM((taps, cols), F32),
                pltpu.VMEM((round_up(taps, SUB), wide), F32),
                pltpu.VMEM((2 * step, 2 * LANES), BF),
                pltpu.VMEM((2 * step, 2 * LANES), BF),
                pltpu.VMEM((comps, packed, LANES), F32),
                pltpu.VMEM((comps, packed, LANES), F32),
                pltpu.VMEM((comps, packed, LANES), F32),
                pltpu.VMEM((comps, packed, LANES), F32),
                pltpu.VMEM((taps, LANES), F32),
                pltpu.VMEM((taps, LANES), F32),
                pltpu.VMEM((comps, rows, cols), F32),
                pltpu.VMEM((pairs, rows, cols), F32),
                pltpu.VMEM((comps, inner, wide), F32),
                pltpu.VMEM((comps, innermost, cols), F32),
                pltpu.VMEM((comps, width, cols), F32),
                pltpu.VMEM((comps, SUB, LANES), F32),
                pltpu.VMEM((comps, SUB, LANES), F32),
                pltpu.SemaphoreType.DMA((5 + comps,)),
                pltpu.SemaphoreType.DMA((8 + 2 * comps,)),
                pltpu.SemaphoreType.DMA((8 + 2 * comps,)),
                pltpu.SemaphoreType.REGULAR((7,)),
            ],
            compiler_params=pltpu.CompilerParams(
                collective_id=plane, has_side_effects=True, vmem_limit_bytes=20 << 20),
            name="interior",
        )(*[pltpu.with_memory_space_constraint(x, pltpu.HBM) for x in (
            v, grid_y.T, grid_x.reshape(1, taps), test_x.reshape(1, taps), test_y.T)])
        out = shape((pairs, rows, cols), F32)
        sub, ger = pl.pallas_call(
            functools.partial(edge_kernel, margin),
            out_shape=(out, out),
            in_specs=[vmem] * 15,
            out_specs=(anywhere, anywhere),
            scratch_shapes=[
                pltpu.VMEM((pairs, 2, margin, cols), F32),
                pltpu.VMEM((pairs, 2, width, cols), F32),
                pltpu.SemaphoreType.DMA((2 * pairs + 4,)),
            ],
            compiler_params=pltpu.CompilerParams(
                vmem_limit_bytes=8 << 20),
            name="edge",
        )(*parts)
        subs.append(jnp.swapaxes(sub, 1, 2))
        gers.append(jnp.swapaxes(ger, 1, 2))
    return jnp.stack(subs, axis=1), jnp.stack(gers, axis=1)


def solution(mesh):
    nx, ny = mesh.shape["gx"], mesh.shape["gy"]
    field = P(None, None, "gy", "gx")
    return jax.shard_map(
        functools.partial(local, nx, ny),
        mesh=mesh,
        in_specs=(field, P(), P("gy", None), P(), P("gy", None)),
        out_specs=(field, field),
        check_vma=False,
    )
```

```python
import functools

import jax
import jax.numpy as jnp
from jax import lax
from jax.experimental import pallas as pl
from jax.experimental.pallas import tpu as pltpu
from jax.sharding import PartitionSpec as P

MESH = pl.DeviceIdType.MESH
LANES = 128
SUB = 8
BF = jnp.bfloat16
F32 = jnp.float32


def round_up(value, unit):
    return (value + unit - 1) // unit * unit


def split(value):
    high = value.astype(BF)
    return high, (value - high.astype(F32)).astype(BF)


def dot(a, b):
    return jnp.dot(a, b, preferred_element_type=F32)


def x_weights(w_ref, step, out, edge):
    taps = w_ref.shape[1]
    w = jnp.concatenate([w_ref[...], jnp.zeros((1, LANES - taps), F32)], axis=1)
    w = w / jnp.sum(w)
    band = pltpu.roll(jnp.broadcast_to(w, (LANES, LANES)), 0, 1, stride=1, stride_axis=0)
    high, low = split(band[0:step])
    out[0:step, 0:LANES] = high
    out[0:step, LANES:] = high
    out[step:, 0:LANES] = low
    out[step:, LANES:] = jnp.zeros((step, LANES), BF)
    width = edge.shape[0] // 2
    high, low = split(band[0:width])
    high = high.astype(F32)
    edge[0:width] = (high + pltpu.roll(high, 2 * width, 1)).astype(BF)
    edge[width:] = low


def spread(value, margin):
    lane = lax.broadcasted_iota(jnp.int32, value.shape, 1)
    near = jnp.where((lane < margin) | (lane >= LANES - margin), value, 0.0)
    return pltpu.roll(jnp.where(lane < LANES // 2, near, 0.0), margin, 1) + pltpu.roll(
        jnp.where(lane < LANES // 2, 0.0, near), LANES - margin, 1)


def y_weights(table, taps, first_row, total, cols, main, edge=None, tiles=None):
    margin = (taps - 1) // 2
    width = 2 * margin
    lanes = table.shape[1]
    wide = cols + LANES
    k = lax.broadcasted_iota(jnp.int32, (LANES, lanes), 0)
    lane = lax.broadcasted_iota(jnp.int32, (LANES, lanes), 1)
    y = first_row + jnp.where(lane < cols + LANES // 2, lane, lane - wide)
    source = y + k - margin
    keep = (k < taps) & (source >= 0) & (source < total) & (y >= 0) & (y < total)
    w = jnp.where(keep, jnp.concatenate(
        [table, jnp.zeros((LANES - table.shape[0], lanes), F32)], axis=0), 0.0)
    s = jnp.sum(w, axis=0, keepdims=True)
    w = (w / jnp.where(s > 0.0, s, 1.0)).T
    zeros = jnp.zeros((LANES, cols), F32)
    for t in (range(lanes // LANES) if tiles is None else tiles):
        at = slice(t * LANES, (t + 1) * LANES)
        tile = jnp.concatenate([w[at], zeros], axis=1)
        band = pltpu.roll(tile, (t * LANES - margin) % wide, 1, stride=1, stride_axis=0)
        if t * LANES < cols:
            own, halo = band[:, 0:cols].T, band[:, cols:]
            own_high, own_low = split(own)
            main[0:cols, at] = own_high
            main[cols:2 * cols, at] = own_low
            main[2 * cols:3 * cols, at] = own_high
            halo = spread(halo, margin)
            high = halo.astype(BF).astype(F32)
            packed = high + pltpu.roll(high, width, 1) + pltpu.roll(halo - high, 2 * width, 1)
            main[3 * cols:, at] = packed.T.astype(BF)
        else:
            low_own, high_own, halo = band[:, 0:LANES].T, band[:, cols - LANES:cols].T, band[:, cols:].T
            near = jnp.concatenate([
                low_own[0:margin], halo[0:width], jnp.zeros((LANES - 2 * margin - 2 * width, LANES), F32),
                halo[LANES - width:], high_own[LANES - margin:]], axis=0)
            near = spread(near, margin)
            near = near + pltpu.roll(near, width, 1) + pltpu.roll(near, 2 * width, 1)
            high, low = split(near)
            edge[0:LANES] = high
            edge[LANES:2 * LANES] = high
            edge[2 * LANES:] = low


def y_own(value, cols, main):
    high, low = split(value)
    return dot(jnp.concatenate([high, high, low], axis=1), main[0:3 * cols])


def second(shape, width):
    lane = lax.broadcasted_iota(jnp.int32, shape, 1)
    return (lane < width // 2) | ((lane >= width + width // 2) & (lane < 2 * width))


def thrice(halo, width):
    lane = lax.broadcasted_iota(jnp.int32, halo.shape, 1)
    margin = width // 2
    home = ((lane >= margin) & (lane < width)) | ((lane >= LANES - width) & (lane < LANES - margin))
    return jnp.where(home, halo, jnp.where(
        second(halo.shape, width), pltpu.roll(halo, width, 1), pltpu.roll(halo, 2 * width, 1)))


def packed_halo(halo, margin):
    high = halo.astype(BF).astype(F32)
    return jnp.where(second(halo.shape, 2 * margin), halo - high, high).astype(BF)


def y_halo(halo, margin, cols, main):
    return dot(packed_halo(halo, margin), main[3 * cols:])


def y_filter(value, margin, cols, main):
    high, low = split(value[:, 0:cols])
    return dot(jnp.concatenate([high, high, low, packed_halo(value[:, cols:], margin)], axis=1), main[...])


def y_ends(own, halo, margin, edge):
    lane = lax.broadcasted_iota(jnp.int32, halo.shape, 1)
    ends = jnp.where(lane < margin, own[:, 0:LANES],
                     jnp.where(lane >= LANES - margin, own[:, own.shape[1] - LANES:], halo))
    high, low = split(ends)
    return dot(jnp.concatenate([high, low, high], axis=1), edge[...])


def side_lanes(up, down, q, width):
    lane = lax.broadcasted_iota(jnp.int32, up.shape, 1)
    margin = width // 2
    return jnp.where(lane < LANES // 2, pltpu.roll(up, (LANES + margin - q * width) % LANES, 1),
                     pltpu.roll(down, (2 * LANES - margin - (q + 1) * width) % LANES, 1))


def x_filter(zh, zl, count, weights, put):
    step = weights.shape[0] // 2
    for s in range(0, count, step):
        size = min(step, count - s)
        at = slice(s, s + LANES)
        w = weights[...] if size == step else stacked([weights[0:size], weights[step:step + size]])
        r = dot(w, jnp.concatenate([zh[at], zl[at]], axis=0))
        put(slice(s, s + size), r[0:size] + r[size:])


def stacked(values):
    return jnp.concatenate(values, axis=0)


def interior_kernel(nx, ny, width, v_hbm, t_hbm, gx_hbm, tx_hbm, ty_hbm,
                    halo, corners, z1h, z1l, zph, zpl, z2h, z2l, sub, ger, gxe, txe, gym, gye, tym,
                    ext, t_ref, gx_ref, tx_ref, ty_ref, text_ref, gxw, txw,
                    pack_d, pack_u, from_d, from_u, t_low, t_high,
                    own_v, own_p, coarse, tested, tail_v, corner_u, corner_d, load_sem, send_sem, recv_sem, ready):
    comps, rows, _ = ext.shape
    taps, cols = t_ref.shape
    margin = width // 2
    pairs, inner, _ = sub.shape
    innermost = ger.shape[1]
    me_x, me_y = lax.axis_index("gx"), lax.axis_index("gy")
    first, last = me_x == 0, me_x == nx - 1
    not_first, not_last = me_x > 0, me_x < nx - 1
    has_up, has_down = me_y < ny - 1, me_y > 0
    vertical = jnp.where(has_up, 1, 0) + jnp.where(has_down, 1, 0)
    sides = ((1, has_up), (-1, has_down))
    columns = ((0, None), (1, has_up), (-1, has_down))

    def device(dx, dy):
        return {"gx": lax.rem(me_x + dx + nx, nx), "gy": lax.rem(me_y + dy + ny, ny)}

    def signal(sem, dx, dy):
        pl.semaphore_signal(sem, inc=1, device_id=device(dx, dy), device_id_type=MESH)

    def column(condition, act):
        for dy, present in columns:
            pl.when(condition if present is None else condition & present)(lambda dy=dy: act(dy))

    barrier = pltpu.get_barrier_semaphore()
    pl.when(has_up)(lambda: signal(barrier, 0, 1))
    column(not_last, lambda dy: signal(barrier, 1, dy))
    column(first, lambda dy: signal(barrier, -1, dy))

    own = slice(0, cols)
    order = [(i, j) for i in range(comps) for j in range(i, comps)]
    loads = [pltpu.make_async_copy(src, dst, load_sem.at[i]) for i, (src, dst) in enumerate(
        [(v_hbm.at[0], ext.at[0, :, own]), (t_hbm, t_ref)]
        + [(v_hbm.at[c], ext.at[c, :, own]) for c in range(1, comps)]
        + [(gx_hbm, gx_ref), (tx_hbm, tx_ref), (ty_hbm, ty_ref)])]
    ahead = pltpu.make_async_copy(v_hbm.at[:, pl.ds(rows - width, width), :], tail_v, load_sem.at[4 + comps])
    pl.when(last)(lambda: ahead.start())
    for load in loads:
        load.start()

    per = LANES // width
    groups = rows // width
    head, tail = pl.ds(0, SUB), pl.ds((groups - 1) * SUB, SUB)
    low_x, high_x = v_hbm.at[:, pl.ds(0, width), :], v_hbm.at[:, pl.ds(rows - width, width), :]
    copies = {}

    def remote(key, src, dst, dx, dy):
        n = len(copies)
        copies[key] = pltpu.make_async_remote_copy(
            src_ref=src, dst_ref=dst, send_sem=send_sem.at[n], recv_sem=recv_sem.at[n],
            device_id=device(dx, dy), device_id_type=MESH)

    remote((1, 0), high_x, halo.at[0], 1, 0)
    remote((-1, 0), low_x, halo.at[1], -1, 0)
    remote((1, 1), pack_u.at[:, tail, :], corners.at[0], 1, 1)
    remote((-1, 1), pack_u.at[:, head, :], corners.at[1], -1, 1)
    remote((1, -1), pack_d.at[:, tail, :], corners.at[2], 1, -1)
    remote((-1, -1), pack_d.at[:, head, :], corners.at[3], -1, -1)
    remote(("t", 1), t_ref.at[:, pl.ds(cols - LANES, LANES)], t_low, 0, 1)
    remote(("t", -1), t_ref.at[:, pl.ds(0, LANES)], t_high, 0, -1)
    for c in range(comps):
        remote((c, "v", 1), pack_u.at[c], from_d.at[c], 0, 1)
        remote((c, "v", -1), pack_d.at[c], from_u.at[c], 0, -1)

    @pl.when(last)
    def _():
        pl.semaphore_wait(barrier, jnp.where(has_down, 1, 0) + jnp.where(first, 0, 1 + vertical) + 1 + vertical)
        copies[1, 0].start()

    column(last, lambda dy: signal(ready.at[1 - dy], 1, dy))

    @pl.when(last)
    def _():
        ahead.wait()
        for c in range(comps):
            for q in range(per):
                at = slice(q * SUB, (q + 1) * SUB)
                corner_u[c, :, q * width:(q + 1) * width] = tail_v[c, at, cols - width:cols]
                corner_d[c, :, q * width:(q + 1) * width] = tail_v[c, at, 0:width]

    @pl.when(not_last & (not_first | has_down))
    def _():
        pl.semaphore_wait(barrier, jnp.where(has_down, 1, 0) + jnp.where(first, 0, 1 + vertical))

    pl.when(not_first)(lambda: copies[-1, 0].start())
    pl.when(has_down)(lambda: signal(ready.at[3], 0, -1))
    column(not_first, lambda dy: signal(ready.at[5 - dy], -1, dy))

    for n, dy, src, present in ((2, 1, corner_u, has_up), (4, -1, corner_d, has_down)):
        wrapped = pltpu.make_async_remote_copy(
            src_ref=src, dst_ref=corners.at[n - 2], send_sem=send_sem.at[n],
            recv_sem=recv_sem.at[n], device_id=device(1, dy), device_id_type=MESH)
        pl.when(last & present)(lambda wrapped=wrapped: wrapped.start())

    def pack(c):
        for g in range(groups):
            for q in range(per):
                src = pl.ds(g * width + q * SUB, SUB)
                dst = pl.ds(g * SUB, SUB)
                pack_u[c, dst, q * width:(q + 1) * width] = ext[c, src, cols - width:cols]
                pack_d[c, dst, q * width:(q + 1) * width] = ext[c, src, 0:width]

    for c in range(comps):
        loads[c + (c > 0)].wait()
        pack(c)
        if c == 0:
            loads[1].wait()
            pl.when(has_down)(lambda: copies["t", -1].start())
        else:
            pl.when(has_down)(lambda c=c: copies[c - 1, "v", -1].start())

    text_ref[...] = jnp.zeros_like(text_ref)
    for z, full in ((z1h, rows), (z1l, rows), (zph, rows), (zpl, rows), (z2h, inner), (z2l, inner)):
        if z.shape[1] > full:
            z[:, full:, :] = jnp.zeros((z.shape[0], z.shape[1] - full, z.shape[2]), BF)
    for sign, present, mid in ((1, has_up, from_u), (-1, has_down, from_d)):
        @pl.when(jnp.logical_not(present))
        def _(sign=sign, mid=mid):
            mid[...] = jnp.zeros_like(mid)
            for side in range(2):
                corners[side + (2 if sign > 0 else 0)] = jnp.zeros(corners.shape[1:], F32)

    pl.when(has_down)(lambda: copies[comps - 1, "v", -1].start())

    @pl.when(has_up)
    def _():
        pl.semaphore_wait(ready.at[3], 1)
        copies["t", 1].start()
        for c in range(comps):
            copies[c, "v", 1].start()

    for dy, present in sides:
        pl.when(not_first & present)(lambda dy=dy: copies[-1, dy].start())

    for load in loads[comps + 1:]:
        load.wait()
    text_ref[0:taps, 0:cols] = t_ref[...]
    first_row, total = me_y * cols, cols * ny
    own_tiles = range(cols // LANES)
    y_weights(t_ref[...], taps, first_row, total, cols, gym, tiles=own_tiles)

    def own_pair(p):
        i, j = order[p]
        own_p[p] = y_own(ext[i, :, own] * ext[j, :, own], cols, gym)

    held = {}
    for n, dx, at in ((0, 1, rows - width), (1, -1, 0)):
        held[dx, 0] = pltpu.make_async_remote_copy(
            src_ref=ext.at[:, pl.ds(at, width), own], dst_ref=halo.at[n], send_sem=send_sem.at[n],
            recv_sem=recv_sem.at[n], device_id=device(dx, 0), device_id_type=MESH)

    def forward(dx, dy):
        pl.semaphore_wait(ready.at[(5 if dx > 0 else 1) + dy], 1)
        held.get((dx, dy), copies[dx, dy]).start()

    for c in range(comps):
        own_v[c] = y_own(ext[c, :, own], cols, gym)
    for p in range(0):
        own_pair(p)
    pl.when(not_last)(lambda: forward(1, 0))
    x_weights(gx_ref, gxw.shape[0] // 2, gxw, gxe)
    x_weights(tx_ref, txw.shape[0] // 2, txw, txe)
    y_weights(ty_ref[...], taps, first_row, total, cols, tym, tiles=own_tiles)
    for p in range(0, pairs):
        own_pair(p)
    for dy, present in sides:
        pl.when(not_last & present)(lambda dy=dy: forward(1, dy))

    for sign, present, tile, at in ((1, has_down, t_low, LANES - margin), (-1, has_up, t_high, 0)):
        @pl.when(present)
        def _(sign=sign, tile=tile, at=at):
            copies["t", sign].wait_recv()
            text_ref[0:taps, cols + at:cols + at + margin] = tile[:, at:at + margin]

    y_weights(text_ref[...], taps, first_row, total, cols, gym, gye, tiles=(cols // LANES,))

    def store(high, low, index, lanes, z):
        high[index, 0:z.shape[0], lanes], low[index, 0:z.shape[0], lanes] = split(z)

    def y_grid(c):
        blocks = []
        for g in range(groups):
            at = pl.ds(g * SUB, SUB)
            up, down = from_u[c, at, :], from_d[c, at, :]
            blocks += [side_lanes(up, down, q, width) for q in range(per)]
        halo = stacked(blocks)
        spread_halo = thrice(halo, width)
        ext[c, :, cols:] = spread_halo
        store(z1h, z1l, c, own, own_v[c] + y_halo(spread_halo, margin, cols, gym))
        store(z1h, z1l, c, slice(cols, cols + LANES), y_ends(ext[c, :, own], halo, margin, gye))

    def x_grid(c):
        def put(at, value):
            coarse[c, at, :] = value

        x_filter(z1h.at[c], z1l.at[c], inner, gxw, put)

    def y_pair(p):
        i, j = order[p]
        store(zph, zpl, p, own, own_p[p] + y_halo(ext[i, :, cols:] * ext[j, :, cols:], margin, cols, gym))

    def y_test(c):
        store(z2h, z2l, c, own, y_filter(coarse[c], margin, cols, tym))

    def x_test(c):
        def put(at, value):
            tested[c, at, :] = value

        x_filter(z2h.at[c], z2l.at[c], innermost, txw, put)

    def y_resolved(p):
        i, j = order[p]
        store(z2h, z2l, comps + p, own, y_filter(coarse[i] * coarse[j], margin, cols, tym))

    def x_sub(p):
        i, j = order[p]

        def put(at, value):
            sub[p, at, :] = value - coarse[i, at, own] * coarse[j, at, own]

        x_filter(zph.at[p], zpl.at[p], inner, gxw, put)

    def x_ger(p):
        i, j = order[p]

        def put(at, value):
            ger[p, at, :] = value - tested[i, at, :] * tested[j, at, :]

        x_filter(z2h.at[comps + p], z2l.at[comps + p], innermost, txw, put)

    def arrive(c):
        for sign, present in ((1, has_down), (-1, has_up)):
            pl.when(present)(lambda sign=sign: copies[c, "v", sign].wait_recv())

    for c in range(comps):
        if c < 2:
            arrive(c)
        if c == 1:
            for n in range(2, comps):
                arrive(n)
        y_grid(c)
        for p, (i, j) in enumerate(order):
            if j == c:
                y_pair(p)
        if c > 0:
            x_grid(c - 1)
    x_grid(comps - 1)
    for c in range(comps):
        if c == 0:
            column(first, lambda dy: forward(-1, dy))
        y_test(c)
        x_sub(c)
    for c in range(comps):
        y_resolved(c)
        x_test(c)

    for p in range(comps, pairs):
        y_resolved(p)
        x_sub(p)
        x_ger(p - comps)
    for p in range(pairs - comps, pairs):
        x_ger(p)

    copies[1, 0].wait_recv()
    copies[-1, 0].wait_recv()
    for sign, present in ((1, has_down), (-1, has_up)):
        @pl.when(present)
        def _(sign=sign):
            copies[1, sign].wait_recv()
            copies[-1, sign].wait_recv()

    copies[1, 0].wait_send()
    copies[-1, 0].wait_send()
    for sign, present in sides:
        @pl.when(present)
        def _(sign=sign):
            copies[1, sign].wait_send()
            copies[-1, sign].wait_send()
            copies["t", sign].wait_send()
            for c in range(comps):
                copies[c, "v", sign].wait_send()


def edge_kernel(margin, halo, corners, z1h, z1l, zph, zpl, z2h, z2l, sub_in, ger_in,
                gxe, txe, gym, gye, tym, sub_ref, ger_ref, sub_e, ger_e, sems):
    comps, cols = halo.shape[1], halo.shape[3]
    pairs, rows, _ = sub_ref.shape
    width = 2 * margin
    inner, innermost = sub_in.shape[1], ger_in.shape[1]
    order = [(i, j) for i in range(comps) for j in range(i, comps)]
    outs = []

    def leave(source, target):
        copy = pltpu.make_async_copy(source, target, sems.at[len(outs)])
        copy.start()
        outs.append(copy)

    leave(sub_in, sub_ref.at[:, pl.ds(margin, inner), :])
    leave(ger_in, ger_ref.at[:, pl.ds(width, innermost), :])

    def ends(side, c):
        up, down = corners[2 + side, c], corners[side, c]
        return halo[side, c], stacked([side_lanes(up, down, q, width) for q in range(width // SUB)])

    def pieces(z, size, count):
        high, low = split(z)
        return [(high[n * size:(n + 1) * size], low[n * size:(n + 1) * size]) for n in range(count)]

    def x_ends(side, late, high, low, n, count, size, weights):
        at = slice(0, size) if side == 0 else slice(count - size, count)
        h = (late[0], high[n, at]) if side == 0 else (high[n, at], late[0])
        l = (late[1], low[n, at]) if side == 0 else (low[n, at], late[1])
        r = dot(weights, stacked(h + l))
        half = weights.shape[0] // 2
        return r[0:half] + r[half:]

    near = (slice(width - margin, width), slice(0, margin))
    everywhere = range(pairs)

    def grid(side):
        parts = [ends(side, c) for c in range(comps)]
        rows_own, rows_halo = stacked([part[0] for part in parts]), stacked([part[1] for part in parts])
        values = jnp.concatenate([rows_own, thrice(rows_halo, width)], axis=1)
        ext = [values[c * width:(c + 1) * width] for c in range(comps)]
        products = stacked([ext[i][near[side]] * ext[j][near[side]] for i, j in order])
        z = y_filter(stacked([values, products]), margin, cols, gym)
        count = comps * width
        late = pieces(jnp.concatenate([z[0:count], y_ends(rows_own, rows_halo, margin, gye)], axis=1), width, comps)
        return late, pieces(z[count:], margin, pairs)

    def coarsen(side, late):
        return [x_ends(side, part, z1h, z1l, c, rows, width, gxe[...]) for c, part in enumerate(late)]

    def stress(side, coarse, late):
        weights = stacked([gxe[0:margin], gxe[width:width + margin]] if side == 0 else
                          [gxe[width - margin:width], gxe[2 * width - margin:]])
        for p, part in enumerate(late):
            value = x_ends(side, part, zph, zpl, p, rows, width + margin, weights)
            i, j = order[p]
            sub_e[p, side] = value - coarse[i][near[side], 0:cols] * coarse[j][near[side], 0:cols]

    def test(side, coarse):
        z = y_filter(stacked(coarse + [coarse[i] * coarse[j] for i, j in order]), margin, cols, tym)
        return pieces(z, width, comps + pairs)

    def resolve(side, late):
        tested = [x_ends(side, part, z2h, z2l, c, inner, width, txe[...]) for c, part in enumerate(late[0:comps])]
        for p, part in enumerate(late[comps:]):
            i, j = order[p]
            ger_e[p, side] = (x_ends(side, part, z2h, z2l, comps + p, inner, width, txe[...])
                              - tested[i] * tested[j])

    late = [grid(side) for side in range(2)]
    coarse = [coarsen(side, late[side][0]) for side in range(2)]
    tests = []
    for side in range(2):
        tests.append(test(side, coarse[side]))
        stress(side, coarse[side], late[side][1])
    leave(sub_e.at[:, 0], sub_ref.at[:, pl.ds(0, margin), :])
    leave(sub_e.at[:, 1], sub_ref.at[:, pl.ds(rows - margin, margin), :])
    resolve(0, tests[0])
    leave(ger_e.at[:, 0], ger_ref.at[:, pl.ds(0, width), :])
    resolve(1, tests[1])
    leave(ger_e.at[:, 1], ger_ref.at[:, pl.ds(rows - width, width), :])
    for copy in outs:
        copy.wait()


def local(nx, ny, velocity, grid_x, grid_y, test_x, test_y):
    comps, planes, cols, rows = velocity.shape
    taps = grid_x.shape[0]
    margin = (taps - 1) // 2
    width = 2 * margin
    wide = cols + LANES
    step = LANES - width
    pairs = comps * (comps + 1) // 2
    vmem = pl.BlockSpec(memory_space=pltpu.VMEM)
    anywhere = pl.BlockSpec(memory_space=pl.ANY)
    packed = rows // width * SUB
    inner, innermost = rows - width, rows - 2 * width

    def filled(count):
        return round_up(count, step) + width

    fields = comps + pairs
    subs, gers = [], []
    shape = jax.ShapeDtypeStruct
    for plane in range(planes):
        v = jnp.swapaxes(velocity[:, plane], 1, 2)
        parts = pl.pallas_call(
            functools.partial(interior_kernel, nx, ny, width),
            out_shape=(
                shape((2, comps, width, cols), F32),
                shape((4, comps, SUB, LANES), F32),
                shape((comps, max(rows, filled(inner)), wide), BF),
                shape((comps, max(rows, filled(inner)), wide), BF),
                shape((pairs, max(rows, filled(inner)), cols), BF),
                shape((pairs, max(rows, filled(inner)), cols), BF),
                shape((fields, max(inner, filled(innermost)), cols), BF),
                shape((fields, max(inner, filled(innermost)), cols), BF),
                shape((pairs, inner, cols), F32),
                shape((pairs, innermost, cols), F32),
                shape((2 * width, LANES), BF),
                shape((2 * width, LANES), BF),
                shape((3 * cols + LANES, cols), BF),
                shape((3 * LANES, LANES), BF),
                shape((3 * cols + LANES, cols), BF),
            ),
            in_specs=[pl.BlockSpec(memory_space=pltpu.HBM)] * 5,
            out_specs=(vmem,) * 15,
            scratch_shapes=[
                pltpu.VMEM((comps, rows, wide), F32),
                pltpu.VMEM((taps, cols), F32),
                pltpu.VMEM((1, taps), F32),
                pltpu.VMEM((1, taps), F32),
                pltpu.VMEM((taps, cols), F32),
                pltpu.VMEM((round_up(taps, SUB), wide), F32),
                pltpu.VMEM((2 * step, 2 * LANES), BF),
                pltpu.VMEM((2 * step, 2 * LANES), BF),
                pltpu.VMEM((comps, packed, LANES), F32),
                pltpu.VMEM((comps, packed, LANES), F32),
                pltpu.VMEM((comps, packed, LANES), F32),
                pltpu.VMEM((comps, packed, LANES), F32),
                pltpu.VMEM((taps, LANES), F32),
                pltpu.VMEM((taps, LANES), F32),
                pltpu.VMEM((comps, rows, cols), F32),
                pltpu.VMEM((pairs, rows, cols), F32),
                pltpu.VMEM((comps, inner, wide), F32),
                pltpu.VMEM((comps, innermost, cols), F32),
                pltpu.VMEM((comps, width, cols), F32),
                pltpu.VMEM((comps, SUB, LANES), F32),
                pltpu.VMEM((comps, SUB, LANES), F32),
                pltpu.SemaphoreType.DMA((5 + comps,)),
                pltpu.SemaphoreType.DMA((8 + 2 * comps,)),
                pltpu.SemaphoreType.DMA((8 + 2 * comps,)),
                pltpu.SemaphoreType.REGULAR((7,)),
            ],
            compiler_params=pltpu.CompilerParams(
                collective_id=plane, has_side_effects=True, vmem_limit_bytes=20 << 20),
            name="interior",
        )(*[pltpu.with_memory_space_constraint(x, pltpu.HBM) for x in (
            v, grid_y.T, grid_x.reshape(1, taps), test_x.reshape(1, taps), test_y.T)])
        out = shape((pairs, rows, cols), F32)
        sub, ger = pl.pallas_call(
            functools.partial(edge_kernel, margin),
            out_shape=(out, out),
            in_specs=[vmem] * 15,
            out_specs=(anywhere, anywhere),
            scratch_shapes=[
                pltpu.VMEM((pairs, 2, margin, cols), F32),
                pltpu.VMEM((pairs, 2, width, cols), F32),
                pltpu.SemaphoreType.DMA((6,)),
            ],
            compiler_params=pltpu.CompilerParams(
                vmem_limit_bytes=8 << 20),
            name="edge",
        )(*parts)
        subs.append(jnp.swapaxes(sub, 1, 2))
        gers.append(jnp.swapaxes(ger, 1, 2))
    return jnp.stack(subs, axis=1), jnp.stack(gers, axis=1)


def solution(mesh):
    nx, ny = mesh.shape["gx"], mesh.shape["gy"]
    field = P(None, None, "gy", "gx")
    return jax.shard_map(
        functools.partial(local, nx, ny),
        mesh=mesh,
        in_specs=(field, P(), P("gy", None), P(), P("gy", None)),
        out_specs=(field, field),
        check_vma=False,
    )
```

```python
import functools

import jax
import jax.numpy as jnp
from jax import lax
from jax.experimental import pallas as pl
from jax.experimental.pallas import tpu as pltpu
from jax.sharding import PartitionSpec as P

MESH = pl.DeviceIdType.MESH
LANES = 128
SUB = 8
BF = jnp.bfloat16
F32 = jnp.float32


def round_up(value, unit):
    return (value + unit - 1) // unit * unit


def split(value):
    high = value.astype(BF)
    return high, (value - high.astype(F32)).astype(BF)


def dot(a, b):
    return jnp.dot(a, b, preferred_element_type=F32)


def x_weights(w_ref, step, out, edge):
    taps = w_ref.shape[1]
    w = jnp.concatenate([w_ref[...], jnp.zeros((1, LANES - taps), F32)], axis=1)
    w = w / jnp.sum(w)
    band = pltpu.roll(jnp.broadcast_to(w, (LANES, LANES)), 0, 1, stride=1, stride_axis=0)
    high, low = split(band[0:step])
    out[0:step, 0:LANES] = high
    out[0:step, LANES:] = high
    out[step:, 0:LANES] = low
    out[step:, LANES:] = jnp.zeros((step, LANES), BF)
    width = edge.shape[0] // 2
    high, low = split(band[0:width])
    high = high.astype(F32)
    edge[0:width] = (high + pltpu.roll(high, 2 * width, 1)).astype(BF)
    edge[width:] = low


def spread(value, margin):
    lane = lax.broadcasted_iota(jnp.int32, value.shape, 1)
    near = jnp.where((lane < margin) | (lane >= LANES - margin), value, 0.0)
    return pltpu.roll(jnp.where(lane < LANES // 2, near, 0.0), margin, 1) + pltpu.roll(
        jnp.where(lane < LANES // 2, 0.0, near), LANES - margin, 1)


def y_weights(table, taps, first_row, total, cols, main, edge=None, tiles=None):
    margin = (taps - 1) // 2
    width = 2 * margin
    lanes = table.shape[1]
    wide = cols + LANES
    k = lax.broadcasted_iota(jnp.int32, (LANES, lanes), 0)
    lane = lax.broadcasted_iota(jnp.int32, (LANES, lanes), 1)
    y = first_row + jnp.where(lane < cols + LANES // 2, lane, lane - wide)
    source = y + k - margin
    keep = (k < taps) & (source >= 0) & (source < total) & (y >= 0) & (y < total)
    w = jnp.where(keep, jnp.concatenate(
        [table, jnp.zeros((LANES - table.shape[0], lanes), F32)], axis=0), 0.0)
    s = jnp.sum(w, axis=0, keepdims=True)
    w = (w / jnp.where(s > 0.0, s, 1.0)).T
    zeros = jnp.zeros((LANES, cols), F32)
    for t in (range(lanes // LANES) if tiles is None else tiles):
        at = slice(t * LANES, (t + 1) * LANES)
        tile = jnp.concatenate([w[at], zeros], axis=1)
        band = pltpu.roll(tile, (t * LANES - margin) % wide, 1, stride=1, stride_axis=0)
        if t * LANES < cols:
            own, halo = band[:, 0:cols].T, band[:, cols:]
            own_high, own_low = split(own)
            main[0:cols, at] = own_high
            main[cols:2 * cols, at] = own_low
            main[2 * cols:3 * cols, at] = own_high
            halo = spread(halo, margin)
            high = halo.astype(BF).astype(F32)
            packed = high + pltpu.roll(high, width, 1) + pltpu.roll(halo - high, 2 * width, 1)
            main[3 * cols:, at] = packed.T.astype(BF)
        else:
            low_own, high_own, halo = band[:, 0:LANES].T, band[:, cols - LANES:cols].T, band[:, cols:].T
            near = jnp.concatenate([
                low_own[0:margin], halo[0:width], jnp.zeros((LANES - 2 * margin - 2 * width, LANES), F32),
                halo[LANES - width:], high_own[LANES - margin:]], axis=0)
            near = spread(near, margin)
            near = near + pltpu.roll(near, width, 1) + pltpu.roll(near, 2 * width, 1)
            high, low = split(near)
            edge[0:LANES] = high
            edge[LANES:2 * LANES] = high
            edge[2 * LANES:] = low


def y_own(value, cols, main):
    high, low = split(value)
    return dot(jnp.concatenate([high, high, low], axis=1), main[0:3 * cols])


def second(shape, width):
    lane = lax.broadcasted_iota(jnp.int32, shape, 1)
    return (lane < width // 2) | ((lane >= width + width // 2) & (lane < 2 * width))


def thrice(halo, width):
    lane = lax.broadcasted_iota(jnp.int32, halo.shape, 1)
    margin = width // 2
    home = ((lane >= margin) & (lane < width)) | ((lane >= LANES - width) & (lane < LANES - margin))
    return jnp.where(home, halo, jnp.where(
        second(halo.shape, width), pltpu.roll(halo, width, 1), pltpu.roll(halo, 2 * width, 1)))


def packed_halo(halo, margin):
    high = halo.astype(BF).astype(F32)
    return jnp.where(second(halo.shape, 2 * margin), halo - high, high).astype(BF)


def y_halo(halo, margin, cols, main):
    return dot(packed_halo(halo, margin), main[3 * cols:])


def y_filter(value, margin, cols, main):
    high, low = split(value[:, 0:cols])
    return dot(jnp.concatenate([high, high, low, packed_halo(value[:, cols:], margin)], axis=1), main[...])


def y_ends(own, halo, margin, edge):
    lane = lax.broadcasted_iota(jnp.int32, halo.shape, 1)
    ends = jnp.where(lane < margin, own[:, 0:LANES],
                     jnp.where(lane >= LANES - margin, own[:, own.shape[1] - LANES:], halo))
    high, low = split(ends)
    return dot(jnp.concatenate([high, low, high], axis=1), edge[...])


def side_lanes(up, down, q, width):
    lane = lax.broadcasted_iota(jnp.int32, up.shape, 1)
    margin = width // 2
    return jnp.where(lane < LANES // 2, pltpu.roll(up, (LANES + margin - q * width) % LANES, 1),
                     pltpu.roll(down, (2 * LANES - margin - (q + 1) * width) % LANES, 1))


def x_filter(zh, zl, count, weights, put):
    step = weights.shape[0] // 2
    for s in range(0, count, step):
        size = min(step, count - s)
        at = slice(s, s + LANES)
        w = weights[...] if size == step else stacked([weights[0:size], weights[step:step + size]])
        r = dot(w, jnp.concatenate([zh[at], zl[at]], axis=0))
        put(slice(s, s + size), r[0:size] + r[size:])


def stacked(values):
    return jnp.concatenate(values, axis=0)


def interior_kernel(nx, ny, width, v_hbm, t_hbm, gx_hbm, tx_hbm, ty_hbm,
                    halo, corners, z1h, z1l, zph, zpl, z2h, z2l, sub, ger, gxe, txe, gym, gye, tym,
                    ext, t_ref, gx_ref, tx_ref, ty_ref, text_ref, gxw, txw,
                    pack_d, pack_u, from_d, from_u, t_low, t_high,
                    own_v, own_p, coarse, tested, tail_v, corner_u, corner_d, load_sem, send_sem, recv_sem, ready):
    comps, rows, _ = ext.shape
    taps, cols = t_ref.shape
    margin = width // 2
    pairs, inner, _ = sub.shape
    innermost = ger.shape[1]
    me_x, me_y = lax.axis_index("gx"), lax.axis_index("gy")
    first, last = me_x == 0, me_x == nx - 1
    not_first, not_last = me_x > 0, me_x < nx - 1
    has_up, has_down = me_y < ny - 1, me_y > 0
    vertical = jnp.where(has_up, 1, 0) + jnp.where(has_down, 1, 0)
    sides = ((1, has_up), (-1, has_down))
    columns = ((0, None), (1, has_up), (-1, has_down))

    def device(dx, dy):
        return {"gx": lax.rem(me_x + dx + nx, nx), "gy": lax.rem(me_y + dy + ny, ny)}

    def signal(sem, dx, dy):
        pl.semaphore_signal(sem, inc=1, device_id=device(dx, dy), device_id_type=MESH)

    def column(condition, act):
        for dy, present in columns:
            pl.when(condition if present is None else condition & present)(lambda dy=dy: act(dy))

    barrier = pltpu.get_barrier_semaphore()
    pl.when(has_up)(lambda: signal(barrier, 0, 1))
    column(not_last, lambda dy: signal(barrier, 1, dy))
    column(first, lambda dy: signal(barrier, -1, dy))

    own = slice(0, cols)
    order = [(i, j) for i in range(comps) for j in range(i, comps)]
    loads = [pltpu.make_async_copy(src, dst, load_sem.at[i]) for i, (src, dst) in enumerate(
        [(v_hbm.at[0], ext.at[0, :, own]), (t_hbm, t_ref)]
        + [(v_hbm.at[c], ext.at[c, :, own]) for c in range(1, comps)]
        + [(gx_hbm, gx_ref), (tx_hbm, tx_ref), (ty_hbm, ty_ref)])]
    ahead = pltpu.make_async_copy(v_hbm.at[:, pl.ds(rows - width, width), :], tail_v, load_sem.at[4 + comps])
    pl.when(last)(lambda: ahead.start())
    for load in loads:
        load.start()

    per = LANES // width
    groups = rows // width
    head, tail = pl.ds(0, SUB), pl.ds((groups - 1) * SUB, SUB)
    low_x, high_x = v_hbm.at[:, pl.ds(0, width), :], v_hbm.at[:, pl.ds(rows - width, width), :]
    copies = {}

    def remote(key, src, dst, dx, dy):
        n = len(copies)
        copies[key] = pltpu.make_async_remote_copy(
            src_ref=src, dst_ref=dst, send_sem=send_sem.at[n], recv_sem=recv_sem.at[n],
            device_id=device(dx, dy), device_id_type=MESH)

    remote((1, 0), high_x, halo.at[0], 1, 0)
    remote((-1, 0), low_x, halo.at[1], -1, 0)
    remote((1, 1), pack_u.at[:, tail, :], corners.at[0], 1, 1)
    remote((-1, 1), pack_u.at[:, head, :], corners.at[1], -1, 1)
    remote((1, -1), pack_d.at[:, tail, :], corners.at[2], 1, -1)
    remote((-1, -1), pack_d.at[:, head, :], corners.at[3], -1, -1)
    remote(("t", 1), t_ref.at[:, pl.ds(cols - LANES, LANES)], t_low, 0, 1)
    remote(("t", -1), t_ref.at[:, pl.ds(0, LANES)], t_high, 0, -1)
    for c in range(comps):
        remote((c, "v", 1), pack_u.at[c], from_d.at[c], 0, 1)
        remote((c, "v", -1), pack_d.at[c], from_u.at[c], 0, -1)

    @pl.when(last)
    def _():
        pl.semaphore_wait(barrier, jnp.where(has_down, 1, 0) + jnp.where(first, 0, 1 + vertical) + 1 + vertical)
        copies[1, 0].start()

    column(last, lambda dy: signal(ready.at[1 - dy], 1, dy))

    @pl.when(last)
    def _():
        ahead.wait()
        for c in range(comps):
            for q in range(per):
                at = slice(q * SUB, (q + 1) * SUB)
                corner_u[c, :, q * width:(q + 1) * width] = tail_v[c, at, cols - width:cols]
                corner_d[c, :, q * width:(q + 1) * width] = tail_v[c, at, 0:width]

    @pl.when(not_last & (not_first | has_down))
    def _():
        pl.semaphore_wait(barrier, jnp.where(has_down, 1, 0) + jnp.where(first, 0, 1 + vertical))

    pl.when(not_first)(lambda: copies[-1, 0].start())
    pl.when(has_down)(lambda: signal(ready.at[3], 0, -1))
    column(not_first, lambda dy: signal(ready.at[5 - dy], -1, dy))

    for n, dy, src, present in ((2, 1, corner_u, has_up), (4, -1, corner_d, has_down)):
        wrapped = pltpu.make_async_remote_copy(
            src_ref=src, dst_ref=corners.at[n - 2], send_sem=send_sem.at[n],
            recv_sem=recv_sem.at[n], device_id=device(1, dy), device_id_type=MESH)
        pl.when(last & present)(lambda wrapped=wrapped: wrapped.start())

    def pack(c):
        for g in range(groups):
            for q in range(per):
                src = pl.ds(g * width + q * SUB, SUB)
                dst = pl.ds(g * SUB, SUB)
                pack_u[c, dst, q * width:(q + 1) * width] = ext[c, src, cols - width:cols]
                pack_d[c, dst, q * width:(q + 1) * width] = ext[c, src, 0:width]

    for c in range(comps):
        loads[c + (c > 0)].wait()
        pack(c)
        if c == 0:
            loads[1].wait()
            pl.when(has_down)(lambda: copies["t", -1].start())
        else:
            pl.when(has_down)(lambda c=c: copies[c - 1, "v", -1].start())

    text_ref[...] = jnp.zeros_like(text_ref)
    for z, full in ((z1h, rows), (z1l, rows), (zph, rows), (zpl, rows), (z2h, inner), (z2l, inner)):
        if z.shape[1] > full:
            z[:, full:, :] = jnp.zeros((z.shape[0], z.shape[1] - full, z.shape[2]), BF)
    for sign, present, mid in ((1, has_up, from_u), (-1, has_down, from_d)):
        @pl.when(jnp.logical_not(present))
        def _(sign=sign, mid=mid):
            mid[...] = jnp.zeros_like(mid)
            for side in range(2):
                corners[side + (2 if sign > 0 else 0)] = jnp.zeros(corners.shape[1:], F32)

    pl.when(has_down)(lambda: copies[comps - 1, "v", -1].start())

    @pl.when(has_up)
    def _():
        pl.semaphore_wait(ready.at[3], 1)
        copies["t", 1].start()
        for c in range(comps):
            copies[c, "v", 1].start()

    for dy, present in sides:
        pl.when(not_first & present)(lambda dy=dy: copies[-1, dy].start())

    for load in loads[comps + 1:]:
        load.wait()
    text_ref[0:taps, 0:cols] = t_ref[...]
    first_row, total = me_y * cols, cols * ny
    own_tiles = range(cols // LANES)
    y_weights(t_ref[...], taps, first_row, total, cols, gym, tiles=own_tiles)

    def own_pair(p):
        i, j = order[p]
        own_p[p] = y_own(ext[i, :, own] * ext[j, :, own], cols, gym)

    held = {}
    for n, dx, at in ((0, 1, rows - width), (1, -1, 0)):
        held[dx, 0] = pltpu.make_async_remote_copy(
            src_ref=ext.at[:, pl.ds(at, width), own], dst_ref=halo.at[n], send_sem=send_sem.at[n],
            recv_sem=recv_sem.at[n], device_id=device(dx, 0), device_id_type=MESH)

    def forward(dx, dy):
        pl.semaphore_wait(ready.at[(5 if dx > 0 else 1) + dy], 1)
        held.get((dx, dy), copies[dx, dy]).start()

    for c in range(comps):
        own_v[c] = y_own(ext[c, :, own], cols, gym)
    for p in range(0):
        own_pair(p)
    x_weights(gx_ref, gxw.shape[0] // 2, gxw, gxe)
    x_weights(tx_ref, txw.shape[0] // 2, txw, txe)
    y_weights(ty_ref[...], taps, first_row, total, cols, tym, tiles=own_tiles)
    pl.when(not_last)(lambda: forward(1, 0))
    for p in range(0, pairs):
        own_pair(p)
    for dy, present in sides:
        pl.when(not_last & present)(lambda dy=dy: forward(1, dy))

    for sign, present, tile, at in ((1, has_down, t_low, LANES - margin), (-1, has_up, t_high, 0)):
        @pl.when(present)
        def _(sign=sign, tile=tile, at=at):
            copies["t", sign].wait_recv()
            text_ref[0:taps, cols + at:cols + at + margin] = tile[:, at:at + margin]

    y_weights(text_ref[...], taps, first_row, total, cols, gym, gye, tiles=(cols // LANES,))

    def store(high, low, index, lanes, z):
        high[index, 0:z.shape[0], lanes], low[index, 0:z.shape[0], lanes] = split(z)

    def y_grid(c):
        blocks = []
        for g in range(groups):
            at = pl.ds(g * SUB, SUB)
            up, down = from_u[c, at, :], from_d[c, at, :]
            blocks += [side_lanes(up, down, q, width) for q in range(per)]
        halo = stacked(blocks)
        spread_halo = thrice(halo, width)
        ext[c, :, cols:] = spread_halo
        store(z1h, z1l, c, own, own_v[c] + y_halo(spread_halo, margin, cols, gym))
        store(z1h, z1l, c, slice(cols, cols + LANES), y_ends(ext[c, :, own], halo, margin, gye))

    def x_grid(c):
        def put(at, value):
            coarse[c, at, :] = value

        x_filter(z1h.at[c], z1l.at[c], inner, gxw, put)

    def y_pair(p):
        i, j = order[p]
        store(zph, zpl, p, own, own_p[p] + y_halo(ext[i, :, cols:] * ext[j, :, cols:], margin, cols, gym))

    def y_test(c):
        store(z2h, z2l, c, own, y_filter(coarse[c], margin, cols, tym))

    def x_test(c):
        def put(at, value):
            tested[c, at, :] = value

        x_filter(z2h.at[c], z2l.at[c], innermost, txw, put)

    def y_resolved(p):
        i, j = order[p]
        store(z2h, z2l, comps + p, own, y_filter(coarse[i] * coarse[j], margin, cols, tym))

    def x_sub(p):
        i, j = order[p]

        def put(at, value):
            sub[p, at, :] = value - coarse[i, at, own] * coarse[j, at, own]

        x_filter(zph.at[p], zpl.at[p], inner, gxw, put)

    def x_ger(p):
        i, j = order[p]

        def put(at, value):
            ger[p, at, :] = value - tested[i, at, :] * tested[j, at, :]

        x_filter(z2h.at[comps + p], z2l.at[comps + p], innermost, txw, put)

    def arrive(c):
        for sign, present in ((1, has_down), (-1, has_up)):
            pl.when(present)(lambda sign=sign: copies[c, "v", sign].wait_recv())

    for c in range(comps):
        if c < 2:
            arrive(c)
        if c == 1:
            for n in range(2, comps):
                arrive(n)
        y_grid(c)
        for p, (i, j) in enumerate(order):
            if j == c:
                y_pair(p)
        if c > 0:
            x_grid(c - 1)
    x_grid(comps - 1)
    for c in range(comps):
        if c == 0:
            column(first, lambda dy: forward(-1, dy))
        y_test(c)
        x_sub(c)
    for c in range(comps):
        y_resolved(c)
        x_test(c)

    for p in range(comps, pairs):
        y_resolved(p)
        x_sub(p)
        x_ger(p - comps)
    for p in range(pairs - comps, pairs):
        x_ger(p)

    copies[1, 0].wait_recv()
    copies[-1, 0].wait_recv()
    for sign, present in ((1, has_down), (-1, has_up)):
        @pl.when(present)
        def _(sign=sign):
            copies[1, sign].wait_recv()
            copies[-1, sign].wait_recv()

    copies[1, 0].wait_send()
    copies[-1, 0].wait_send()
    for sign, present in sides:
        @pl.when(present)
        def _(sign=sign):
            copies[1, sign].wait_send()
            copies[-1, sign].wait_send()
            copies["t", sign].wait_send()
            for c in range(comps):
                copies[c, "v", sign].wait_send()


def edge_kernel(margin, halo, corners, z1h, z1l, zph, zpl, z2h, z2l, sub_in, ger_in,
                gxe, txe, gym, gye, tym, sub_ref, ger_ref, sub_e, ger_e, sems):
    comps, cols = halo.shape[1], halo.shape[3]
    pairs, rows, _ = sub_ref.shape
    width = 2 * margin
    inner, innermost = sub_in.shape[1], ger_in.shape[1]
    order = [(i, j) for i in range(comps) for j in range(i, comps)]
    outs = []

    def leave(source, target):
        copy = pltpu.make_async_copy(source, target, sems.at[len(outs)])
        copy.start()
        outs.append(copy)

    leave(sub_in, sub_ref.at[:, pl.ds(margin, inner), :])
    leave(ger_in, ger_ref.at[:, pl.ds(width, innermost), :])

    def ends(side, c):
        up, down = corners[2 + side, c], corners[side, c]
        return halo[side, c], stacked([side_lanes(up, down, q, width) for q in range(width // SUB)])

    def pieces(z, size, count):
        high, low = split(z)
        return [(high[n * size:(n + 1) * size], low[n * size:(n + 1) * size]) for n in range(count)]

    def x_ends(side, late, high, low, n, count, size, weights):
        at = slice(0, size) if side == 0 else slice(count - size, count)
        h = (late[0], high[n, at]) if side == 0 else (high[n, at], late[0])
        l = (late[1], low[n, at]) if side == 0 else (low[n, at], late[1])
        r = dot(weights, stacked(h + l))
        half = weights.shape[0] // 2
        return r[0:half] + r[half:]

    near = (slice(width - margin, width), slice(0, margin))
    everywhere = range(pairs)

    def grid(side):
        parts = [ends(side, c) for c in range(comps)]
        rows_own, rows_halo = stacked([part[0] for part in parts]), stacked([part[1] for part in parts])
        values = jnp.concatenate([rows_own, thrice(rows_halo, width)], axis=1)
        ext = [values[c * width:(c + 1) * width] for c in range(comps)]
        products = stacked([ext[i][near[side]] * ext[j][near[side]] for i, j in order])
        z = y_filter(stacked([values, products]), margin, cols, gym)
        count = comps * width
        late = pieces(jnp.concatenate([z[0:count], y_ends(rows_own, rows_halo, margin, gye)], axis=1), width, comps)
        return late, pieces(z[count:], margin, pairs)

    def coarsen(side, late):
        return [x_ends(side, part, z1h, z1l, c, rows, width, gxe[...]) for c, part in enumerate(late)]

    def stress(side, coarse, late):
        weights = stacked([gxe[0:margin], gxe[width:width + margin]] if side == 0 else
                          [gxe[width - margin:width], gxe[2 * width - margin:]])
        for p, part in enumerate(late):
            value = x_ends(side, part, zph, zpl, p, rows, width + margin, weights)
            i, j = order[p]
            sub_e[p, side] = value - coarse[i][near[side], 0:cols] * coarse[j][near[side], 0:cols]

    def test(side, coarse):
        z = y_filter(stacked(coarse + [coarse[i] * coarse[j] for i, j in order]), margin, cols, tym)
        return pieces(z, width, comps + pairs)

    def resolve(side, late):
        tested = [x_ends(side, part, z2h, z2l, c, inner, width, txe[...]) for c, part in enumerate(late[0:comps])]
        for p, part in enumerate(late[comps:]):
            i, j = order[p]
            ger_e[p, side] = (x_ends(side, part, z2h, z2l, comps + p, inner, width, txe[...])
                              - tested[i] * tested[j])

    late = [grid(side) for side in range(2)]
    coarse = [coarsen(side, late[side][0]) for side in range(2)]
    tests = []
    for side in range(2):
        tests.append(test(side, coarse[side]))
        stress(side, coarse[side], late[side][1])
    leave(sub_e.at[:, 0], sub_ref.at[:, pl.ds(0, margin), :])
    leave(sub_e.at[:, 1], sub_ref.at[:, pl.ds(rows - margin, margin), :])
    resolve(0, tests[0])
    leave(ger_e.at[:, 0], ger_ref.at[:, pl.ds(0, width), :])
    resolve(1, tests[1])
    leave(ger_e.at[:, 1], ger_ref.at[:, pl.ds(rows - width, width), :])
    for copy in outs:
        copy.wait()


def local(nx, ny, velocity, grid_x, grid_y, test_x, test_y):
    comps, planes, cols, rows = velocity.shape
    taps = grid_x.shape[0]
    margin = (taps - 1) // 2
    width = 2 * margin
    wide = cols + LANES
    step = LANES - width
    pairs = comps * (comps + 1) // 2
    vmem = pl.BlockSpec(memory_space=pltpu.VMEM)
    anywhere = pl.BlockSpec(memory_space=pl.ANY)
    packed = rows // width * SUB
    inner, innermost = rows - width, rows - 2 * width

    def filled(count):
        return round_up(count, step) + width

    fields = comps + pairs
    subs, gers = [], []
    shape = jax.ShapeDtypeStruct
    for plane in range(planes):
        v = jnp.swapaxes(velocity[:, plane], 1, 2)
        parts = pl.pallas_call(
            functools.partial(interior_kernel, nx, ny, width),
            out_shape=(
                shape((2, comps, width, cols), F32),
                shape((4, comps, SUB, LANES), F32),
                shape((comps, max(rows, filled(inner)), wide), BF),
                shape((comps, max(rows, filled(inner)), wide), BF),
                shape((pairs, max(rows, filled(inner)), cols), BF),
                shape((pairs, max(rows, filled(inner)), cols), BF),
                shape((fields, max(inner, filled(innermost)), cols), BF),
                shape((fields, max(inner, filled(innermost)), cols), BF),
                shape((pairs, inner, cols), F32),
                shape((pairs, innermost, cols), F32),
                shape((2 * width, LANES), BF),
                shape((2 * width, LANES), BF),
                shape((3 * cols + LANES, cols), BF),
                shape((3 * LANES, LANES), BF),
                shape((3 * cols + LANES, cols), BF),
            ),
            in_specs=[pl.BlockSpec(memory_space=pltpu.HBM)] * 5,
            out_specs=(vmem,) * 15,
            scratch_shapes=[
                pltpu.VMEM((comps, rows, wide), F32),
                pltpu.VMEM((taps, cols), F32),
                pltpu.VMEM((1, taps), F32),
                pltpu.VMEM((1, taps), F32),
                pltpu.VMEM((taps, cols), F32),
                pltpu.VMEM((round_up(taps, SUB), wide), F32),
                pltpu.VMEM((2 * step, 2 * LANES), BF),
                pltpu.VMEM((2 * step, 2 * LANES), BF),
                pltpu.VMEM((comps, packed, LANES), F32),
                pltpu.VMEM((comps, packed, LANES), F32),
                pltpu.VMEM((comps, packed, LANES), F32),
                pltpu.VMEM((comps, packed, LANES), F32),
                pltpu.VMEM((taps, LANES), F32),
                pltpu.VMEM((taps, LANES), F32),
                pltpu.VMEM((comps, rows, cols), F32),
                pltpu.VMEM((pairs, rows, cols), F32),
                pltpu.VMEM((comps, inner, wide), F32),
                pltpu.VMEM((comps, innermost, cols), F32),
                pltpu.VMEM((comps, width, cols), F32),
                pltpu.VMEM((comps, SUB, LANES), F32),
                pltpu.VMEM((comps, SUB, LANES), F32),
                pltpu.SemaphoreType.DMA((5 + comps,)),
                pltpu.SemaphoreType.DMA((8 + 2 * comps,)),
                pltpu.SemaphoreType.DMA((8 + 2 * comps,)),
                pltpu.SemaphoreType.REGULAR((7,)),
            ],
            compiler_params=pltpu.CompilerParams(
                collective_id=plane, has_side_effects=True, vmem_limit_bytes=20 << 20),
            name="interior",
        )(*[pltpu.with_memory_space_constraint(x, pltpu.HBM) for x in (
            v, grid_y.T, grid_x.reshape(1, taps), test_x.reshape(1, taps), test_y.T)])
        out = shape((pairs, rows, cols), F32)
        sub, ger = pl.pallas_call(
            functools.partial(edge_kernel, margin),
            out_shape=(out, out),
            in_specs=[vmem] * 15,
            out_specs=(anywhere, anywhere),
            scratch_shapes=[
                pltpu.VMEM((pairs, 2, margin, cols), F32),
                pltpu.VMEM((pairs, 2, width, cols), F32),
                pltpu.SemaphoreType.DMA((6,)),
            ],
            compiler_params=pltpu.CompilerParams(
                vmem_limit_bytes=8 << 20),
            name="edge",
        )(*parts)
        subs.append(jnp.swapaxes(sub, 1, 2))
        gers.append(jnp.swapaxes(ger, 1, 2))
    return jnp.stack(subs, axis=1), jnp.stack(gers, axis=1)


def solution(mesh):
    nx, ny = mesh.shape["gx"], mesh.shape["gy"]
    field = P(None, None, "gy", "gx")
    return jax.shard_map(
        functools.partial(local, nx, ny),
        mesh=mesh,
        in_specs=(field, P(), P("gy", None), P(), P("gy", None)),
        out_specs=(field, field),
        check_vma=False,
    )
```
